32 devices in a mesh: pipe: 2 (over core), row: 4 (over y, x), col: 4 (over z).
Axes of the slice: x: 2, y: 2, z: 4, core: 2. Of those that a mesh axis runs over, the one named last changes fastest.
Arguments:
- inputs: bfloat16 [2, 1024, 1536], P(None, 'row'), may hold values from -6 to 6
- cotangent: bfloat16 [2, 1024, 1536], P(None, 'row'), may hold values from -6 to 6
- segment_ids: int32 [2, 1024], P(None, 'row'), may hold values from 0 to 3, never falling along the last dimension, each value on 1 to 512 neighbouring positions
- batch_order: int32 [2], replicated, may hold values from 0 to 1, each once
- norm_gain: float32 [2, 1536], P('pipe'), may hold values from 0.5 to 1.5
- gate_proj: bfloat16 [2, 1536, 3072], P('pipe', 'row', 'col'), may hold values from -0.15625 to 0.15625
- value_proj: bfloat16 [2, 1536, 3072], P('pipe', 'row', 'col'), may hold values from -0.15625 to 0.15625
- step_proj: bfloat16 [2, 1536, 48], P('pipe', 'row', 'col'), may hold values from -0.15625 to 0.15625
- state_proj: bfloat16 [2, 1536, 256], P('pipe', 'row'), may hold values from -0.15625 to 0.15625
- conv_value: float32 [2, 4, 3072], P('pipe', None, 'col'), may hold values from -3 to 3
- conv_value_bias: float32 [2, 3072], P('pipe', 'col'), may hold values from -3 to 3
- conv_state: float32 [2, 4, 256], P('pipe'), may hold values from -3 to 3
- conv_state_bias: float32 [2, 256], P('pipe'), may hold values from -3 to 3
- step_bias: float32 [2, 48], P('pipe', 'col'), may hold values from -6 to -2
- decay_log: float32 [2, 48], P('pipe', 'col'), may hold values from 0 to 2.7
- skip_gain: float32 [2, 48], P('pipe', 'col'), may hold values from 0.5 to 1.5
- gate_gain: float32 [2, 3072], P('pipe', 'col'), may hold values from 0.5 to 1.5
- out_proj: bfloat16 [2, 3072, 1536], P('pipe', 'col', 'row'), may hold values from -0.109375 to 0.109375
Outputs:
- layer_outputs: bfloat16 [2, 2, 1024, 1536], P('pipe', None, 'row')
- input_grads: float32 [2, 2, 1024, 1536], P('pipe', None, 'row')
- grad_norm_gain: float32 [2, 1536], P('pipe')
- grad_gate_proj: float32 [2, 1536, 3072], P('pipe', 'row', 'col')
- grad_value_proj: float32 [2, 1536, 3072], P('pipe', 'row', 'col')
- grad_step_proj: float32 [2, 1536, 48], P('pipe', 'row', 'col')
- grad_state_proj: float32 [2, 1536, 256], P('pipe', 'row')
- grad_conv_value: float32 [2, 4, 3072], P('pipe', None, 'col')
- grad_conv_value_bias: float32 [2, 3072], P('pipe', 'col')
- grad_conv_state: float32 [2, 4, 256], P('pipe')
- grad_conv_state_bias: float32 [2, 256], P('pipe')
- grad_step_bias: float32 [2, 48], P('pipe', 'col')
- grad_decay_log: float32 [2, 48], P('pipe', 'col')
- grad_skip_gain: float32 [2, 48], P('pipe', 'col')
- grad_gate_gain: float32 [2, 3072], P('pipe', 'col')
- grad_out_proj: float32 [2, 3072, 1536], P('pipe', 'col', 'row')
The draws below stay inside these ranges and needn't reach their ends.
Inputs may be any that keep to these rules, and one draw needn't show every extreme that they name: `segment_ids`: document numbers never fall along a sequence; every sequence holds 4 documents, numbered from 0. `batch_order`: each micro-batch is named once.
All inputs are finite; a program needn't handle non-finite values.
Results may differ from the reference program's by a relative error of at most 0.011.
Values may be sent and summed in bfloat16 or wider, within the bound.
No kernel may reach another device: no remote copies, remote signals or barrier semaphores. Data moves between devices by JAX's collectives and lax.ppermute only.
A program may use at most 192 MiB of HBM per device.

```python
import math
import jax
import jax.numpy as jnp
import numpy as np
from jax import lax

D = 1536
HEADS = 48
HEAD_DIM = 64
STATE = 128
CONV = 4
TOK_DEV = 256
MB = 2
DOCS = 4
INNER = 3072
TOKENS = 1024
N_PIPE = 2
N_ROW = 4


def strengthened(values, own_key, source, target, blocks, factor):
    def block_of(dim):
        return (jnp.arange(values.shape[dim]) // (values.shape[dim] // blocks)).reshape((-1,) + (1,) * (values.ndim - 1 - dim))

    near = jax.random.permutation(own_key, blocks)[block_of(target)]
    far = (block_of(target) + blocks // 2) % blocks
    return jnp.where((block_of(source) == near) | (block_of(source) == far), factor * values, values)


def steps_of(stream_key, extent, pieces, least, largest):
    def one(dim, shards_of):
        draws = jax.random.uniform(jax.random.fold_in(jax.random.fold_in(stream_key, 6), dim), (shards_of,), jnp.float32, least / len(pieces), largest / len(pieces))
        return jnp.repeat(jnp.exp(draws), extent[dim] // shards_of).reshape((-1,) + (1,) * (len(extent) - dim - 1))

    gain = one(*pieces[0])
    for cut in pieces[1:]:
        gain = gain * one(*cut)
    return gain


def profile(count, total, limit, lean):
    portions = [(1 << 20) // math.isqrt(standing ** lean) + 1 for standing in range(2, count + 1)]
    spare, given = total - limit - (count - 1), [1] * (count - 1)
    while spare > 0:
        movable = [i for i in range(count - 1) if given[i] < limit]
        pool, budget = sum([portions[i] for i in movable]), spare
        for i in movable:
            more = min(limit - given[i], max(1, budget * portions[i] // pool), spare)
            given[i] = given[i] + more
            spare = spare - more
    return np.array([limit] + given)


def ragged_sizes(own_key, amount, total, bound, lean):
    if amount == 2:
        one = jax.random.randint(own_key, (), max(1, total - bound), min(bound, total - 1) + 1)
        return jnp.stack([one, total - one])
    tallies = jnp.asarray(profile(amount, total, bound, lean), jnp.int32)
    couples = (amount - 1) // 2
    donor, taker = tallies[1:1 + 2 * couples:2], tallies[2:2 + 2 * couples:2]
    slack = jnp.minimum(donor - 1, bound - taker)
    moved = jax.random.randint(jax.random.fold_in(own_key, 1), (couples,), 0, 1 << 20) % (slack + 1)
    tallies = tallies.at[1:1 + 2 * couples:2].set(donor - moved).at[2:2 + 2 * couples:2].set(taker + moved)
    return tallies[jax.random.permutation(jax.random.fold_in(own_key, 2), amount)]


def normal_values(rng, dims, deviation, most, split=(), dtype=jnp.bfloat16):
    values = deviation * jax.random.normal(rng, dims, jnp.float32)
    if split:
        values = values * steps_of(rng, dims, split, -0.22, 0.18)
    return jnp.clip(values, -most, most).astype(dtype)


def bell_draw_with(stream_key, extent, spread, most, split, heavy, dtype=jnp.bfloat16):
    values = spread * jax.random.normal(stream_key, extent, jnp.float32)
    if split:
        values = values * steps_of(stream_key, extent, split, -0.22, 0.18)
    return jnp.clip(strengthened(values, jax.random.fold_in(stream_key, 3), *heavy), -most, most).astype(dtype)


def setup_inputs(seed: int = 0) -> dict:
    arg_keys = jax.random.split(jax.random.key(seed), 19)
    inputs = bell_draw_with(arg_keys[0], (MB, TOKENS, D), 1.0, 6.0, ((1, 4),), (1, 2, 4, 2.0))
    cotangent = normal_values(arg_keys[1], (MB, TOKENS, D), 1.0, 6.0, ((1, 4),))
    segment_ids = jax.vmap(lambda own: jnp.searchsorted(jnp.cumsum(ragged_sizes(own, DOCS, TOKENS, TOKENS // 2, 1)), jnp.arange(TOKENS), side="right"))(jax.random.split(arg_keys[2], MB)).reshape((MB, TOKENS)).astype(jnp.int32)
    batch_order = jax.random.permutation(arg_keys[3], MB).astype(jnp.int32)
    norm_gain = jnp.clip(1.0 + 0.1 * jax.random.normal(arg_keys[4], (N_PIPE, D), jnp.float32), 0.5, 1.5)
    gate_proj = normal_values(arg_keys[5], (N_PIPE, D, INNER), D ** -0.5, 0.15625, ((0, 2), (1, 4), (2, 4)))
    value_proj = normal_values(arg_keys[6], (N_PIPE, D, INNER), D ** -0.5, 0.15625, ((0, 2), (1, 4), (2, 4)))
    step_proj = normal_values(arg_keys[7], (N_PIPE, D, HEADS), D ** -0.5, 0.15625, ((0, 2), (1, 4), (2, 4)))
    state_proj = normal_values(arg_keys[8], (N_PIPE, D, 2 * STATE), D ** -0.5, 0.15625, ((0, 2), (1, 4)))
    conv_value = normal_values(arg_keys[9], (N_PIPE, CONV, INNER), CONV ** -0.5, 3.0, ((0, 2), (2, 4)), jnp.float32)
    conv_value_bias = normal_values(arg_keys[10], (N_PIPE, INNER), 0.5, 3.0, ((0, 2), (1, 4)), jnp.float32)
    conv_state = normal_values(arg_keys[11], (N_PIPE, CONV, 2 * STATE), CONV ** -0.5, 3.0, ((0, 2),), jnp.float32)
    conv_state_bias = normal_values(arg_keys[12], (N_PIPE, 2 * STATE), 0.5, 3.0, ((0, 2),), jnp.float32)
    step_bias = jnp.clip(-6.0 + 4.0 * jax.random.uniform(arg_keys[13], (N_PIPE, HEADS), jnp.float32) ** steps_of(arg_keys[13], (N_PIPE, HEADS), ((0, 2), (1, 4)), -0.2, 0.2), -6.0, -2.0)
    decay_log = jnp.clip(2.7 * jax.random.uniform(arg_keys[14], (N_PIPE, HEADS), jnp.float32) ** steps_of(arg_keys[14], (N_PIPE, HEADS), ((0, 2), (1, 4)), -0.2, 0.2), 0.0, 2.7)
    skip_gain = jnp.clip(0.5 + 1.0 * jax.random.uniform(arg_keys[15], (N_PIPE, HEADS), jnp.float32) ** steps_of(arg_keys[15], (N_PIPE, HEADS), ((0, 2), (1, 4)), -0.2, 0.2), 0.5, 1.5)
    gate_gain = jnp.clip(1.0 + 0.1 * jax.random.normal(arg_keys[16], (N_PIPE, INNER), jnp.float32), 0.5, 1.5)
    out_proj = normal_values(arg_keys[17], (N_PIPE, INNER, D), INNER ** -0.5, 0.109375, ((0, 2), (1, 4), (2, 4)))
    return {"inputs": inputs, "cotangent": cotangent, "segment_ids": segment_ids, "batch_order": batch_order, "norm_gain": norm_gain, "gate_proj": gate_proj, "value_proj": value_proj, "step_proj": step_proj, "state_proj": state_proj, "conv_value": conv_value, "conv_value_bias": conv_value_bias, "conv_state": conv_state, "conv_state_bias": conv_state_bias, "step_bias": step_bias, "decay_log": decay_log, "skip_gain": skip_gain, "gate_gain": gate_gain, "out_proj": out_proj}


EPSILON = 1e-05
PRECISE = lax.Precision.HIGHEST

@jax.custom_vjp
def low(v):
    return lax.optimization_barrier(v.astype(jnp.bfloat16)).astype(jnp.float32)

@jax.custom_vjp
def low_back(v):
    return v

def low_keep(v):
    return (low(v), None)

def low_pass(kept, grad):
    return (grad,)

def back_keep(v):
    return (v, None)

def back_low(kept, grad):
    return (low(grad),)
low.defvjp(low_keep, low_pass)
low_back.defvjp(back_keep, back_low)

def pre_norm(values, gain_row):
    scale_row = lax.rsqrt(lax.optimization_barrier(jnp.mean(values * values, axis=-1, keepdims=True)) + EPSILON)
    return values * scale_row * gain_row[None, :]

def causal_conv(values, halo_vals, seg_now, seg_halo, weight, bias_row):
    taps = weight.shape[0]
    length = values.shape[0]
    extended = jnp.concatenate([halo_vals, values], axis=0)
    seg_ext = jnp.concatenate([seg_halo, seg_now], axis=0)
    summed = jnp.zeros_like(values) + bias_row[None, :]
    for offset in range(taps):
        shifted = extended[offset:offset + length]
        same_seg = (seg_ext[offset:offset + length] == seg_now).astype(jnp.float32)
        summed = summed + weight[offset][None, :] * shifted * same_seg[:, None]
    return jax.nn.silu(summed)

def mixer_inputs(value_pre, state_pre, halo_value, halo_state, conv_vw, conv_vb, conv_sw, conv_sb, step_raw, step_bias, decay_log, seg_now, seg_halo):
    value_conv = causal_conv(value_pre, halo_value, seg_now, seg_halo, conv_vw, conv_vb)
    state_conv = causal_conv(state_pre, halo_state, seg_now, seg_halo, conv_sw, conv_sb)
    half_width = state_conv.shape[1] // 2
    step_size = jax.nn.softplus(step_raw + step_bias[None, :])
    decay_rates = -step_size * jnp.exp(decay_log)[None, :]
    return (value_conv, state_conv[:, :half_width], state_conv[:, half_width:], step_size, decay_rates)

def decay_sums(decay_rates):
    length = decay_rates.shape[0]
    positions = jnp.arange(length)
    lower = (positions[:, None] >= positions[None, :]).astype(jnp.float32)
    return jnp.dot(lower, decay_rates, precision=PRECISE)

def block_output(value_conv, b_mat, c_mat, step_size, decay_rates, skip_gain, gate_act, carried, seg_now, seg_prev):
    length, head_count = step_size.shape
    value_heads = value_conv.reshape(length, head_count, -1)
    decay_cum = decay_sums(decay_rates)
    positions = jnp.arange(length)
    same_doc = (positions[:, None] >= positions[None, :]) & (seg_now[:, None] == seg_now[None, :])
    decay_gap = jnp.where(same_doc[:, :, None], decay_cum[:, None, :] - decay_cum[None, :, :], 0.0)
    mixing = jnp.where(same_doc[:, :, None], jnp.exp(decay_gap), 0.0)
    scores = jnp.dot(c_mat, b_mat.T, precision=PRECISE)
    weights = mixing * scores[:, :, None] * step_size[None, :, :]
    result = jnp.einsum('tsh,shp->thp', weights, value_heads, precision=PRECISE)
    carry_in = (seg_now == seg_prev).astype(jnp.float32)[:, None] * jnp.exp(decay_cum)
    result = result + carry_in[:, :, None] * jnp.einsum('tn,hpn->thp', c_mat, carried, precision=PRECISE)
    result = result + skip_gain[None, :, None] * value_heads
    gated_out = result.reshape(length, -1) * jax.nn.silu(gate_act)
    return (gated_out, lax.optimization_barrier(jnp.sum(gated_out * gated_out, axis=1)))

def block_state(value_conv, b_mat, step_size, decay_rates, seg_now, seg_prev):
    length, head_count = step_size.shape
    value_heads = value_conv.reshape(length, head_count, -1)
    decay_cum = decay_sums(decay_rates)
    last_cum = decay_cum[length - 1]
    inside = (seg_now == seg_now[length - 1]).astype(jnp.float32)
    lead_weight = inside[:, None] * jnp.exp(last_cum[None, :] - decay_cum) * step_size
    state_local = jnp.einsum('sh,shp,sn->hpn', lead_weight, value_heads, b_mat, precision=PRECISE)
    through = jnp.exp(last_cum) * (seg_now[length - 1] == seg_prev).astype(jnp.float32)
    return (through, state_local)

def gate_norm(gated_out, sumsq_total, gain_row, norm_width):
    return gated_out * lax.rsqrt(sumsq_total[:, None] / norm_width + EPSILON) * gain_row[None, :]

def mamba_layer(layer_in, seg_now, layer_params):
    gain_in, gate_w, value_w, step_w, state_w, conv_vw, conv_vb, conv_sw, conv_sb, step_b, decay_l, skip_g, gate_g, out_w = layer_params
    normed = low(pre_norm(layer_in, gain_in))
    gate_act = low_back(jnp.dot(normed, gate_w, precision=PRECISE))
    value_pre = low_back(jnp.dot(normed, value_w, precision=PRECISE))
    state_pre = low_back(jnp.dot(normed, state_w, precision=PRECISE))
    step_raw = low_back(jnp.dot(normed, step_w, precision=PRECISE))
    rim_rows = conv_vw.shape[0] - 1
    seg_halo = jnp.full((rim_rows,), -1.0, jnp.float32)
    mixed = mixer_inputs(value_pre, state_pre, jnp.zeros((rim_rows, INNER), jnp.float32), jnp.zeros((rim_rows, 2 * STATE), jnp.float32), conv_vw, conv_vb, conv_sw, conv_sb, step_raw, step_b, decay_l, seg_now, seg_halo)
    value_conv, b_mat, c_mat, step_size, decay_rates = mixed
    blocked = tuple((array.reshape((N_ROW, TOK_DEV) + array.shape[1:]) for array in (value_conv, b_mat, c_mat, step_size, decay_rates, gate_act, seg_now)))

    def one_block(carried_pair, block_data):
        carried, seg_prev = carried_pair
        value_blk, b_blk, c_blk, step_blk, rate_blk, gate_blk, seg_blk = block_data
        gated_out, squares = block_output(value_blk, b_blk, c_blk, step_blk, rate_blk, skip_g, gate_blk, carried, seg_blk, seg_prev)
        through, state_local = block_state(value_blk, b_blk, step_blk, rate_blk, seg_blk, seg_prev)
        renewed = through[:, None, None] * carried + state_local
        return ((renewed, seg_blk[TOK_DEV - 1]), (gated_out, squares))
    start_pair = (jnp.zeros((HEADS, HEAD_DIM, STATE), jnp.float32), jnp.array(-1.0, jnp.float32))
    final_pair, (gated_all, squares_all) = lax.scan(jax.checkpoint(one_block), start_pair, blocked)
    gated_all = gated_all.reshape(TOKENS, INNER)
    squares_all = squares_all.reshape(TOKENS)
    branch = low(gate_norm(gated_all, squares_all, gate_g, INNER))
    out_branch = low_back(jnp.dot(branch, out_w, precision=PRECISE))
    return layer_in + out_branch

def reference(inputs, cotangent, segment_ids, batch_order, norm_gain, gate_proj, value_proj, step_proj, state_proj, conv_value, conv_value_bias, conv_state, conv_state_bias, step_bias, decay_log, skip_gain, gate_gain, out_proj):
    params = tuple((array.astype(jnp.float32) for array in (norm_gain, gate_proj, value_proj, step_proj, state_proj, conv_value, conv_value_bias, conv_state, conv_state_bias, step_bias, decay_log, skip_gain, gate_gain, out_proj)))
    inputs_f32 = inputs.astype(jnp.float32)
    seg_all = segment_ids.astype(jnp.float32)
    probe = jnp.zeros((N_PIPE - 1, MB, TOKENS, D), jnp.float32)
    layered = jax.checkpoint(mamba_layer)

    def whole(inputs_in, probe_in, params_in):

        def one_batch(unused_carry, batch_slot):
            source_row = batch_order[batch_slot]
            current = inputs_in[source_row]
            seg_now = seg_all[source_row]
            produced = []
            for layer_index in range(N_PIPE):
                layer_params = tuple((array[layer_index] for array in params_in))
                current = layered(current, seg_now, layer_params)
                if layer_index + 1 < N_PIPE:
                    current = low_back(low(current)) + probe_in[layer_index, batch_slot]
                produced.append(current)
            return (unused_carry, jnp.stack(produced))
        final_carry, stacked = lax.scan(one_batch, jnp.zeros((), jnp.float32), jnp.arange(MB))
        return jnp.transpose(stacked, (1, 0, 2, 3))
    primal, pullback = jax.vjp(whole, inputs_f32, probe, params)
    cot_full = jnp.concatenate([jnp.zeros((N_PIPE - 1, MB, TOKENS, D), jnp.float32), cotangent.astype(jnp.float32)[None]], axis=0)
    grad_inputs, grad_probe, grad_params = pullback(cot_full)
    input_grads = jnp.concatenate([grad_inputs[None], grad_probe], axis=0)
    return (primal.astype(jnp.bfloat16), input_grads, grad_params[0], grad_params[1], grad_params[2], grad_params[3], grad_params[4], grad_params[5], grad_params[6], grad_params[7], grad_params[8], grad_params[9], grad_params[10], grad_params[11], grad_params[12], grad_params[13])
```

```python
import functools
import math

import jax
import jax.numpy as jnp
from jax import lax
from jax.experimental import pallas as pl
from jax.experimental.pallas import tpu as pltpu
from jax.sharding import PartitionSpec as P

EPSILON = 1e-05
LOG2E = math.log2(math.e)
LANE = 128
F32 = jnp.float32
BF16 = jnp.bfloat16
SMALL_ROWS = 16


def dot_nn(a, b):
    return lax.dot_general(a, b, (((1,), (0,)), ((), ())), preferred_element_type=F32)


def dot_nt(a, b):
    return lax.dot_general(a, b, (((1,), (1,)), ((), ())), preferred_element_type=F32)


def dot_tn(a, b):
    return lax.dot_general(a, b, (((0,), (0,)), ((), ())), preferred_element_type=F32)


def dot_exact(a, b):
    return lax.dot_general(
        a, b, (((1,), (0,)), ((), ())), precision=lax.Precision.HIGHEST, preferred_element_type=F32
    )


def sigmoid(v):
    return 1.0 / (1.0 + jnp.exp(-v))


def split_pair(v):
    high = v.astype(BF16)
    return high, (v - high.astype(F32)).astype(BF16)


def on_chip(kernel, out_shapes, scratch=()):
    whole = pl.BlockSpec(memory_space=pltpu.VMEM)

    def call(*operands):
        return pl.pallas_call(
            kernel,
            out_shape=out_shapes,
            in_specs=[whole] * len(operands),
            out_specs=jax.tree.map(lambda _: whole, out_shapes),
            scratch_shapes=scratch,
            compiler_params=pltpu.CompilerParams(vmem_limit_bytes=60 * 1024 * 1024),
        )(*operands)

    return call


def shaped(shape, dtype=F32):
    return jax.ShapeDtypeStruct(shape, dtype)


def tile_of(q):
    return slice(q * LANE, (q + 1) * LANE)


def spread(columns, q, heads_tile, lane_head):
    first = q * heads_tile
    out = columns[:, first : first + 1]
    for i in range(1, heads_tile):
        out = jnp.where(lane_head == i, columns[:, first + i : first + i + 1], out)
    return out


def lane_heads(rows, heads_tile):
    lanes = lax.broadcasted_iota(jnp.int32, (rows, LANE), 1)
    return lanes // (LANE // heads_tile)


def tri_mask(tokens, seg_col, seg_row, transposed):
    first = lax.broadcasted_iota(jnp.int32, (tokens, tokens), 0)
    second = lax.broadcasted_iota(jnp.int32, (tokens, tokens), 1)
    order = first <= second if transposed else first >= second
    return order & (seg_col == seg_row)


def prep_kernel(
    inner, heads_tile, z_ref, halo_ref, aux_ref, taps_ref, heads_ref,
    conv_ref, value_ref, scaled_ref, bc_ref, step_ref, cum_ref, cumt_ref, lead_ref, carry_ref,
    msg_ref, ext_ref, leadu_ref,
):
    tokens = z_ref.shape[0]
    width = halo_ref.shape[1]
    aux = aux_ref[...]
    ext_ref[0:8, :] = halo_ref[...]
    ext_ref[8 : 8 + tokens, :] = z_ref[:, :width]
    raw = z_ref[:, width : width + LANE] + heads_ref[0:1, :]
    step = jnp.maximum(raw, 0.0) + jnp.log1p(jnp.exp(-jnp.abs(raw)))
    rates = -step * jnp.exp(heads_ref[1:2, :])
    rows = lax.broadcasted_iota(jnp.int32, (tokens, tokens), 0)
    cols = lax.broadcasted_iota(jnp.int32, (tokens, tokens), 1)
    cum = dot_exact((rows >= cols).astype(F32), rates) * LOG2E
    lead = aux[:, 5:6] * jnp.exp2(cum[tokens - 1 : tokens, :] - cum)
    carry = aux[:, 4:5] * jnp.exp2(cum)
    step_ref[...] = step
    cum_ref[...] = cum
    cumt_ref[...] = cum.T
    lead_ref[...] = lead
    carry_ref[...] = carry
    lane_head = lane_heads(tokens, heads_tile)
    for q in range(width // LANE):
        at = tile_of(q)
        acc = taps_ref[4:5, at] + taps_ref[3:4, at] * z_ref[:, at]
        for j in range(3):
            acc = acc + taps_ref[j : j + 1, at] * (aux[:, j : j + 1] * ext_ref[5 + j : 5 + j + tokens, at])
        conv_ref[:, at] = acc
        value = acc * sigmoid(acc)
        if q < inner // LANE:
            value_ref[:, at] = value
            scaled = spread(step, q, heads_tile, lane_head) * value
            scaled_ref[:, at] = scaled.astype(BF16)
            leadu_ref[:, at] = (spread(lead, q, heads_tile, lane_head) * scaled).astype(BF16)
        else:
            base = q - inner // LANE
            bc_ref[:, tile_of(base)] = value.astype(BF16)
    state = dot_tn(bc_ref[:, :LANE], leadu_ref[...])
    msg_ref[0:LANE, :] = state.astype(BF16)
    msg_ref[LANE:, :] = jnp.zeros((SMALL_ROWS, inner), BF16)
    lane_row = lane_heads(1, heads_tile)
    for q in range(inner // LANE):
        through = spread(carry[tokens - 1 : tokens, :], q, heads_tile, lane_row)
        high, low = split_pair(through)
        msg_ref[LANE : LANE + 1, tile_of(q)] = high
        msg_ref[LANE + 1 : LANE + 2, tile_of(q)] = low


def intra_kernel(
    inner, heads_tile, scaled_ref, value_ref, bc_ref, cum_ref, cumt_ref, aux_ref, segt_ref, heads_ref,
    out_ref,
):
    tokens = scaled_ref.shape[0]
    scores = dot_nt(bc_ref[:, LANE:], bc_ref[:, :LANE])
    scores = jnp.where(tri_mask(tokens, aux_ref[:, 3:4], segt_ref[0:1, :], False), scores, 0.0)
    lane_head = lane_heads(tokens, heads_tile)
    lane_row = lane_heads(1, heads_tile)
    for q in range(inner // LANE):
        at = tile_of(q)
        total = spread(heads_ref[2:3, :], q, heads_tile, lane_row) * value_ref[:, at]
        scaled = scaled_ref[:, at]
        for i in range(heads_tile):
            h = q * heads_tile + i
            gap = jnp.minimum(cum_ref[:, h : h + 1] - cumt_ref[h : h + 1, :], 0.0)
            mixed = (jnp.exp2(gap) * scores).astype(BF16)
            total = total + jnp.where(lane_head == i, dot_nn(mixed, scaled), 0.0)
        out_ref[:, at] = total


def enter_states(messages):
    state = None
    for message in reversed(messages):
        own = message[0:LANE, :].astype(F32)
        through = message[LANE : LANE + 1, :].astype(F32) + message[LANE + 1 : LANE + 2, :].astype(F32)
        state = own if state is None else own + through * state
    return state


def gate_kernel(
    inner, heads_tile, count, with_grad, intra_ref, bc_ref, carry_ref, gate_ref, gain_ref, *refs
):
    messages = refs[:count]
    refs = refs[count:]
    if with_grad:
        branch_grad_ref, refs = refs[0], refs[1:]
    ssd_ref, state_ref, gated_ref, sums_ref = refs
    tokens = intra_ref.shape[0]
    state = enter_states([m[...] for m in messages]).astype(BF16)
    state_ref[...] = state
    inter = dot_nn(bc_ref[:, LANE:], state)
    lane_head = lane_heads(tokens, heads_tile)
    carry = carry_ref[...]
    squares = jnp.zeros((tokens, LANE), F32)
    products = jnp.zeros((tokens, LANE), F32)
    for q in range(inner // LANE):
        at = tile_of(q)
        ssd = intra_ref[:, at] + spread(carry, q, heads_tile, lane_head) * inter[:, at]
        ssd_ref[:, at] = ssd
        gate = gate_ref[:, at]
        gated = ssd * (gate * sigmoid(gate))
        squares = squares + gated * gated
        scaled = gated * gain_ref[0:1, at]
        gated_ref[:, at] = scaled.astype(BF16)
        if with_grad:
            products = products + scaled * branch_grad_ref[:, at]
    total = jnp.sum(squares, axis=1, keepdims=True)
    lanes = lax.broadcasted_iota(jnp.int32, (tokens, LANE), 1)
    packed = jnp.where(lanes == 0, total, 0.0)
    if with_grad:
        packed = packed + jnp.where(lanes == 1, jnp.sum(products, axis=1, keepdims=True), 0.0)
        sums_ref[...] = packed.T[0:8, :]
    else:
        sums_ref[...] = packed


def ungate_kernel(
    inner, heads_tile, norm_width, branch_grad_ref, norm_ref, gate_ref, ssd_ref, gain_ref, carry_ref, bc_ref,
    gssd_ref, ggate_ref, branch_ref, msg_ref, ggain_ref, cg_ref,
):
    tokens = branch_grad_ref.shape[0]
    rho = norm_ref[:, 0:1]
    pull = norm_ref[:, 1:2] * (rho * rho * rho / norm_width)
    lane_head = lane_heads(tokens, heads_tile)
    carry = carry_ref[...]
    ggain_ref[...] = jnp.zeros(ggain_ref.shape, F32)
    for q in range(inner // LANE):
        at = tile_of(q)
        gate = gate_ref[:, at]
        sig = sigmoid(gate)
        ssd = ssd_ref[:, at]
        gated = ssd * (gate * sig)
        grad = branch_grad_ref[:, at]
        gain = gain_ref[0:1, at]
        normed = gated * rho
        ggain_ref[0:1, at] = jnp.sum(grad * normed, axis=0, keepdims=True)
        branch_ref[:, at] = (normed * gain).astype(BF16)
        ggated = rho * (gain * grad) - gated * pull
        gssd = ggated * (gate * sig)
        gssd_ref[:, at] = gssd
        ggate_ref[:, at] = (ggated * ssd * (sig * (1.0 + gate * (1.0 - sig)))).astype(BF16)
        cg_ref[:, at] = (spread(carry, q, heads_tile, lane_head) * gssd).astype(BF16)
    msg_ref[0:LANE, :] = dot_tn(bc_ref[:, LANE:], cg_ref[...]).astype(BF16)
    msg_ref[LANE:, :] = jnp.zeros((SMALL_ROWS, inner), BF16)
    lane_row = lane_heads(1, heads_tile)
    for q in range(inner // LANE):
        through = spread(carry[tokens - 1 : tokens, :], q, heads_tile, lane_row)
        high, low = split_pair(through)
        msg_ref[LANE : LANE + 1, tile_of(q)] = high
        msg_ref[LANE + 1 : LANE + 2, tile_of(q)] = low


def intra_grad_kernel(
    inner, heads_tile, scaled_ref, gssd_ref, bc_ref, cum_ref, cumt_ref, aux_ref, segt_ref,
    gscaled_ref, gbc_ref, gcum_ref, sums_ref,
):
    tokens = scaled_ref.shape[0]
    mask = tri_mask(tokens, aux_ref[:, 3:4], segt_ref[0:1, :], True)
    scores = jnp.where(mask, dot_nt(bc_ref[:, :LANE], bc_ref[:, LANE:]), 0.0)
    lane_head = lane_heads(tokens, heads_tile)
    gscores = jnp.zeros((tokens, tokens), F32)
    gcum_ref[...] = jnp.zeros(gcum_ref.shape, F32)
    sums_ref[...] = jnp.zeros(sums_ref.shape, F32)
    for q in range(inner // LANE):
        at = tile_of(q)
        grad = gssd_ref[:, at].astype(BF16)
        scaled = scaled_ref[:, at]
        total = jnp.zeros((tokens, LANE), F32)
        for i in range(heads_tile):
            h = q * heads_tile + i
            gap = jnp.minimum(cumt_ref[h : h + 1, :] - cum_ref[:, h : h + 1], 0.0)
            decay = jnp.exp2(gap)
            mixed = decay * scores
            picked = jnp.where(lane_head == i, scaled, jnp.zeros_like(scaled))
            gmixed = dot_nt(picked, grad)
            total = total + jnp.where(lane_head == i, dot_nn(mixed.astype(BF16), grad), 0.0)
            product = gmixed * mixed
            sums_ref[h : h + 1, :] = jnp.sum(product, axis=0, keepdims=True)
            gcum_ref[:, h : h + 1] = -jnp.sum(product, axis=1, keepdims=True)
            gscores = gscores + gmixed * decay
        gscaled_ref[:, at] = total
    gscores = jnp.where(mask, gscores, 0.0)
    gbc_ref[:, :LANE] = dot_nn(gscores.astype(BF16), bc_ref[:, LANE:])
    gbc_ref[:, LANE:] = dot_nn(gscores.T.astype(BF16), bc_ref[:, :LANE])
    gcum_ref[...] = gcum_ref[...] + sums_ref[...].T


def inter_grad_kernel(
    inner, heads_tile, count, state_ref, scaled_ref, value_ref, gssd_ref, gscaled_ref, bc_ref, gbc_ref, gcum_ref,
    step_ref, lead_ref, carry_ref, z_ref, halo_ref, conv_ref, aux_ref, taps_ref, heads_ref, pick_ref, *refs,
):
    messages = refs[:count]
    (
        gpre_ref, gstep_ref, gtaps_ref, gheads_ref,
        ext_ref, em_ref, leadu_ref, cg_ref, gain_ref, lose_ref, gsize_ref,
    ) = refs[count:]
    tokens = scaled_ref.shape[0]
    width = halo_ref.shape[1]
    aux = aux_ref[...]
    adjoint = enter_states([m[...] for m in messages])
    adjoint_low = adjoint.astype(BF16)
    state = state_ref[...]
    from_adjoint = dot_nn(bc_ref[:, :LANE], adjoint_low)
    from_state = dot_nn(bc_ref[:, LANE:], state)
    overlap = jnp.sum(adjoint * state.astype(F32), axis=0, keepdims=True)
    lane_head = lane_heads(tokens, heads_tile)
    lane_row = lane_heads(1, heads_tile)
    step = step_ref[...]
    lead = lead_ref[...]
    carry = carry_ref[...]
    ext_ref[0:8, :] = halo_ref[...]
    ext_ref[8 : 8 + tokens, :] = z_ref[:, :width]
    em_ref[0:8, :] = jnp.zeros((8, LANE), F32)
    em_ref[8 + tokens :, :] = jnp.zeros((8, LANE), F32)
    gtaps_ref[...] = jnp.zeros(gtaps_ref.shape, F32)
    gheads_ref[...] = jnp.zeros(gheads_ref.shape, F32)

    def through_conv(q, grad):
        at = tile_of(q)
        conv = conv_ref[:, at]
        sig = sigmoid(conv)
        e = grad * (sig * (1.0 + conv * (1.0 - sig)))
        gtaps_ref[4:5, at] = jnp.sum(e, axis=0, keepdims=True)
        gtaps_ref[3:4, at] = jnp.sum(e * z_ref[:, at], axis=0, keepdims=True)
        total = None
        for j in range(3):
            masked = aux[:, j : j + 1] * e
            gtaps_ref[j : j + 1, at] = jnp.sum(masked * ext_ref[5 + j : 5 + j + tokens, at], axis=0, keepdims=True)
            em_ref[8 : 8 + tokens, :] = masked
            term = taps_ref[j : j + 1, at] * em_ref[3 - j : 11 - j + tokens, :]
            total = term if total is None else total + term
        gpre_ref[0:8, at] = total[0:8, :]
        gpre_ref[8:, at] = total[8:, :] + taps_ref[3:4, at] * e

    for q in range(inner // LANE):
        at = tile_of(q)
        scaled = scaled_ref[:, at].astype(F32)
        grad = gssd_ref[:, at]
        value = value_ref[:, at]
        leads = spread(lead, q, heads_tile, lane_head)
        carries = spread(carry, q, heads_tile, lane_head)
        pushed = leads * from_adjoint[:, at]
        gscaled = gscaled_ref[:, at] + pushed
        carried = carries * grad
        leadu_ref[:, at] = (leads * scaled).astype(BF16)
        cg_ref[:, at] = carried.astype(BF16)
        gain_ref[:, at] = (carried * from_state[:, at]).astype(BF16)
        lose_ref[:, at] = (scaled * pushed).astype(BF16)
        gsize_ref[:, at] = (gscaled * value).astype(BF16)
        gtaps_ref[5:6, at] = jnp.sum(grad * value, axis=0, keepdims=True)
        gvalue = spread(step, q, heads_tile, lane_head) * gscaled
        gvalue = gvalue + spread(heads_ref[2:3, :], q, heads_tile, lane_row) * grad
        through_conv(q, gvalue)
    gb = gbc_ref[:, :LANE] + dot_nt(leadu_ref[...], adjoint_low)
    gc = gbc_ref[:, LANE:] + dot_nt(cg_ref[...], state)
    through_conv(inner // LANE, gb)
    through_conv(inner // LANE + 1, gc)
    pick = pick_ref[...]
    lose = dot_nn(lose_ref[...], pick)
    gcum = gcum_ref[...] + dot_nn(gain_ref[...], pick) - lose
    high, low = split_pair(overlap)
    ends = dot_nn(jnp.broadcast_to(high, (8, inner)), pick) + dot_nn(jnp.broadcast_to(low, (8, inner)), pick)
    last = carry[tokens - 1 : tokens, :] * ends[0:1, :] + jnp.sum(lose, axis=0, keepdims=True)
    row_of = lax.broadcasted_iota(jnp.int32, (tokens, LANE), 0)
    gcum = gcum + jnp.where(row_of == tokens - 1, last, 0.0)
    rows = lax.broadcasted_iota(jnp.int32, (tokens, tokens), 0)
    cols = lax.broadcasted_iota(jnp.int32, (tokens, tokens), 1)
    grate = dot_exact((rows <= cols).astype(F32), gcum)
    speed = jnp.exp(heads_ref[1:2, :])
    gsize = dot_nn(gsize_ref[...], pick) - speed * grate
    raw = z_ref[:, width : width + LANE] + heads_ref[0:1, :]
    graw = gsize * sigmoid(raw)
    gstep_ref[...] = graw.astype(BF16)
    gheads_ref[0:1, :] = jnp.sum(graw, axis=0, keepdims=True)
    gheads_ref[1:2, :] = jnp.sum(grate * (-speed * step), axis=0, keepdims=True)


def permute(block, axis, route):
    return lax.ppermute(block, axis, route)


def from_before(block, count, distance):
    return permute(block, "row", [(i, i + distance) for i in range(count - distance)])


def from_after(block, count, distance):
    return permute(block, "row", [(i + distance, i) for i in range(count - distance)])


def swapped(block):
    return permute(block, "pipe", [(0, 1), (1, 0)])


def col_sum(block):
    count = lax.axis_size("col")
    rows = block.shape[0] // count
    parts = lax.all_to_all(block.reshape(count, rows, block.shape[1]), "col", 0, 0)
    own = jnp.sum(parts.astype(F32), axis=0)
    return own


def col_gather(block):
    return lax.all_gather(block, "col", axis=0, tiled=True)


def local(
    inputs, cotangent, segment_ids, batch_order, norm_gain, gate_proj, value_proj, step_proj, state_proj,
    conv_value, conv_value_bias, conv_state, conv_state_bias, step_bias, decay_log, skip_gain, gate_gain, out_proj,
):
    core = lax.axis_index("pipe")
    first = core == 0
    rows = lax.axis_size("row")
    row = lax.axis_index("row")
    tokens, width = inputs.shape[1], inputs.shape[2]
    shard = gate_proj.shape[1]
    inner = gate_proj.shape[2]
    heads = step_proj.shape[2]
    states = state_proj.shape[2] // 2
    heads_tile = LANE // (inner // heads)
    half = inner // 2
    conv_width = inner + 2 * states
    norm_width = inner * lax.axis_size("col")
    distances = range(1, rows)

    def pick_mine(a, b):
        return jnp.where(first, a, b)

    step_pad = jnp.pad(step_proj[0], ((0, 0), (0, LANE - heads)))
    out_t = out_proj[0].T
    packs_a = [
        jnp.concatenate(
            [value_proj[0][:, i * half : (i + 1) * half], state_proj[0][:, i * states : (i + 1) * states], step_pad],
            axis=1,
        )
        for i in range(2)
    ]
    packs_b = [
        jnp.concatenate([gate_proj[0][:, i * half : (i + 1) * half], out_t[:, i * half : (i + 1) * half]], axis=1)
        for i in range(2)
    ]
    keep_a, give_a = pick_mine(packs_a[0], packs_a[1]), pick_mine(packs_a[1], packs_a[0])
    keep_b, give_b = pick_mine(packs_b[0], packs_b[1]), pick_mine(packs_b[1], packs_b[0])
    take_a, take_b = swapped(give_a), swapped(give_b)
    gather = functools.partial(lax.all_gather, axis_name="row", axis=0, tiled=True)
    mine_a = [gather(pick_mine(keep_a, take_a))]
    mine_b = [gather(pick_mine(keep_b, take_b))]
    mine_a.append(gather(pick_mine(take_a, keep_a)))
    mine_b.append(gather(pick_mine(take_b, keep_b)))
    other_a = [swapped(w) for w in mine_a]
    other_b = [swapped(w) for w in mine_b]

    small = jnp.concatenate(
        [
            v.reshape(-1)
            for v in (norm_gain, conv_value, conv_value_bias, conv_state, conv_state_bias, step_bias, decay_log, skip_gain, gate_gain)
        ]
    )
    small_other = swapped(small)
    smalls = (pick_mine(small, small_other), pick_mine(small_other, small))

    def unpack(vector):
        out, at = [], 0
        for v in (norm_gain, conv_value, conv_value_bias, conv_state, conv_state_bias, step_bias, decay_log, skip_gain, gate_gain):
            out.append(vector[at : at + v.size].reshape(v.shape[1:]))
            at += v.size
        gain_in, cvw, cvb, csw, csb, sbias, dlog, skip, gain_out = out
        taps = jnp.concatenate(
            [jnp.concatenate([cvw, csw], axis=1), jnp.concatenate([cvb, csb])[None], jnp.zeros((3, conv_width), F32)], axis=0
        )
        head_rows = jnp.pad(jnp.stack([sbias, dlog, skip]), ((0, 5), (0, LANE - heads)))
        return gain_in, taps, head_rows, gain_out[None]

    params = [unpack(v) for v in smalls]

    source = batch_order[core]
    layer_in = inputs[source]
    seg = segment_ids[source].astype(F32)
    seg_before = from_before(seg[-3:], rows, 1)
    seg_before = jnp.where(row == 0, -1.0, seg_before)
    seg_ext = jnp.concatenate([seg_before, seg])
    same = [(seg_ext[j : j + tokens] == seg).astype(F32) for j in range(3)]
    carry_mask = (seg == seg_before[2]).astype(F32)
    inside = (seg == seg[tokens - 1]).astype(F32)
    aux = jnp.pad(jnp.stack(same + [seg, carry_mask, inside], axis=1), ((0, 0), (0, LANE - 6)))
    seg_t = jnp.broadcast_to(seg[None], (8, tokens))
    pick = (
        (lax.broadcasted_iota(jnp.int32, (inner, LANE), 0) // (inner // heads))
        == lax.broadcasted_iota(jnp.int32, (inner, LANE), 1)
    ).astype(BF16)

    prep = on_chip(
        functools.partial(prep_kernel, inner, heads_tile),
        (
            shaped((tokens, conv_width)), shaped((tokens, inner)), shaped((tokens, inner), BF16),
            shaped((tokens, 2 * states), BF16), shaped((tokens, LANE)), shaped((tokens, LANE)), shaped((LANE, tokens)),
            shaped((tokens, LANE)), shaped((tokens, LANE)), shaped((states + SMALL_ROWS, inner), BF16),
        ),
        [pltpu.VMEM((tokens + 8, conv_width), F32), pltpu.VMEM((tokens, inner), BF16)],
    )
    intra = on_chip(functools.partial(intra_kernel, inner, heads_tile), shaped((tokens, inner)))
    gate_outs = (shaped((tokens, inner)), shaped((states, inner), BF16), shaped((tokens, inner), BF16))
    gates = [
        on_chip(
            functools.partial(gate_kernel, inner, heads_tile, rows - 1, with_grad),
            gate_outs + (shaped((8, tokens)) if with_grad else shaped((tokens, LANE)),),
        )
        for with_grad in (False, True)
    ]
    ungate = on_chip(
        functools.partial(ungate_kernel, inner, heads_tile, norm_width),
        (
            shaped((tokens, inner)), shaped((tokens, inner), BF16), shaped((tokens, inner), BF16),
            shaped((states + SMALL_ROWS, inner), BF16), shaped((8, inner)),
        ),
        [pltpu.VMEM((tokens, inner), BF16)],
    )
    intra_grad = on_chip(
        functools.partial(intra_grad_kernel, inner, heads_tile),
        (shaped((tokens, inner)), shaped((tokens, 2 * states)), shaped((tokens, LANE))),
        [pltpu.VMEM((LANE, tokens), F32)],
    )
    inter_grad = on_chip(
        functools.partial(inter_grad_kernel, inner, heads_tile, rows - 1),
        (
            shaped((tokens + 8, conv_width)), shaped((tokens, LANE), BF16), shaped((8, conv_width)), shaped((8, LANE)),
        ),
        [pltpu.VMEM((tokens + 8, conv_width), F32), pltpu.VMEM((tokens + 16, LANE), F32)]
        + [pltpu.VMEM((tokens, inner), BF16)] * 5,
    )

    def halves(a):
        return a[:, :half], a[:, half:]

    def joined(mine, other):
        return jnp.where(first, jnp.concatenate([mine, other], 1), jnp.concatenate([other, mine], 1))

    def project(layer, x):
        gain_in = params[layer][0]
        xf = x.astype(F32)
        scale = lax.rsqrt(jnp.mean(xf * xf, axis=-1, keepdims=True) + EPSILON)
        normed = (xf * scale * gain_in[None]).astype(BF16)
        za_mine = dot_nn(normed, mine_a[layer])
        za_other = dot_nn(normed, other_a[layer])
        z = jnp.concatenate(
            [
                joined(za_mine[:, :half], za_other[:, :half]),
                joined(za_mine[:, half : half + states], za_other[:, half : half + states]),
                za_mine[:, half + states :],
            ],
            axis=1,
        )
        halo = jnp.pad(from_before(z[tokens - 3 :, :conv_width], rows, 1), ((5, 0), (0, 0)))
        gate = joined(dot_nn(normed, mine_b[layer][:, :half]), dot_nn(normed, other_b[layer][:, :half]))
        return scale, normed, z, halo, gate

    def scan_part(layer, z, halo):
        taps, head_rows = params[layer][1:3]
        made = prep(z, halo, aux, taps, head_rows)
        conv, value, scaled, bc, step, cum, cumt, lead, carry, message = made
        messages = [from_before(message, rows, d) for d in distances]
        inside_part = intra(scaled, value, bc, cum, cumt, aux, seg_t, head_rows)
        return made, messages, inside_part

    def out_product(layer, gated):
        low, high = halves(gated)
        mine, other = pick_mine(low, high), pick_mine(high, low)
        return dot_nt(mine, mine_b[layer][:, half:]) + dot_nt(other, other_b[layer][:, half:])

    def branch_grad_of(layer, g_out):
        return joined(dot_nn(g_out, mine_b[layer][:, half:]), dot_nn(g_out, other_b[layer][:, half:]))

    scale0, normed0, z0, halo0, gate0 = project(0, layer_in)
    made0, messages0, inside0 = scan_part(0, z0, halo0)
    ssd0, state0, gated0, sums0 = gates[0](inside0, made0[3], made0[8], gate0, params[0][3], *messages0)
    partial0 = out_product(0, gated0)
    square_high, square_low = split_pair(sums0[:, :1])
    lanes_pad = jnp.zeros((tokens, LANE - 2), BF16)
    own0 = col_sum(jnp.concatenate([partial0.astype(BF16), square_high, square_low, lanes_pad], axis=1))
    own_square = own0[:, width : width + 1] + own0[:, width + 1 : width + 2]
    own_high, own_low = split_pair(own_square)
    full0 = col_gather(
        jnp.concatenate([own0[:, :width].astype(BF16), own_high, own_low, lanes_pad[: own_high.shape[0]]], axis=1)
    )
    raw0 = full0[:, :width].astype(F32)
    rho0 = lax.rsqrt(
        (full0[:, width : width + 1].astype(F32) + full0[:, width + 1 : width + 2].astype(F32)) / norm_width + EPSILON
    )
    x1 = (layer_in.astype(F32) + rho0 * raw0).astype(BF16)

    g_out1 = cotangent[core]
    scale1, normed1, z1, halo1, gate1 = project(1, x1)
    made1, messages1, inside1 = scan_part(1, z1, halo1)
    gbranch1 = branch_grad_of(1, g_out1)
    ssd1, state1, gated1, sums1 = gates[1](inside1, made1[3], made1[8], gate1, params[1][3], *messages1, gbranch1)
    totals1 = jnp.sum(lax.all_gather(sums1[0:8], "col"), axis=0)
    rho1 = lax.rsqrt(totals1[0] / norm_width + EPSILON)[:, None]
    norm1 = jnp.pad(jnp.concatenate([rho1, totals1[1][:, None]], axis=1), ((0, 0), (0, LANE - 2)))
    partial1 = out_product(1, gated1).astype(BF16)
    raw1 = lax.psum(partial1, "col")
    x2 = (x1.astype(F32) + rho1 * raw1.astype(F32)).astype(BF16)

    def backward(layer, x, g_sum, g_out, gbranch, norm, scale, normed, z, halo, gate, made, ssd, state):
        conv, value, scaled, bc, step, cum, cumt, lead, carry, _ = made
        gain_in, taps, head_rows, gain_out = params[layer]
        gssd, ggate, branch, message, ggain = ungate(gbranch, norm, gate, ssd, gain_out, carry, bc)
        messages = [from_after(message, rows, d) for d in distances]
        gscaled, gbc, gcum = intra_grad(scaled, gssd, bc, cum, cumt, aux, seg_t)
        gpre, gstep, gtaps, gheads = inter_grad(
            state, scaled, value, gssd, gscaled, bc, gbc, gcum, step, lead, carry, z, halo, conv, aux, taps, head_rows,
            pick, *messages,
        )
        from_next = from_after(gpre[5:8], rows, 1)
        gpre = jnp.concatenate([gpre[8 : tokens + 5], gpre[tokens + 5 :] + from_next], axis=0)
        glow = gpre.astype(BF16)
        v_low, v_high = halves(glow[:, :inner])
        s_low, s_high = glow[:, inner : inner + states], glow[:, inner + states :]
        ga_mine = jnp.concatenate([pick_mine(v_low, v_high), pick_mine(s_low, s_high)], axis=1)
        ga_other = jnp.concatenate([pick_mine(v_high, v_low), pick_mine(s_high, s_low)], axis=1)
        g_low, g_high = halves(ggate)
        gg_mine, gg_other = pick_mine(g_low, g_high), pick_mine(g_high, g_low)
        b_low, b_high = halves(branch)
        br_mine, br_other = pick_mine(b_low, b_high), pick_mine(b_high, b_low)
        ga_full = jnp.concatenate([ga_mine, gstep], axis=1)
        partial = dot_nt(ga_full, mine_a[layer]) + dot_nt(ga_other, other_a[layer][:, : half + states])
        partial = partial + dot_nt(gg_mine, mine_b[layer][:, :half]) + dot_nt(gg_other, other_b[layer][:, :half])
        own = col_sum(jnp.concatenate([partial.astype(BF16), glow[:, inner:]], axis=1))
        full = col_gather(own.astype(BF16))
        gnormed = full[:, :width].astype(F32)
        state_low = full[:, width:]
        xf = x.astype(F32)
        ggx = gnormed * gain_in[None]
        pull = jnp.sum(ggx * xf, axis=1, keepdims=True) * (scale * scale * scale / width)
        g_in = g_sum + scale * ggx - xf * pull
        ggain_in = jnp.sum(gnormed * xf * scale, axis=0)
        st_low, st_high = state_low[:, :states], state_low[:, states:]
        dw_b = [
            jnp.concatenate([dot_tn(normed, a), dot_tn(g_out, b)], axis=1).astype(BF16)
            for a, b in ((gg_mine, br_mine), (gg_other, br_other))
        ]
        dw_a = [
            dot_tn(normed, jnp.concatenate([v, s, gstep], axis=1)).astype(BF16)
            for v, s in (
                (pick_mine(v_low, v_high), pick_mine(st_low, st_high)),
                (pick_mine(v_high, v_low), pick_mine(st_high, st_low)),
            )
        ]

        def reduced(pair):
            both = (pair[0].astype(F32) + swapped(pair[1]).astype(F32)).astype(BF16)
            return lax.psum_scatter(both, "row", scatter_dimension=0, tiled=True)

        shares = (reduced(dw_a), reduced(dw_b))
        terms = (ggain_in, gtaps, gheads, ggain)
        return g_in, shares, terms

    g_sum1 = g_out1.astype(F32)
    g_in1, shares1, terms1 = backward(
        1, x1, g_sum1, g_out1, gbranch1, norm1, scale1, normed1, z1, halo1, gate1, made1, ssd1, state1
    )
    g_out0 = g_in1.astype(BF16)
    dots0 = jnp.sum(g_out0.astype(F32) * raw0, axis=1, keepdims=True)
    norm0 = jnp.pad(jnp.concatenate([rho0, dots0], axis=1), ((0, 0), (0, LANE - 2)))
    gbranch0 = branch_grad_of(0, g_out0)
    g_in0, shares0, terms0 = backward(
        0, layer_in, g_out0.astype(F32), g_out0, gbranch0, norm0, scale0, normed0, z0, halo0, gate0, made0, ssd0, state0
    )

    def small_vector(terms):
        ggain_in, gtaps, gheads, ggain = terms
        skip = gtaps[5, :inner].reshape(heads, inner // heads).sum(axis=1)
        own = [ggain_in, gtaps[:4, :inner], gtaps[4, :inner], gheads[0, :heads], gheads[1, :heads], skip, ggain[0]]
        return jnp.concatenate([v.reshape(-1) for v in own]), jnp.concatenate([gtaps[:4, inner:].reshape(-1), gtaps[4, inner:]])

    (own0_vec, part0), (own1_vec, part1) = small_vector(terms0), small_vector(terms1)
    own_sum = lax.psum(jnp.stack([own0_vec, own1_vec]), ("pipe", "row"))
    part_sum = lax.psum(jnp.stack([part0, part1]), ("pipe", "row", "col"))
    own_sum = pick_mine(own_sum[0], own_sum[1])
    part_sum = pick_mine(part_sum[0], part_sum[1])

    def cut(vector, sizes):
        out, at = [], 0
        for size in sizes:
            out.append(vector[at : at + size])
            at += size
        return out

    s_gain, s_cv, s_cvb, s_sb, s_dl, s_sk, s_gg = cut(own_sum, (width, 4 * inner, inner, heads, heads, heads, inner))
    s_cs, s_csb = cut(part_sum, (8 * states, 2 * states))

    def settled(index):
        mine = pick_mine(shares0[index], shares1[index])
        other = swapped(pick_mine(shares1[index], shares0[index]))
        low, high = pick_mine(mine, other).astype(F32), pick_mine(other, mine).astype(F32)
        return low, high

    a_low, a_high = settled(0)
    b_low, b_high = settled(1)
    d_value = jnp.concatenate([a_low[:, :half], a_high[:, :half]], axis=1)
    d_state = jnp.concatenate([a_low[:, half : half + states], a_high[:, half : half + states]], axis=1)
    d_step = a_low[:, half + states : half + states + heads]
    d_gate = jnp.concatenate([b_low[:, :half], b_high[:, :half]], axis=1)
    d_out = jnp.concatenate([b_low[:, half:], b_high[:, half:]], axis=1).T

    mine_out, give_out = pick_mine(x1, x2), pick_mine(x2, x1)
    take_out = swapped(give_out)
    layer_outputs = jnp.stack([pick_mine(mine_out, take_out), pick_mine(take_out, mine_out)])
    mine_grad, give_grad = pick_mine(g_in0, g_in1), pick_mine(g_in1, g_in0)
    take_grad = swapped(give_grad)
    by_batch = (pick_mine(mine_grad, take_grad), pick_mine(take_grad, mine_grad))
    flipped = first & (batch_order[0] == 1)
    input_grads = jnp.stack([jnp.where(flipped, by_batch[1], by_batch[0]), jnp.where(flipped, by_batch[0], by_batch[1])])

    return (
        layer_outputs[None],
        input_grads[None],
        s_gain[None],
        d_gate[None],
        d_value[None],
        d_step[None],
        d_state[None],
        s_cv.reshape(1, 4, inner),
        s_cvb[None],
        s_cs.reshape(1, 4, 2 * states),
        s_csb[None],
        s_sb[None],
        s_dl[None],
        s_sk[None],
        s_gg[None],
        d_out[None],
    )


def solution(mesh):
    in_specs = (
        P(None, "row", None),
        P(None, "row", None),
        P(None, "row"),
        P(),
        P("pipe", None),
        P("pipe", "row", "col"),
        P("pipe", "row", "col"),
        P("pipe", "row", "col"),
        P("pipe", "row", None),
        P("pipe", None, "col"),
        P("pipe", "col"),
        P("pipe", None, None),
        P("pipe", None),
        P("pipe", "col"),
        P("pipe", "col"),
        P("pipe", "col"),
        P("pipe", "col"),
        P("pipe", "col", "row"),
    )
    out_specs = (
        P("pipe", None, "row", None),
        P("pipe", None, "row", None),
        P("pipe", None),
        P("pipe", "row", "col"),
        P("pipe", "row", "col"),
        P("pipe", "row", "col"),
        P("pipe", "row", None),
        P("pipe", None, "col"),
        P("pipe", "col"),
        P("pipe", None, None),
        P("pipe", None),
        P("pipe", "col"),
        P("pipe", "col"),
        P("pipe", "col"),
        P("pipe", "col"),
        P("pipe", "col", "row"),
    )
    return jax.shard_map(local, mesh=mesh, in_specs=in_specs, out_specs=out_specs, check_vma=False)
```

```python
import functools
import math

import jax
import jax.numpy as jnp
from jax import lax
from jax.experimental import pallas as pl
from jax.experimental.pallas import tpu as pltpu
from jax.sharding import PartitionSpec as P

EPSILON = 1e-05
LOG2E = math.log2(math.e)
LANE = 128
F32 = jnp.float32
BF16 = jnp.bfloat16
SMALL_ROWS = 16
LEAD = 16
TAPS_ROWS = 32
SMALL = 48
BLOCKS = 4


def dot_nn(a, b):
    return lax.dot_general(a, b, (((1,), (0,)), ((), ())), preferred_element_type=F32)


def dot_nt(a, b):
    return lax.dot_general(a, b, (((1,), (1,)), ((), ())), preferred_element_type=F32)


def dot_tn(a, b):
    return lax.dot_general(a, b, (((0,), (0,)), ((), ())), preferred_element_type=F32)


def dot_exact(a, b):
    return lax.dot_general(
        a, b, (((1,), (0,)), ((), ())), precision=lax.Precision.HIGHEST, preferred_element_type=F32
    )


def sigmoid(v):
    return 1.0 / (1.0 + jnp.exp(-v))


def split_pair(v):
    high = v.astype(BF16)
    return high, (v - high.astype(F32)).astype(BF16)


def on_chip(kernel, out_shapes, scratch=()):
    whole = pl.BlockSpec(memory_space=pltpu.VMEM)
    scalar = pl.BlockSpec(memory_space=pltpu.SMEM)

    def call(*operands):
        return pl.pallas_call(
            kernel,
            out_shape=out_shapes,
            in_specs=[scalar if o.dtype == jnp.int32 else whole for o in operands],
            out_specs=jax.tree.map(lambda _: whole, out_shapes),
            scratch_shapes=scratch,
            compiler_params=pltpu.CompilerParams(vmem_limit_bytes=60 * 1024 * 1024),
        )(*operands)

    return call


def shaped(shape, dtype=F32):
    return jax.ShapeDtypeStruct(shape, dtype)


def tile_of(q):
    return slice(q * LANE, (q + 1) * LANE)


def spread(columns, q, heads_tile, lane_head):
    first = q * heads_tile
    out = columns[:, first : first + 1]
    for i in range(1, heads_tile):
        out = jnp.where(lane_head == i, columns[:, first + i : first + i + 1], out)
    return out


def lane_heads(rows, heads_tile):
    lanes = lax.broadcasted_iota(jnp.int32, (rows, LANE), 1)
    return lanes // (LANE // heads_tile)


def tri_mask(tokens, seg_col, seg_row, transposed):
    first = lax.broadcasted_iota(jnp.int32, (tokens, tokens), 0)
    second = lax.broadcasted_iota(jnp.int32, (tokens, tokens), 1)
    order = first <= second if transposed else first >= second
    return order & (seg_col == seg_row)


def pack_a_kernel(core_ref, value_ref, state_ref, step_ref, keep_ref, give_ref):
    half = value_ref.shape[1] // 2
    heads = step_ref.shape[1]
    core = core_ref[0]
    for ref, place in ((keep_ref, core), (give_ref, 1 - core)):
        ref[:, :half] = value_ref[:, pl.ds(pl.multiple_of(place * half, LANE), half)]
        ref[:, half : half + LANE] = state_ref[:, pl.ds(pl.multiple_of(place * LANE, LANE), LANE)]
        ref[:, half + LANE :] = jnp.zeros((ref.shape[0], LANE), BF16)
        ref[:, half + LANE : half + LANE + heads] = step_ref[...]


def pack_b_kernel(core_ref, gate_ref, out_ref, keep_ref, give_ref):
    half = gate_ref.shape[1] // 2
    core = core_ref[0]
    for ref, place in ((keep_ref, core), (give_ref, 1 - core)):
        ref[:, :half] = gate_ref[:, pl.ds(pl.multiple_of(place * half, LANE), half)]
        ref[:, half:] = out_ref[pl.ds(pl.multiple_of(place * half, LANE), half), :].astype(F32).T.astype(BF16)


def enter_kernel(
    inner, heads_tile, places, core_ref, x_ref, before_ref, small_ref, aux_ref, *refs,
):
    taps_ref, heads_ref, gain_ref, _ = views(small_ref, places)
    mine, other = refs[:BLOCKS], refs[BLOCKS : 2 * BLOCKS]
    (
        normed_ref, scale_ref, z_ref, conv_ref, value_ref, scaled_ref, bc_ref, step_ref, cum_ref, cumt_ref, lead_ref,
        carry_ref, msg_ref, leadu_ref,
    ) = refs[2 * BLOCKS :]
    tokens, width = x_ref.shape
    half = inner // 2
    conv_width = conv_ref.shape[1]
    for ref, at in ((before_ref, slice(0, LEAD)), (x_ref, slice(LEAD, LEAD + tokens))):
        x = ref[...].astype(F32)
        scale = lax.rsqrt(jnp.mean(x * x, axis=1, keepdims=True) + EPSILON)
        normed_ref[at, :] = (x * scale * gain_ref[0:1, :]).astype(BF16)
    scale_ref[...] = jnp.broadcast_to(scale, scale_ref.shape)
    core = core_ref[0]
    block = width // BLOCKS
    for pieces, place in ((mine, core), (other, 1 - core)):
        z = None
        for i in range(BLOCKS):
            term = dot_nn(normed_ref[:, i * block : (i + 1) * block], pieces[i][...])
            z = term if z is None else z + term
        z_ref[:, pl.ds(pl.multiple_of(place * half, LANE), half)] = z[:, :half]
        z_ref[:, pl.ds(pl.multiple_of(inner + place * LANE, LANE), LANE)] = z[:, half : half + LANE]
        if pieces is mine:
            z_ref[:, conv_width:] = z[:, half + LANE :]
    aux = aux_ref[...]
    raw = z_ref[LEAD:, conv_width:] + heads_ref[0:1, :]
    step = jnp.maximum(raw, 0.0) + jnp.log1p(jnp.exp(-jnp.abs(raw)))
    rates = -step * jnp.exp(heads_ref[1:2, :])
    rows = lax.broadcasted_iota(jnp.int32, (tokens, tokens), 0)
    cols = lax.broadcasted_iota(jnp.int32, (tokens, tokens), 1)
    cum = dot_exact((rows >= cols).astype(F32), rates) * LOG2E
    lead = aux[:, 5:6] * jnp.exp2(cum[tokens - 1 : tokens, :] - cum)
    carry = aux[:, 4:5] * jnp.exp2(cum)
    step_ref[...] = step
    cum_ref[...] = cum
    cumt_ref[...] = cum.T
    lead_ref[...] = lead
    carry_ref[...] = carry
    lane_head = lane_heads(tokens, heads_tile)
    for q in range(conv_width // LANE):
        at = tile_of(q)
        acc = taps_ref[4:5, at] + taps_ref[3:4, at] * z_ref[LEAD:, at]
        for j in range(3):
            shifted = z_ref[LEAD - 3 + j : LEAD - 3 + j + tokens, at]
            acc = acc + taps_ref[j : j + 1, at] * (aux[:, j : j + 1] * shifted)
        conv_ref[:, at] = acc
        value = acc * sigmoid(acc)
        if q < inner // LANE:
            value_ref[:, at] = value
            scaled = spread(step, q, heads_tile, lane_head) * value
            scaled_ref[:, at] = scaled.astype(BF16)
            leadu_ref[:, at] = (spread(lead, q, heads_tile, lane_head) * scaled).astype(BF16)
        else:
            bc_ref[:, tile_of(q - inner // LANE)] = value.astype(BF16)
    msg_ref[0:LANE, :] = dot_tn(bc_ref[:, :LANE], leadu_ref[...]).astype(BF16)
    put_through(msg_ref, carry[tokens - 1 : tokens, :], inner, heads_tile)


def enter_first_kernel(
    inner, heads_tile, places, core_ref, x_ref, before_ref, small_ref, seg_ref, seg_before_ref, *refs,
):
    weights, refs = refs[: 2 * BLOCKS], refs[2 * BLOCKS :]
    aux_ref, segt_ref, *made, seg_ext_ref, leadu_ref = refs
    tokens = x_ref.shape[0]
    seg = seg_ref[...]
    seg_ext_ref[0:LEAD, :] = seg_before_ref[...]
    seg_ext_ref[LEAD:, :] = seg
    lanes = lax.broadcasted_iota(jnp.int32, (tokens, LANE), 1)
    flags = jnp.where(lanes == 3, seg, 0.0)
    for j in range(3):
        same = (seg_ext_ref[LEAD - 3 + j : LEAD - 3 + j + tokens, :] == seg).astype(F32)
        flags = jnp.where(lanes == j, same, flags)
    flags = jnp.where(lanes == 4, (seg == seg_ext_ref[LEAD - 1 : LEAD, :]).astype(F32), flags)
    flags = jnp.where(lanes == 5, (seg == seg[tokens - 1 :, :]).astype(F32), flags)
    aux_ref[...] = flags
    segt_ref[...] = seg.T[0:8, :]
    enter_kernel(
        inner, heads_tile, places, core_ref, x_ref, before_ref, small_ref, aux_ref, *weights, *made, leadu_ref
    )


def views(ref, places):
    return tuple(ref.at[:, p] for p in places)


def put_through(msg_ref, last, inner, heads_tile):
    msg_ref[LANE:, :] = jnp.zeros((SMALL_ROWS, inner), BF16)
    lane_row = lane_heads(1, heads_tile)
    for q in range(inner // LANE):
        high, low = split_pair(spread(last, q, heads_tile, lane_row))
        msg_ref[LANE : LANE + 1, tile_of(q)] = high
        msg_ref[LANE + 1 : LANE + 2, tile_of(q)] = low


def wide_kernel(offset, lead, core_ref, a_ref, *refs):
    mine, other = refs[:BLOCKS], refs[BLOCKS : 2 * BLOCKS]
    out_ref = refs[2 * BLOCKS]
    core = core_ref[0]
    half = out_ref.shape[1] // 2
    block = a_ref.shape[1] // BLOCKS
    for pieces, place in ((mine, core), (other, 1 - core)):
        total = None
        for i in range(BLOCKS):
            term = dot_nn(a_ref[lead:, i * block : (i + 1) * block], pieces[i][:, offset : offset + half])
            total = term if total is None else total + term
        out_ref[:, pl.ds(pl.multiple_of(place * half, LANE), half)] = total


def intra_kernel(
    inner, heads_tile, places, scaled_ref, value_ref, bc_ref, cum_ref, cumt_ref, aux_ref, segt_ref, small_ref,
    out_ref,
):
    heads_ref = views(small_ref, places)[1]
    tokens = scaled_ref.shape[0]
    scores = dot_nt(bc_ref[:, LANE:], bc_ref[:, :LANE])
    scores = jnp.where(tri_mask(tokens, aux_ref[:, 3:4], segt_ref[0:1, :], False), scores, 0.0)
    lane_head = lane_heads(tokens, heads_tile)
    lane_row = lane_heads(1, heads_tile)
    for q in range(inner // LANE):
        at = tile_of(q)
        total = spread(heads_ref[2:3, :], q, heads_tile, lane_row) * value_ref[:, at]
        scaled = scaled_ref[:, at]
        for i in range(heads_tile):
            h = q * heads_tile + i
            gap = jnp.minimum(cum_ref[:, h : h + 1] - cumt_ref[h : h + 1, :], 0.0)
            mixed = (jnp.exp2(gap) * scores).astype(BF16)
            total = total + jnp.where(lane_head == i, dot_nn(mixed, scaled), 0.0)
        out_ref[:, at] = total


def enter_states(messages):
    state = None
    for message in reversed(messages):
        own = message[0:LANE, :].astype(F32)
        through = message[LANE : LANE + 1, :].astype(F32) + message[LANE + 1 : LANE + 2, :].astype(F32)
        state = own if state is None else own + through * state
    return state


def gate_kernel(
    inner, heads_tile, places, count, with_grad, core_ref, intra_ref, bc_ref, carry_ref, gate_ref, small_ref, *refs
):
    gain_ref = views(small_ref, places)[3]
    messages = refs[:count]
    mine, other = refs[count : count + BLOCKS], refs[count + BLOCKS : count + 2 * BLOCKS]
    refs = refs[count + 2 * BLOCKS :]
    if with_grad:
        branch_grad_ref, refs = refs[0], refs[1:]
        ssd_ref, state_ref, msg_ref, sums_ref, gated_ref = refs
    else:
        ssd_ref, state_ref, msg_ref, gated_ref = refs
    tokens = intra_ref.shape[0]
    state = enter_states([m[...] for m in messages]).astype(BF16)
    state_ref[...] = state
    inter = dot_nn(bc_ref[:, LANE:], state)
    lane_head = lane_heads(tokens, heads_tile)
    carry = carry_ref[...]
    squares = jnp.zeros((tokens, LANE), F32)
    products = jnp.zeros((tokens, LANE), F32)
    for q in range(inner // LANE):
        at = tile_of(q)
        ssd = intra_ref[:, at] + spread(carry, q, heads_tile, lane_head) * inter[:, at]
        ssd_ref[:, at] = ssd
        gate = gate_ref[:, at]
        gated = ssd * (gate * sigmoid(gate))
        squares = squares + gated * gated
        scaled = gated * gain_ref[0:1, at]
        gated_ref[:, at] = scaled.astype(BF16)
        if with_grad:
            products = products + scaled * branch_grad_ref[:, at]
    half = inner // 2
    core = core_ref[0]
    low = gated_ref[:, pl.ds(pl.multiple_of(core * half, LANE), half)]
    high = gated_ref[:, pl.ds(pl.multiple_of((1 - core) * half, LANE), half)]
    block = mine[0].shape[0]
    for i in range(BLOCKS):
        part = dot_nt(low, mine[i][:, half:]) + dot_nt(high, other[i][:, half:])
        msg_ref[:, i * block : (i + 1) * block] = part.astype(BF16)
    total = jnp.sum(squares, axis=1, keepdims=True)
    lanes = lax.broadcasted_iota(jnp.int32, (tokens, LANE), 1)
    if with_grad:
        packed = jnp.where(lanes == 0, total, 0.0)
        packed = packed + jnp.where(lanes == 1, jnp.sum(products, axis=1, keepdims=True), 0.0)
        sums_ref[...] = packed.T[0:8, :]
    else:
        rest = total - total.astype(BF16).astype(F32)
        packed = jnp.where(lanes == 0, total, jnp.where(lanes == 1, rest, 0.0))
        msg_ref[:, BLOCKS * block :] = packed.astype(BF16)


def ungate_kernel(
    inner, heads_tile, places, norm_width, branch_grad_ref, norm_ref, gate_ref, ssd_ref, small_ref, carry_ref, bc_ref,
    gssd_ref, ggate_ref, branch_ref, msg_ref, ggain_ref, cg_ref,
):
    gain_ref = views(small_ref, places)[3]
    tokens = branch_grad_ref.shape[0]
    rho = norm_ref[:, 0:1]
    pull = norm_ref[:, 1:2] * (rho * rho * rho / norm_width)
    lane_head = lane_heads(tokens, heads_tile)
    carry = carry_ref[...]
    ggain_ref[...] = jnp.zeros(ggain_ref.shape, F32)
    for q in range(inner // LANE):
        at = tile_of(q)
        gate = gate_ref[:, at]
        sig = sigmoid(gate)
        ssd = ssd_ref[:, at]
        gated = ssd * (gate * sig)
        grad = branch_grad_ref[:, at]
        gain = gain_ref[0:1, at]
        normed = gated * rho
        ggain_ref[0:1, at] = jnp.sum(grad * normed, axis=0, keepdims=True)
        branch_ref[:, at] = (normed * gain).astype(BF16)
        ggated = rho * (gain * grad) - gated * pull
        gssd = ggated * (gate * sig)
        gssd_ref[:, at] = gssd
        ggate_ref[:, at] = (ggated * ssd * (sig * (1.0 + gate * (1.0 - sig)))).astype(BF16)
        cg_ref[:, at] = (spread(carry, q, heads_tile, lane_head) * gssd).astype(BF16)
    msg_ref[0:LANE, :] = dot_tn(bc_ref[:, LANE:], cg_ref[...]).astype(BF16)
    put_through(msg_ref, carry[tokens - 1 : tokens, :], inner, heads_tile)


def intra_grad_kernel(
    inner, heads_tile, scaled_ref, gssd_ref, bc_ref, cum_ref, cumt_ref, aux_ref, segt_ref,
    gscaled_ref, gbc_ref, gcum_ref, sums_ref,
):
    tokens = scaled_ref.shape[0]
    mask = tri_mask(tokens, aux_ref[:, 3:4], segt_ref[0:1, :], True)
    scores = jnp.where(mask, dot_nt(bc_ref[:, :LANE], bc_ref[:, LANE:]), 0.0)
    lane_head = lane_heads(tokens, heads_tile)
    gscores = jnp.zeros((tokens, tokens), F32)
    gcum_ref[...] = jnp.zeros(gcum_ref.shape, F32)
    sums_ref[...] = jnp.zeros(sums_ref.shape, F32)
    for q in range(inner // LANE):
        at = tile_of(q)
        grad = gssd_ref[:, at].astype(BF16)
        scaled = scaled_ref[:, at]
        total = jnp.zeros((tokens, LANE), F32)
        for i in range(heads_tile):
            h = q * heads_tile + i
            gap = jnp.minimum(cumt_ref[h : h + 1, :] - cum_ref[:, h : h + 1], 0.0)
            decay = jnp.exp2(gap)
            mixed = decay * scores
            picked = jnp.where(lane_head == i, scaled, jnp.zeros_like(scaled))
            gmixed = dot_nt(picked, grad)
            total = total + jnp.where(lane_head == i, dot_nn(mixed.astype(BF16), grad), 0.0)
            product = gmixed * mixed
            sums_ref[h : h + 1, :] = jnp.sum(product, axis=0, keepdims=True)
            gcum_ref[:, h : h + 1] = -jnp.sum(product, axis=1, keepdims=True)
            gscores = gscores + gmixed * decay
        gscaled_ref[:, at] = total
    gscores = jnp.where(mask, gscores, 0.0)
    gbc_ref[:, :LANE] = dot_nn(gscores.astype(BF16), bc_ref[:, LANE:])
    gbc_ref[:, LANE:] = dot_nn(gscores.T.astype(BF16), bc_ref[:, :LANE])
    gcum_ref[...] = gcum_ref[...] + sums_ref[...].T


def inter_grad_kernel(
    inner, heads_tile, places, count, state_ref, scaled_ref, value_ref, gssd_ref, gscaled_ref, bc_ref, gbc_ref, gcum_ref,
    step_ref, lead_ref, carry_ref, z_ref, conv_ref, aux_ref, small_ref, ggain_ref, *refs,
):
    taps_ref, heads_ref, _, _ = views(small_ref, places)
    messages = refs[:count]
    gpre_ref, gstep_ref, gtaps_ref, em_ref, leadu_ref, cg_ref, gain_ref, lose_ref, gsize_ref = refs[count:]
    tokens = scaled_ref.shape[0]
    width = conv_ref.shape[1]
    aux = aux_ref[...]
    adjoint = enter_states([m[...] for m in messages])
    adjoint_low = adjoint.astype(BF16)
    state = state_ref[...]
    from_adjoint = dot_nn(bc_ref[:, :LANE], adjoint_low)
    from_state = dot_nn(bc_ref[:, LANE:], state)
    overlap = jnp.sum(adjoint * state.astype(F32), axis=0, keepdims=True)
    lane_head = lane_heads(tokens, heads_tile)
    lane_row = lane_heads(1, heads_tile)
    step = step_ref[...]
    lead = lead_ref[...]
    carry = carry_ref[...]
    em_ref[0:8, :] = jnp.zeros((8, LANE), F32)
    em_ref[8 + tokens :, :] = jnp.zeros((8, LANE), F32)
    gpre_ref[0:8, :] = jnp.zeros((8, width), F32)
    gtaps_ref[...] = jnp.zeros(gtaps_ref.shape, F32)

    def through_conv(q, grad):
        at = tile_of(q)
        conv = conv_ref[:, at]
        sig = sigmoid(conv)
        e = grad * (sig * (1.0 + conv * (1.0 - sig)))
        gtaps_ref[4:5, at] = jnp.sum(e, axis=0, keepdims=True)
        gtaps_ref[3:4, at] = jnp.sum(e * z_ref[LEAD:, at], axis=0, keepdims=True)
        total = None
        for j in range(3):
            masked = aux[:, j : j + 1] * e
            shifted = z_ref[LEAD - 3 + j : LEAD - 3 + j + tokens, at]
            gtaps_ref[j : j + 1, at] = jnp.sum(masked * shifted, axis=0, keepdims=True)
            em_ref[8 : 8 + tokens, :] = masked
            term = taps_ref[j : j + 1, at] * em_ref[3 - j : 11 - j + tokens, :]
            total = term if total is None else total + term
        gpre_ref[8:LEAD, at] = total[0:8, :]
        gpre_ref[LEAD:, at] = total[8:, :] + taps_ref[3:4, at] * e

    for q in range(inner // LANE):
        at = tile_of(q)
        scaled = scaled_ref[:, at].astype(F32)
        grad = gssd_ref[:, at]
        value = value_ref[:, at]
        leads = spread(lead, q, heads_tile, lane_head)
        carries = spread(carry, q, heads_tile, lane_head)
        pushed = leads * from_adjoint[:, at]
        gscaled = gscaled_ref[:, at] + pushed
        carried = carries * grad
        leadu_ref[:, at] = (leads * scaled).astype(BF16)
        cg_ref[:, at] = carried.astype(BF16)
        gain_ref[:, at] = (carried * from_state[:, at]).astype(BF16)
        lose_ref[:, at] = (scaled * pushed).astype(BF16)
        gsize_ref[:, at] = (gscaled * value).astype(BF16)
        gtaps_ref[5:6, at] = jnp.sum(grad * value, axis=0, keepdims=True)
        gvalue = spread(step, q, heads_tile, lane_head) * gscaled
        gvalue = gvalue + spread(heads_ref[2:3, :], q, heads_tile, lane_row) * grad
        through_conv(q, gvalue)
    gb = gbc_ref[:, :LANE] + dot_nt(leadu_ref[...], adjoint_low)
    gc = gbc_ref[:, LANE:] + dot_nt(cg_ref[...], state)
    through_conv(inner // LANE, gb)
    through_conv(inner // LANE + 1, gc)
    head_of = lax.broadcasted_iota(jnp.int32, (inner, LANE), 0) // (LANE // heads_tile)
    pick = (head_of == lax.broadcasted_iota(jnp.int32, (inner, LANE), 1)).astype(BF16)
    lose = dot_nn(lose_ref[...], pick)
    gcum = gcum_ref[...] + dot_nn(gain_ref[...], pick) - lose
    high, low = split_pair(overlap)
    ends = dot_nn(jnp.broadcast_to(high, (8, inner)), pick) + dot_nn(jnp.broadcast_to(low, (8, inner)), pick)
    last = carry[tokens - 1 : tokens, :] * ends[0:1, :] + jnp.sum(lose, axis=0, keepdims=True)
    row_of = lax.broadcasted_iota(jnp.int32, (tokens, LANE), 0)
    gcum = gcum + jnp.where(row_of == tokens - 1, last, 0.0)
    rows = lax.broadcasted_iota(jnp.int32, (tokens, tokens), 0)
    cols = lax.broadcasted_iota(jnp.int32, (tokens, tokens), 1)
    grate = dot_exact((rows <= cols).astype(F32), gcum)
    speed = jnp.exp(heads_ref[1:2, :])
    gsize = dot_nn(gsize_ref[...], pick) - speed * grate
    raw = z_ref[LEAD:, width:] + heads_ref[0:1, :]
    graw = gsize * sigmoid(raw)
    gstep_ref[...] = graw.astype(BF16)
    gtaps_ref[6:7, :inner] = ggain_ref[0:1, :]
    gtaps_ref[7:8, 0:LANE] = jnp.sum(graw, axis=0, keepdims=True)
    gtaps_ref[7:8, LANE : 2 * LANE] = jnp.sum(grate * (-speed * step), axis=0, keepdims=True)


def give_b_kernel(
    core_ref, ggate_ref, normed_ref, g_out_ref, branch_ref,
    other_b_ref, gg_mine_ref, gg_other_ref, normed_t_ref, g_out_t_ref,
):
    width = g_out_ref.shape[1]
    half = ggate_ref.shape[1] // 2
    core = core_ref[0]
    gg_mine_ref[...] = ggate_ref[:, pl.ds(pl.multiple_of(core * half, LANE), half)]
    gg_other_ref[...] = ggate_ref[:, pl.ds(pl.multiple_of((1 - core) * half, LANE), half)]
    block = width // BLOCKS
    for i in range(BLOCKS):
        at = slice(i * block, (i + 1) * block)
        normed_t_ref[at, :] = normed_ref[LEAD:, at].astype(F32).T.astype(BF16)
        g_out_t_ref[at, :] = g_out_ref[:, at].astype(F32).T.astype(BF16)
    other_b_ref[:, :half] = dot_nn(normed_t_ref[...], gg_other_ref[...]).astype(BF16)
    branch = branch_ref[:, pl.ds(pl.multiple_of((1 - core) * half, LANE), half)]
    other_b_ref[:, half:] = dot_nn(g_out_t_ref[...], branch).astype(BF16)


def keep_b_kernel(core_ref, normed_t_ref, g_out_t_ref, branch_ref, gg_mine_ref, their_ref, *refs):
    size = normed_t_ref.shape[0] // len(refs)
    half = gg_mine_ref.shape[1]
    branch = branch_ref[:, pl.ds(pl.multiple_of(core_ref[0] * half, LANE), half)]
    for i, ref in enumerate(refs):
        at = slice(i * size, (i + 1) * size)
        part = dot_nn(normed_t_ref[at, :], gg_mine_ref[...]) + their_ref[at, :half].astype(F32)
        ref[:, :half] = part.astype(BF16)
        part = dot_nn(g_out_t_ref[at, :], branch) + their_ref[at, half:].astype(F32)
        ref[:, half:] = part.astype(BF16)


def taps_rows(taps, wide):
    left, right = taps[:, :wide], taps[:, wide:]
    right = jnp.concatenate([right, jnp.zeros((8, 2 * wide - taps.shape[1]), F32)], axis=1)
    rows = []
    for part in (left, right):
        high = part.astype(BF16).astype(F32)
        rows += [high, part - high]
    return jnp.concatenate(rows, axis=0).astype(BF16)


def gain_rows(gain, wide):
    high = gain.astype(BF16).astype(F32)
    index = lax.broadcasted_iota(jnp.int32, (16, wide), 0)
    out = jnp.zeros((16, wide), F32)
    count = -(-gain.shape[1] // wide)
    for i in range(count):
        for base, part in ((0, high), (8, gain - high)):
            piece = part[:, i * wide : (i + 1) * wide]
            if piece.shape[1] < wide:
                piece = jnp.concatenate([piece, jnp.zeros((1, wide - piece.shape[1]), F32)], axis=1)
            out = jnp.where(index == base + i, piece, out)
    return out.astype(BF16)


def give_a_kernel(
    core_ref, gpre_ref, next_ref, gstep_ref, normed_t_ref, gtaps_ref, other_a_ref, ga_mine_ref, ga_other_ref, glow_ref
):
    tokens, width = glow_ref.shape
    inner = width - 2 * LANE
    half = inner // 2
    core = core_ref[0]
    cut = tokens - LEAD
    glow_ref[:cut, :] = gpre_ref[LEAD : LEAD + cut, :].astype(BF16)
    glow_ref[cut:, :] = (gpre_ref[LEAD + cut :, :] + next_ref[...]).astype(BF16)
    for ga_ref, place in ((ga_mine_ref, core), (ga_other_ref, 1 - core)):
        ga_ref[:, :half] = glow_ref[:, pl.ds(pl.multiple_of(place * half, LANE), half)]
        ga_ref[:, half : half + LANE] = glow_ref[:, pl.ds(pl.multiple_of(inner + place * LANE, LANE), LANE)]
        ga_ref[:, half + LANE :] = gstep_ref[...]
    rows = normed_t_ref.shape[0]
    other_a_ref[:rows, :] = dot_nn(normed_t_ref[...], ga_other_ref[...]).astype(BF16)
    other_a_ref[rows:, :] = taps_rows(gtaps_ref[...], other_a_ref.shape[1])


def keep_a_kernel(normed_t_ref, ga_mine_ref, their_ref, gtaps_ref, ggain_ref, *refs):
    rows = normed_t_ref.shape[0]
    size = rows // len(refs)
    wide = ga_mine_ref.shape[1]
    theirs = [their_ref[rows + 16 * i : rows + 16 * (i + 1), :].astype(F32) for i in range(2)]
    taps = jnp.concatenate([t[0:8] + t[8:16] for t in theirs], axis=1)[:, : gtaps_ref.shape[1]] + gtaps_ref[...]
    small = taps_rows(taps, wide)
    gain = gain_rows(ggain_ref[0:1, :], wide)
    for i, ref in enumerate(refs):
        at = slice(i * size, (i + 1) * size)
        ref[:size, :] = (dot_nn(normed_t_ref[at, :], ga_mine_ref[...]) + their_ref[at, :].astype(F32)).astype(BF16)
        ref[size : size + TAPS_ROWS, :] = small
        ref[size + TAPS_ROWS :, :] = gain


def pull_kernel(ga_mine_ref, ga_other_ref, gg_mine_ref, gg_other_ref, x_ref, scale_ref, *refs):
    mine_a, other_a, mine_b, other_b = (refs[i * BLOCKS : (i + 1) * BLOCKS] for i in range(4))
    msg_ref, ggain_ref = refs[4 * BLOCKS :]
    half = gg_mine_ref.shape[1]
    block = mine_a[0].shape[0]
    scale = scale_ref[:, 0:1]
    ggain_ref[...] = jnp.zeros(ggain_ref.shape, F32)
    for i in range(BLOCKS):
        at = slice(i * block, (i + 1) * block)
        part = dot_nt(ga_mine_ref[...], mine_a[i][...])
        part = part + dot_nt(ga_other_ref[:, : half + LANE], other_a[i][:, : half + LANE])
        part = part + dot_nt(gg_mine_ref[...], mine_b[i][:, :half])
        part = part + dot_nt(gg_other_ref[...], other_b[i][:, :half])
        msg_ref[:, at] = part.astype(BF16)
        ggain_ref[0:1, at] = jnp.sum(part * (x_ref[:, at].astype(F32) * scale), axis=0, keepdims=True)


def leave_kernel(norm_width, places, below, ordered, row_ref, full_ref, x_ref, scale_ref, small_ref, g_out_ref, *refs):
    gain_ref = views(small_ref, places)[2]
    if below:
        raw_ref, grad_ref, low_ref, norm_ref = refs
    else:
        (grad_ref,) = refs
    tokens, width = x_ref.shape
    scale = scale_ref[:, 0:1]
    x = x_ref[...].astype(F32)
    pulled = full_ref[...].astype(F32) * gain_ref[0:1, :]
    slope = jnp.sum(pulled * x, axis=1, keepdims=True) * (scale * scale * scale / width)
    grad = g_out_ref[...].astype(F32) + scale * pulled - x * slope
    if ordered:
        block = width // BLOCKS
        for i in range(BLOCKS):
            start = pl.multiple_of((row_ref[0] ^ i) * block, LANE)
            grad_ref[:, pl.ds(start, block)] = grad[:, i * block : (i + 1) * block]
    else:
        grad_ref[...] = grad
    if below:
        low = grad.astype(BF16)
        low_ref[...] = low
        dots = jnp.sum(low.astype(F32) * raw_ref[:, :width].astype(F32), axis=1, keepdims=True)
        squares = raw_ref[:, width : width + 1].astype(F32) + raw_ref[:, width + 1 : width + 2].astype(F32)
        lanes = lax.broadcasted_iota(jnp.int32, (tokens, LANE), 1)
        norm_ref[...] = jnp.where(lanes == 0, lax.rsqrt(squares / norm_width + EPSILON), dots)


def permute(block, axis, route):
    return lax.ppermute(block, axis, route)


def from_before(block, count, distance):
    return permute(block, "row", [(i, i + distance) for i in range(count - distance)])


def from_after(block, count, distance):
    return permute(block, "row", [(i + distance, i) for i in range(count - distance)])


def swapped(block):
    return permute(block, "pipe", [(0, 1), (1, 0)])


def exchanged(blocks, axis):
    return lax.all_to_all(blocks, axis, 0, 0)


def spread_out(block, axis):
    count = lax.axis_size(axis)
    return exchanged(jnp.broadcast_to(block[None], (count,) + block.shape), axis).reshape(
        (count * block.shape[0],) + block.shape[1:]
    )


def parts_sum(block, axis):
    count = lax.axis_size(axis)
    parts = exchanged(block.reshape((count, block.shape[0] // count) + block.shape[1:]), axis)
    return jnp.sum(parts.astype(F32), axis=0)


def direct_sum(block, axis):
    parts = [block] + [sent_to(block, axis, b) for b in range(1, lax.axis_size(axis))]
    parts = [p.astype(F32) for p in parts]
    while len(parts) > 1:
        parts = [parts[i] + parts[i + 1] for i in range(0, len(parts), 2)]
    return parts[0]


def sent_to(block, axis, flip):
    count = lax.axis_size(axis)
    return permute(block, axis, [(i, i ^ flip) for i in range(count)])


def relative_order(block, dim, axis, place=None):
    count = lax.axis_size(axis)
    size = block.shape[dim] // count
    place = lax.axis_index(axis) if place is None else place
    return jnp.concatenate(
        [lax.dynamic_slice_in_dim(block, (place ^ b) * size, size, dim) for b in range(count)], axis=dim
    )


class Phases:
    def __init__(self, token):
        self.token = token

    def hold(self, value):
        return lax.optimization_barrier((value, self.token))[0]

    def close(self, *values):
        self.token = lax.optimization_barrier((self.token,) + tuple(jax.tree.leaves(values)))[0]


def after(block, *others):
    return lax.optimization_barrier((block,) + others)[0]


def local(
    inputs, cotangent, segment_ids, batch_order, norm_gain, gate_proj, value_proj, step_proj, state_proj,
    conv_value, conv_value_bias, conv_state, conv_state_bias, step_bias, decay_log, skip_gain, gate_gain, out_proj,
):
    core = lax.axis_index("pipe")
    first = core == 0
    core_id = core.reshape(1).astype(jnp.int32)
    rows = lax.axis_size("row")
    row = lax.axis_index("row")
    tokens, width = inputs.shape[1], inputs.shape[2]
    inner = gate_proj.shape[2]
    heads = step_proj.shape[2]
    states = state_proj.shape[2] // 2
    heads_tile = LANE // (inner // heads)
    half = inner // 2
    conv_width = inner + 2 * states
    norm_width = inner * lax.axis_size("col")
    reach = max(rows // 2, 1)
    distances = range(1, reach + 1)
    group = rows // BLOCKS

    def pick_mine(a, b):
        return jnp.where(first, a, b)

    phases = Phases(core_id)
    hold, close = phases.hold, phases.close

    shard = gate_proj.shape[1]
    a_width, b_width = half + states + LANE, inner
    own_a, away_a = on_chip(pack_a_kernel, (shaped((shard, a_width), BF16),) * 2)(
        core_id, value_proj[0], state_proj[0], step_proj[0]
    )
    close(away_a)
    take_a = swapped(hold(away_a))
    own_b, away_b = on_chip(pack_b_kernel, (shaped((shard, b_width), BF16),) * 2)(core_id, hold(gate_proj[0]), out_proj[0])
    close(take_a, away_b)

    def blocks_of(pieces):
        return [jnp.concatenate(pieces[i * group : (i + 1) * group], axis=0) for i in range(BLOCKS)]

    def both_cores(mine):
        return mine, [swapped(p) for p in mine]

    piece_a0 = hold(pick_mine(own_a, take_a))
    pieces_a0 = [piece_a0] + [sent_to(piece_a0, "row", b) for b in range(1, rows)]
    take_b = swapped(hold(away_b))
    piece_b0 = pick_mine(own_b, take_b)

    taps_own = jnp.concatenate(
        [
            jnp.concatenate([hold(conv_value[0]), conv_state[0]], axis=1),
            jnp.concatenate([conv_value_bias, conv_state_bias], axis=1),
            jnp.zeros((3, conv_width), F32),
        ],
        axis=0,
    )
    heads_own = jnp.pad(jnp.concatenate([hold(step_bias), decay_log, skip_gain], axis=0), ((0, 5), (0, LANE - heads)))
    gains_own = jnp.concatenate([relative_order(hold(norm_gain), 1, "row"), gate_gain], axis=1)
    gains_own = jnp.pad(gains_own, ((0, 7), (0, 0)))
    small = jnp.concatenate([taps_own, heads_own, gains_own], axis=1)
    small_other = swapped(small)
    params = (pick_mine(small, small_other), pick_mine(small_other, small))
    places = (slice(0, conv_width), slice(conv_width, conv_width + LANE))
    places += (slice(conv_width + LANE, conv_width + LANE + width), slice(conv_width + LANE + width, small.shape[1]))

    source = hold(batch_order)[core]
    layer_in = relative_order(inputs[source], 1, "row")
    seg = jnp.broadcast_to(segment_ids[source].astype(F32)[:, None], (tokens, LANE))
    sent_rows = jnp.concatenate([layer_in[tokens - LEAD :], seg[tokens - LEAD :].astype(BF16)], axis=1)
    got_rows = from_before(sent_rows, rows, 1)
    other_order = row ^ jnp.maximum(row - 1, 0)
    before0 = relative_order(got_rows[:, :width], 1, "row", other_order)
    seg_before = jnp.where(row == 0, -1.0, got_rows[:, width:].astype(F32))
    g_out1 = relative_order(hold(cotangent)[core], 1, "row")
    close(pieces_a0, piece_b0, params, layer_in, seg, before0, seg_before, g_out1)

    long = tokens + LEAD
    message_shape = shaped((states + SMALL_ROWS, inner), BF16)
    entered = (
        shaped((long, width), BF16), shaped((tokens, LANE)), shaped((long, conv_width + LANE)),
        shaped((tokens, conv_width)), shaped((tokens, inner)), shaped((tokens, inner), BF16),
        shaped((tokens, 2 * states), BF16), shaped((tokens, LANE)), shaped((tokens, LANE)), shaped((LANE, tokens)),
        shaped((tokens, LANE)), shaped((tokens, LANE)), message_shape,
    )
    enter = [
        on_chip(
            functools.partial(enter_first_kernel, inner, heads_tile, places),
            (shaped((tokens, LANE)), shaped((8, tokens))) + entered,
            [pltpu.VMEM((long, LANE), F32), pltpu.VMEM((tokens, inner), BF16)],
        ),
        on_chip(
            functools.partial(enter_kernel, inner, heads_tile, places), entered, [pltpu.VMEM((tokens, inner), BF16)]
        ),
    ]
    intra = on_chip(functools.partial(intra_kernel, inner, heads_tile, places), shaped((tokens, inner)))
    gate_product = on_chip(functools.partial(wide_kernel, 0, LEAD), shaped((tokens, inner)))
    branch_product = on_chip(functools.partial(wide_kernel, half, 0), shaped((tokens, inner)))
    gates = [
        on_chip(
            functools.partial(gate_kernel, inner, heads_tile, places, reach, with_grad),
            (shaped((tokens, inner)), shaped((states, inner), BF16))
            + ((shaped((tokens, width), BF16), shaped((8, tokens))) if with_grad else (shaped((tokens, width + LANE), BF16),)),
            [pltpu.VMEM((tokens, inner), BF16)],
        )
        for with_grad in (False, True)
    ]
    ungate = on_chip(
        functools.partial(ungate_kernel, inner, heads_tile, places, norm_width),
        (
            shaped((tokens, inner)), shaped((tokens, inner), BF16), shaped((tokens, inner), BF16), message_shape,
            shaped((8, inner)),
        ),
        [pltpu.VMEM((tokens, inner), BF16)],
    )
    intra_grad = on_chip(
        functools.partial(intra_grad_kernel, inner, heads_tile),
        (shaped((tokens, inner)), shaped((tokens, 2 * states)), shaped((tokens, LANE))),
        [pltpu.VMEM((LANE, tokens), F32)],
    )
    inter_grad = on_chip(
        functools.partial(inter_grad_kernel, inner, heads_tile, places, reach),
        (shaped((long, conv_width)), shaped((tokens, LANE), BF16), shaped((8, conv_width))),
        [pltpu.VMEM((tokens + 16, LANE), F32)] + [pltpu.VMEM((tokens, inner), BF16)] * 5,
    )
    pull = on_chip(pull_kernel, (shaped((tokens, width), BF16), shaped((8, width))))
    weight_t = shaped((width, tokens), BF16)
    give_a = on_chip(
        give_a_kernel,
        (shaped((width + TAPS_ROWS, a_width), BF16),) + (shaped((tokens, a_width), BF16),) * 2,
        [pltpu.VMEM((tokens, conv_width), BF16)],
    )
    give_b = on_chip(
        give_b_kernel,
        (shaped((width, b_width), BF16), shaped((tokens, half), BF16), shaped((tokens, half), BF16), weight_t, weight_t),
    )
    keep_a = on_chip(keep_a_kernel, (shaped((shard + SMALL, a_width), BF16),) * rows)
    keep_b = on_chip(keep_b_kernel, (shaped((shard, b_width), BF16),) * rows)
    row_id = row.reshape(1).astype(jnp.int32)
    ordered = rows == BLOCKS and shard % LANE == 0
    leave = [
        on_chip(functools.partial(leave_kernel, norm_width, places, False, ordered), shaped((tokens, width))),
        on_chip(
            functools.partial(leave_kernel, norm_width, places, True, ordered),
            (shaped((tokens, width)), shaped((tokens, width), BF16), shaped((tokens, LANE))),
        ),
    ]

    def in_order(grad):
        return grad if ordered else relative_order(grad, 1, "row")

    weights_a0 = both_cores(blocks_of(pieces_a0))
    held_b0 = hold(piece_b0)
    pieces_b0 = [held_b0] + [sent_to(held_b0, "row", b) for b in range(1, rows - 1)]
    aux, seg_t, *made0 = enter[0](
        core_id, hold(layer_in), before0, params[0], seg, seg_before, *weights_a0[0], *weights_a0[1]
    )
    normed0, scale0, z0, conv0, value0, scaled0, bc0, step0, cum0, cumt0, lead0, carry0, message0 = made0
    close(message0, pieces_b0)
    messages0 = [from_before(hold(message0), rows, d) for d in distances]
    pieces_b0.append(sent_to(hold(held_b0), "row", rows - 1))
    inside0 = intra(hold(scaled0), value0, bc0, cum0, cumt0, aux, seg_t, params[0])
    close(messages0, inside0, pieces_b0)
    weights_b0 = both_cores(blocks_of(pieces_b0))
    gate0 = gate_product(core_id, hold(normed0), *weights_b0[0], *weights_b0[1])
    ssd0, state0, partial0 = gates[0](
        core_id, inside0, bc0, carry0, gate0, params[0], *messages0, *weights_b0[0], *weights_b0[1]
    )
    close(partial0)
    piece_a1 = hold(pick_mine(take_a, own_a))
    pieces_a1 = [piece_a1] + [sent_to(piece_a1, "row", b) for b in range(1, rows)]
    own0 = parts_sum(hold(partial0), "col")
    square = own0[:, width : width + 1] + own0[:, width + 1 : width + 2]
    rest = square - square.astype(BF16).astype(F32)
    lanes = lax.broadcasted_iota(jnp.int32, own0.shape, 1)
    own0 = jnp.where(lanes == width, square, jnp.where(lanes == width + 1, rest, own0)).astype(BF16)
    close(own0, pieces_a1)
    piece_b1 = hold(pick_mine(take_b, own_b))
    pieces_b1 = [piece_b1] + [sent_to(piece_b1, "row", b) for b in range(1, rows)]
    weights_a1 = both_cores([hold(w) for w in blocks_of(pieces_a1)])
    full0 = spread_out(hold(own0), "col")
    close(full0, weights_a1, pieces_b1)
    full0 = hold(full0)
    squares0 = full0[:, width : width + 1].astype(F32) + full0[:, width + 1 : width + 2].astype(F32)
    rho0 = lax.rsqrt(squares0 / norm_width + EPSILON)
    x1 = (layer_in.astype(F32) + rho0 * full0[:, :width].astype(F32)).astype(BF16)

    before1 = relative_order(from_before(x1[tokens - LEAD :], rows, 1), 1, "row", other_order)
    close(x1, before1)
    weights_b1 = both_cores([hold(w) for w in blocks_of(pieces_b1)])
    made1 = enter[1](core_id, hold(x1), before1, params[1], aux, *weights_a1[0], *weights_a1[1])
    normed1, scale1, z1, conv1, value1, scaled1, bc1, step1, cum1, cumt1, lead1, carry1, message1 = made1
    close(message1, weights_b1)
    messages1 = [from_before(hold(message1), rows, d) for d in distances]
    inside1 = intra(hold(scaled1), value1, bc1, cum1, cumt1, aux, seg_t, params[1])
    gate1 = gate_product(core_id, hold(normed1), *weights_b1[0], *weights_b1[1])
    close(messages1, inside1, gate1)
    gbranch1 = branch_product(core_id, hold(g_out1), *weights_b1[0], *weights_b1[1])
    ssd1, state1, partial1, sums1 = gates[1](
        core_id, inside1, bc1, carry1, gate1, params[1], *messages1, *weights_b1[0], *weights_b1[1], gbranch1
    )
    totals1 = direct_sum(sums1, "col")
    close(totals1)
    rho1 = lax.rsqrt(totals1[0] / norm_width + EPSILON)[:, None]
    norm1 = jnp.pad(jnp.concatenate([rho1, totals1[1][:, None]], axis=1), ((0, 0), (0, LANE - 2)))

    def scan_back(layer, gbranch, norm, gate, ssd, state, made, beside):
        _, scale, z, conv, value, scaled, bc, step, cum, cumt, lead, carry, _ = made
        gssd, ggate, branch, message, ggain = ungate(gbranch, norm, gate, ssd, params[layer], carry, bc)
        close(message)
        messages = [from_after(hold(message), rows, d) for d in distances]
        gscaled, gbc, gcum = intra_grad(scaled, hold(gssd), bc, cum, cumt, aux, seg_t)
        close(messages, gscaled, beside("intra"))
        gpre, gstep, gtaps = inter_grad(
            state, scaled, value, gssd, hold(gscaled), bc, gbc, gcum, step, lead, carry, z, conv, aux, params[layer],
            ggain, *messages,
        )
        close(gpre)
        return gpre, gstep, gtaps, ggate, branch

    def reduce_back(scanned, normed, scale, x, g_out, weights_a, weights_b, beside):
        gpre, gstep, gtaps, ggate, branch = scanned
        from_next = from_after(hold(gpre[:LEAD]), rows, 1)
        other_b, gg_mine, gg_other, normed_t, g_out_t = give_b(core_id, hold(ggate), normed, g_out, branch)
        close(from_next, other_b, beside("halo"))
        their_b = swapped(hold(other_b))
        other_a, ga_mine, ga_other = give_a(core_id, gpre, hold(from_next), gstep, normed_t, gtaps)
        close(their_b, other_a, beside("give"))
        their_a = swapped(hold(other_a))
        partial, ggain = pull(
            hold(ga_mine), ga_other, gg_mine, gg_other, x, scale,
            *weights_a[0], *weights_a[1], *weights_b[0], *weights_b[1],
        )
        close(their_a, partial, beside("pull"))
        ggain = hold(ggain)
        ggain = relative_order(ggain + swapped(ggain), 1, "row")
        kept_b = keep_b(core_id, hold(normed_t), g_out_t, branch, gg_mine, their_b)
        kept_a = keep_a(normed_t, ga_mine, their_a, gtaps, ggain)
        close(kept_a, kept_b, beside("keep"))
        got_a = [sent_to(hold(v), "row", b) for b, v in enumerate(kept_a) if b]
        own = parts_sum(hold(partial), "col").astype(BF16)
        close(own, got_a, beside("scatter"))
        share_a = functools.reduce(lambda u, v: u + v.astype(F32), got_a, hold(kept_a[0]).astype(F32))
        got_b = [sent_to(hold(v), "row", b) for b, v in enumerate(kept_b) if b]
        full = spread_out(hold(own), "col")
        close(full, got_b, beside("gather", share_a))
        share_b = functools.reduce(lambda u, v: u + v.astype(F32), got_b, hold(kept_b[0]).astype(F32))
        return hold(full), share_a, share_b

    places_of = lax.broadcasted_iota(jnp.int32, (2, 1, 1), 0)

    def both_batches(below, above, place):
        mine, theirs = pick_mine(below, above), swapped(pick_mine(above, below))
        return jnp.where(places_of == place, mine[None], theirs[None])

    def settled(own, others):
        mine = pick_mine(own, others).astype(BF16)
        theirs = swapped(pick_mine(others, own).astype(BF16))
        return pick_mine(mine, theirs).astype(F32), pick_mine(theirs, mine).astype(F32)

    def state_part(share):
        return share[:shard, half : half + states].astype(BF16)

    cols = lax.axis_size("col")
    col = lax.axis_index("col")
    chunk = tokens // cols
    slots = ("intra", "halo", "pull")
    parts1 = [lax.dynamic_slice_in_dim(hold(partial1), (col ^ b) * chunk, chunk, 0) for b in range(cols)]
    received = {1: [], 0: []}
    store = {}

    def exchange(layer, name, sources):
        if name not in slots:
            return ()
        at = slots.index(name)
        mine = range(1 + at, cols) if name == slots[-1] else range(1 + at, min(2 + at, cols))
        got = [sent_to(hold(sources[b]), "col", b) for b in mine]
        received[layer] += got
        return got

    def beside1(name, share=None):
        return exchange(1, name, parts1)

    def beside0(name, share=None):
        got = list(exchange(0, name, [store["chunk"]] * cols))
        if name == "give":
            store["state"] = hold(store["state"])
            store["state_got"] = sent_to(store["state"], "col", 1)
            got.append(store["state_got"])
        if name == "keep":
            total = store["state"].astype(F32) + hold(store["state_got"]).astype(F32)
            reach_out = 2
            while reach_out < cols:
                total = total.astype(BF16)
                total = total.astype(F32) + sent_to(total, "col", reach_out).astype(F32)
                reach_out *= 2
            store["state"] = total
            got.append(total)
        if name == "scatter":
            raw1 = relative_order(jnp.concatenate([store["chunk"]] + received[0], axis=0), 0, "col")
            x2 = (hold(x1).astype(F32) + rho1 * raw1.astype(F32)).astype(BF16)
            store["outputs"] = both_batches(relative_order(x1, 1, "row"), relative_order(x2, 1, "row"), core)
            got.append(store["outputs"])
        if name == "gather":
            store["a"] = settled(share[:shard], share_a1[:shard])
            got.append(store["a"])
        return got

    scanned1 = scan_back(1, gbranch1, norm1, gate1, ssd1, state1, made1, beside1)
    grad_full1, share_a1, share_b1 = reduce_back(
        scanned1, normed1, scale1, x1, g_out1, weights_a1, weights_b1, beside1
    )
    store["chunk"] = functools.reduce(lambda u, v: u + v.astype(F32), received[1], parts1[0].astype(F32)).astype(BF16)
    store["state"] = state_part(share_a1)
    g_in1, g_out0, norm0 = leave[1](row_id, grad_full1, x1, scale1, params[1], g_out1, full0)
    gbranch0 = branch_product(core_id, g_out0, *weights_b0[0], *weights_b0[1])
    scanned0 = scan_back(0, gbranch0, norm0, gate0, ssd0, state0, made0, beside0)
    grad_full0, share_a0, share_b0 = reduce_back(
        scanned0, normed0, scale0, layer_in, g_out0, weights_a0, weights_b0, beside0
    )
    g_in0 = leave[0](row_id, grad_full0, layer_in, scale0, params[0], g_out0)
    close(g_in0)
    layer_outputs = store["outputs"]
    input_grads = both_batches(in_order(hold(g_in0)), in_order(g_in1), jnp.where(first, batch_order[0], core))

    small_sums = pick_mine(share_a0[shard:], share_a1[shard:])
    vec = jnp.concatenate([small_sums[0:8] + small_sums[8:16], small_sums[16:24] + small_sums[24:32]], axis=1)
    vec = vec[:, :conv_width]
    gain_sum = small_sums[TAPS_ROWS : TAPS_ROWS + 8] + small_sums[TAPS_ROWS + 8 :]
    partial_sums = jnp.concatenate([vec[:, inner:], gain_sum], axis=1)
    tiles = partial_sums.shape[1] // LANE
    high, low = split_pair(partial_sums)
    both = jnp.concatenate([high, low], axis=0)
    message = jnp.concatenate([hold(state_part(share_a0))] + [both[:, tile_of(i)] for i in range(tiles)], axis=0)
    summed = direct_sum(message, "col")
    state_sum0, rest_sum = summed[:shard], summed[shard:].reshape(tiles, 16, LANE)
    rest_sum = rest_sum[:, 0:8] + rest_sum[:, 8:16]
    vec_state = jnp.concatenate([rest_sum[i] for i in range(2)], axis=1)
    ggain_in = jnp.concatenate([rest_sum[i] for i in range(2, tiles)], axis=1)
    ggain_in = ggain_in[: -(-width // a_width)].reshape(1, -1)[:, :width]
    d_skip = vec[5, :inner].reshape(heads, inner // heads).sum(axis=1)

    a_low, a_high = store["a"]
    s_low, s_high = settled(state_sum0, store["state"])
    b_low, b_high = settled(share_b0, share_b1)
    d_value = jnp.concatenate([a_low[:, :half], a_high[:, :half]], axis=1)
    d_state = jnp.concatenate([s_low, s_high], axis=1)
    d_step = a_low[:, half + states : half + states + heads]
    d_gate = jnp.concatenate([b_low[:, :half], b_high[:, :half]], axis=1)
    d_out = jnp.concatenate([b_low[:, half:], b_high[:, half:]], axis=1).T

    return (
        layer_outputs[None],
        input_grads[None],
        ggain_in,
        d_gate[None],
        d_value[None],
        d_step[None],
        d_state[None],
        vec[None, 0:4, :inner],
        vec[4:5, :inner],
        vec_state[None, 0:4],
        vec_state[4:5],
        vec[7:8, :heads],
        vec[7:8, LANE : LANE + heads],
        d_skip[None],
        vec[6:7, :inner],
        d_out[None],
    )


def solution(mesh):
    in_specs = (
        P(None, "row", None),
        P(None, "row", None),
        P(None, "row"),
        P(),
        P("pipe", None),
        P("pipe", "row", "col"),
        P("pipe", "row", "col"),
        P("pipe", "row", "col"),
        P("pipe", "row", None),
        P("pipe", None, "col"),
        P("pipe", "col"),
        P("pipe", None, None),
        P("pipe", None),
        P("pipe", "col"),
        P("pipe", "col"),
        P("pipe", "col"),
        P("pipe", "col"),
        P("pipe", "col", "row"),
    )
    out_specs = (
        P("pipe", None, "row", None),
        P("pipe", None, "row", None),
        P("pipe", None),
        P("pipe", "row", "col"),
        P("pipe", "row", "col"),
        P("pipe", "row", "col"),
        P("pipe", "row", None),
        P("pipe", None, "col"),
        P("pipe", "col"),
        P("pipe", None, None),
        P("pipe", None),
        P("pipe", "col"),
        P("pipe", "col"),
        P("pipe", "col"),
        P("pipe", "col"),
        P("pipe", "col", "row"),
    )
    return jax.shard_map(local, mesh=mesh, in_specs=in_specs, out_specs=out_specs, check_vma=False)
```

```python
import functools
import math

import jax
import jax.numpy as jnp
from jax import lax
from jax.experimental import pallas as pl
from jax.experimental.pallas import tpu as pltpu
from jax.sharding import PartitionSpec as P

EPSILON = 1e-05
LOG2E = math.log2(math.e)
LANE = 128
F32 = jnp.float32
BF16 = jnp.bfloat16
SMALL_ROWS = 16
LEAD = 16
TAPS_ROWS = 32
SMALL = 48
STEPS = 16
BLOCKS = 4


def dot_nn(a, b):
    return lax.dot_general(a, b, (((1,), (0,)), ((), ())), preferred_element_type=F32)


def dot_nt(a, b):
    return lax.dot_general(a, b, (((1,), (1,)), ((), ())), preferred_element_type=F32)


def dot_tn(a, b):
    return lax.dot_general(a, b, (((0,), (0,)), ((), ())), preferred_element_type=F32)


def dot_exact(a, b):
    return lax.dot_general(
        a, b, (((1,), (0,)), ((), ())), precision=lax.Precision.HIGHEST, preferred_element_type=F32
    )


def sigmoid(v):
    return 1.0 / (1.0 + jnp.exp(-v))


def split_pair(v):
    high = v.astype(BF16)
    return high, (v - high.astype(F32)).astype(BF16)


def on_chip(kernel, out_shapes, scratch=()):
    whole = pl.BlockSpec(memory_space=pltpu.VMEM)
    scalar = pl.BlockSpec(memory_space=pltpu.SMEM)

    def call(*operands):
        return pl.pallas_call(
            kernel,
            out_shape=out_shapes,
            in_specs=[scalar if o.dtype == jnp.int32 else whole for o in operands],
            out_specs=jax.tree.map(lambda _: whole, out_shapes),
            scratch_shapes=scratch,
            compiler_params=pltpu.CompilerParams(vmem_limit_bytes=16 * 1024 * 1024),
        )(*operands)

    return call


def shaped(shape, dtype=F32):
    return jax.ShapeDtypeStruct(shape, dtype)


def tile_of(q):
    return slice(q * LANE, (q + 1) * LANE)


def spread(columns, q, heads_tile, lane_head):
    first = q * heads_tile
    out = columns[:, first : first + 1]
    for i in range(1, heads_tile):
        out = jnp.where(lane_head == i, columns[:, first + i : first + i + 1], out)
    return out


def lane_heads(rows, heads_tile):
    lanes = lax.broadcasted_iota(jnp.int32, (rows, LANE), 1)
    return lanes // (LANE // heads_tile)


def tri_mask(tokens, seg_col, seg_row, transposed):
    first = lax.broadcasted_iota(jnp.int32, (tokens, tokens), 0)
    second = lax.broadcasted_iota(jnp.int32, (tokens, tokens), 1)
    order = first <= second if transposed else first >= second
    return order & (seg_col == seg_row)


def pack_a_kernel(core_ref, value_ref, state_ref, step_ref, keep_ref, give_ref):
    shard, half = value_ref.shape[0], value_ref.shape[1] // 2
    heads = step_ref.shape[1]
    step = jnp.concatenate([step_ref[...].astype(F32), jnp.zeros((shard, LANE - heads), F32)], axis=1).T
    core = core_ref[0]
    for ref, place in ((keep_ref, core), (give_ref, 1 - core)):
        ref[:shard, :half] = value_ref[:, pl.ds(pl.multiple_of(place * half, LANE), half)]
        ref[:shard, half:] = state_ref[:, pl.ds(pl.multiple_of(place * LANE, LANE), LANE)]
        ref[shard:, :] = jnp.zeros((STEPS, ref.shape[1]), BF16)
        ref[shard:, :shard] = step[0:STEPS, :].astype(BF16)


def pack_b_kernel(core_ref, gate_ref, out_ref, keep_ref, give_ref):
    half = gate_ref.shape[1] // 2
    core = core_ref[0]
    for ref, place in ((keep_ref, core), (give_ref, 1 - core)):
        ref[:, :half] = gate_ref[:, pl.ds(pl.multiple_of(place * half, LANE), half)]
        ref[:, half:] = out_ref[pl.ds(pl.multiple_of(place * half, LANE), half), :].astype(F32).T.astype(BF16)


def enter_kernel(
    inner, heads_tile, places, core_ref, x_ref, before_ref, small_ref, aux_ref, *refs,
):
    taps_ref, heads_ref, gain_ref, _ = views(small_ref, places)
    mine, other = refs[:BLOCKS], refs[BLOCKS : 2 * BLOCKS]
    (
        normed_ref, scale_ref, z_ref, conv_ref, value_ref, scaled_ref, bc_ref, step_ref, cum_ref, cumt_ref, lead_ref,
        carry_ref, msg_ref, leadu_ref,
    ) = refs[2 * BLOCKS :]
    tokens, width = x_ref.shape
    half = inner // 2
    conv_width = conv_ref.shape[1]
    for ref, at in ((before_ref, slice(0, LEAD)), (x_ref, slice(LEAD, LEAD + tokens))):
        x = ref[...].astype(F32)
        scale = lax.rsqrt(jnp.mean(x * x, axis=1, keepdims=True) + EPSILON)
        normed_ref[at, :] = (x * scale * gain_ref[0:1, :]).astype(BF16)
    scale_ref[...] = jnp.broadcast_to(scale, scale_ref.shape)
    core = core_ref[0]
    block = width // BLOCKS
    step = None
    for pieces, place in ((mine, core), (other, 1 - core)):
        z = None
        for i in range(BLOCKS):
            normed = normed_ref[:, i * block : (i + 1) * block]
            term = dot_nn(normed, pieces[i][:block, :])
            z = term if z is None else z + term
            if pieces is mine:
                term = dot_nt(normed, pieces[i][block:, :block])
                step = term if step is None else step + term
        z_ref[:, pl.ds(pl.multiple_of(place * half, LANE), half)] = z[:, :half]
        z_ref[:, pl.ds(pl.multiple_of(inner + place * LANE, LANE), LANE)] = z[:, half:]
    z_ref[:, conv_width:] = jnp.zeros((z_ref.shape[0], LANE), F32)
    z_ref[:, conv_width : conv_width + STEPS] = step
    aux = aux_ref[...]
    raw = z_ref[LEAD:, conv_width:] + heads_ref[0:1, :]
    step = jnp.maximum(raw, 0.0) + jnp.log1p(jnp.exp(-jnp.abs(raw)))
    rates = -step * jnp.exp(heads_ref[1:2, :])
    rows = lax.broadcasted_iota(jnp.int32, (tokens, tokens), 0)
    cols = lax.broadcasted_iota(jnp.int32, (tokens, tokens), 1)
    cum = dot_exact((rows >= cols).astype(F32), rates) * LOG2E
    lead = aux[:, 5:6] * jnp.exp2(cum[tokens - 1 : tokens, :] - cum)
    carry = aux[:, 4:5] * jnp.exp2(cum)
    step_ref[...] = step
    cum_ref[...] = cum
    cumt_ref[...] = cum.T
    lead_ref[...] = lead
    carry_ref[...] = carry
    lane_head = lane_heads(tokens, heads_tile)
    for q in range(conv_width // LANE):
        at = tile_of(q)
        acc = taps_ref[4:5, at] + taps_ref[3:4, at] * z_ref[LEAD:, at]
        for j in range(3):
            shifted = z_ref[LEAD - 3 + j : LEAD - 3 + j + tokens, at]
            acc = acc + taps_ref[j : j + 1, at] * (aux[:, j : j + 1] * shifted)
        conv_ref[:, at] = acc
        value = acc * sigmoid(acc)
        if q < inner // LANE:
            value_ref[:, at] = value
            scaled = spread(step, q, heads_tile, lane_head) * value
            scaled_ref[:, at] = scaled.astype(BF16)
            leadu_ref[:, at] = (spread(lead, q, heads_tile, lane_head) * scaled).astype(BF16)
        else:
            bc_ref[:, tile_of(q - inner // LANE)] = value.astype(BF16)
    msg_ref[0:LANE, :] = dot_tn(bc_ref[:, :LANE], leadu_ref[...]).astype(BF16)
    put_through(msg_ref, carry[tokens - 1 : tokens, :], inner, heads_tile)


def enter_first_kernel(
    inner, heads_tile, places, core_ref, x_ref, before_ref, small_ref, seg_ref, seg_before_ref, *refs,
):
    weights, refs = refs[: 2 * BLOCKS], refs[2 * BLOCKS :]
    aux_ref, segt_ref, *made, seg_ext_ref, leadu_ref = refs
    tokens = x_ref.shape[0]
    seg = seg_ref[...]
    seg_ext_ref[0:LEAD, :] = seg_before_ref[...]
    seg_ext_ref[LEAD:, :] = seg
    lanes = lax.broadcasted_iota(jnp.int32, (tokens, LANE), 1)
    flags = jnp.where(lanes == 3, seg, 0.0)
    for j in range(3):
        same = (seg_ext_ref[LEAD - 3 + j : LEAD - 3 + j + tokens, :] == seg).astype(F32)
        flags = jnp.where(lanes == j, same, flags)
    flags = jnp.where(lanes == 4, (seg == seg_ext_ref[LEAD - 1 : LEAD, :]).astype(F32), flags)
    flags = jnp.where(lanes == 5, (seg == seg[tokens - 1 :, :]).astype(F32), flags)
    aux_ref[...] = flags
    segt_ref[...] = seg.T[0:8, :]
    enter_kernel(
        inner, heads_tile, places, core_ref, x_ref, before_ref, small_ref, aux_ref, *weights, *made, leadu_ref
    )


def views(ref, places):
    return tuple(ref.at[:, p] for p in places)


def put_through(msg_ref, last, inner, heads_tile):
    msg_ref[LANE:, :] = jnp.zeros((SMALL_ROWS, inner), BF16)
    lane_row = lane_heads(1, heads_tile)
    for q in range(inner // LANE):
        high, low = split_pair(spread(last, q, heads_tile, lane_row))
        msg_ref[LANE : LANE + 1, tile_of(q)] = high
        msg_ref[LANE + 1 : LANE + 2, tile_of(q)] = low


def wide_kernel(offset, lead, core_ref, a_ref, *refs):
    mine, other = refs[:BLOCKS], refs[BLOCKS : 2 * BLOCKS]
    out_ref = refs[2 * BLOCKS]
    core = core_ref[0]
    half = out_ref.shape[1] // 2
    block = a_ref.shape[1] // BLOCKS
    for pieces, place in ((mine, core), (other, 1 - core)):
        total = None
        for i in range(BLOCKS):
            term = dot_nn(a_ref[lead:, i * block : (i + 1) * block], pieces[i][:, offset : offset + half])
            total = term if total is None else total + term
        out_ref[:, pl.ds(pl.multiple_of(place * half, LANE), half)] = total


def intra_kernel(
    inner, heads_tile, places, scaled_ref, value_ref, bc_ref, cum_ref, cumt_ref, aux_ref, segt_ref, small_ref,
    out_ref,
):
    heads_ref = views(small_ref, places)[1]
    tokens = scaled_ref.shape[0]
    scores = dot_nt(bc_ref[:, LANE:], bc_ref[:, :LANE])
    scores = jnp.where(tri_mask(tokens, aux_ref[:, 3:4], segt_ref[0:1, :], False), scores, 0.0)
    lane_head = lane_heads(tokens, heads_tile)
    lane_row = lane_heads(1, heads_tile)
    for q in range(inner // LANE):
        at = tile_of(q)
        total = spread(heads_ref[2:3, :], q, heads_tile, lane_row) * value_ref[:, at]
        scaled = scaled_ref[:, at]
        for i in range(heads_tile):
            h = q * heads_tile + i
            gap = jnp.minimum(cum_ref[:, h : h + 1] - cumt_ref[h : h + 1, :], 0.0)
            mixed = (jnp.exp2(gap) * scores).astype(BF16)
            total = total + jnp.where(lane_head == i, dot_nn(mixed, scaled), 0.0)
        out_ref[:, at] = total


def enter_states(messages):
    state = None
    for message in reversed(messages):
        own = message[0:LANE, :].astype(F32)
        through = message[LANE : LANE + 1, :].astype(F32) + message[LANE + 1 : LANE + 2, :].astype(F32)
        state = own if state is None else own + through * state
    return state


def gate_kernel(
    inner, heads_tile, places, count, with_grad, core_ref, intra_ref, bc_ref, carry_ref, gate_ref, small_ref, *refs
):
    gain_ref = views(small_ref, places)[3]
    messages = refs[:count]
    mine, other = refs[count : count + BLOCKS], refs[count + BLOCKS : count + 2 * BLOCKS]
    refs = refs[count + 2 * BLOCKS :]
    if with_grad:
        branch_grad_ref, refs = refs[0], refs[1:]
        ssd_ref, state_ref, msg_ref, sums_ref, gated_ref = refs
    else:
        ssd_ref, state_ref, msg_ref, gated_ref = refs
    tokens = intra_ref.shape[0]
    state = enter_states([m[...] for m in messages]).astype(BF16)
    state_ref[...] = state
    inter = dot_nn(bc_ref[:, LANE:], state)
    lane_head = lane_heads(tokens, heads_tile)
    carry = carry_ref[...]
    squares = jnp.zeros((tokens, LANE), F32)
    products = jnp.zeros((tokens, LANE), F32)
    for q in range(inner // LANE):
        at = tile_of(q)
        ssd = intra_ref[:, at] + spread(carry, q, heads_tile, lane_head) * inter[:, at]
        ssd_ref[:, at] = ssd
        gate = gate_ref[:, at]
        gated = ssd * (gate * sigmoid(gate))
        squares = squares + gated * gated
        scaled = gated * gain_ref[0:1, at]
        gated_ref[:, at] = scaled.astype(BF16)
        if with_grad:
            products = products + scaled * branch_grad_ref[:, at]
    half = inner // 2
    core = core_ref[0]
    low = gated_ref[:, pl.ds(pl.multiple_of(core * half, LANE), half)]
    high = gated_ref[:, pl.ds(pl.multiple_of((1 - core) * half, LANE), half)]
    block = mine[0].shape[0]
    for i in range(BLOCKS):
        part = dot_nt(low, mine[i][:, half:]) + dot_nt(high, other[i][:, half:])
        msg_ref[:, i * block : (i + 1) * block] = part.astype(BF16)
    total = jnp.sum(squares, axis=1, keepdims=True)
    lanes = lax.broadcasted_iota(jnp.int32, (tokens, LANE), 1)
    if with_grad:
        packed = jnp.where(lanes == 0, total, 0.0)
        packed = packed + jnp.where(lanes == 1, jnp.sum(products, axis=1, keepdims=True), 0.0)
        sums_ref[...] = packed.T[0:8, :]
    else:
        rest = total - total.astype(BF16).astype(F32)
        packed = jnp.where(lanes == 0, total, jnp.where(lanes == 1, rest, 0.0))
        msg_ref[:, BLOCKS * block :] = packed.astype(BF16)


def ungate_kernel(
    inner, heads_tile, places, norm_width, branch_grad_ref, norm_ref, gate_ref, ssd_ref, small_ref, carry_ref, bc_ref,
    gssd_ref, ggate_ref, branch_ref, msg_ref, ggain_ref, cg_ref,
):
    gain_ref = views(small_ref, places)[3]
    tokens = branch_grad_ref.shape[0]
    rho = norm_ref[:, 0:1]
    pull = norm_ref[:, 1:2] * (rho * rho * rho / norm_width)
    lane_head = lane_heads(tokens, heads_tile)
    carry = carry_ref[...]
    ggain_ref[...] = jnp.zeros(ggain_ref.shape, F32)
    for q in range(inner // LANE):
        at = tile_of(q)
        gate = gate_ref[:, at]
        sig = sigmoid(gate)
        ssd = ssd_ref[:, at]
        gated = ssd * (gate * sig)
        grad = branch_grad_ref[:, at]
        gain = gain_ref[0:1, at]
        normed = gated * rho
        ggain_ref[0:1, at] = jnp.sum(grad * normed, axis=0, keepdims=True)
        branch_ref[:, at] = (normed * gain).astype(BF16)
        ggated = rho * (gain * grad) - gated * pull
        gssd = ggated * (gate * sig)
        gssd_ref[:, at] = gssd
        ggate_ref[:, at] = (ggated * ssd * (sig * (1.0 + gate * (1.0 - sig)))).astype(BF16)
        cg_ref[:, at] = (spread(carry, q, heads_tile, lane_head) * gssd).astype(BF16)
    msg_ref[0:LANE, :] = dot_tn(bc_ref[:, LANE:], cg_ref[...]).astype(BF16)
    put_through(msg_ref, carry[tokens - 1 : tokens, :], inner, heads_tile)


def intra_grad_kernel(
    inner, heads_tile, scaled_ref, gssd_ref, bc_ref, cum_ref, cumt_ref, aux_ref, segt_ref,
    gscaled_ref, gbc_ref, gcum_ref, sums_ref,
):
    tokens = scaled_ref.shape[0]
    mask = tri_mask(tokens, aux_ref[:, 3:4], segt_ref[0:1, :], True)
    scores = jnp.where(mask, dot_nt(bc_ref[:, :LANE], bc_ref[:, LANE:]), 0.0)
    lane_head = lane_heads(tokens, heads_tile)
    gscores = jnp.zeros((tokens, tokens), F32)
    gcum_ref[...] = jnp.zeros(gcum_ref.shape, F32)
    sums_ref[...] = jnp.zeros(sums_ref.shape, F32)
    for q in range(inner // LANE):
        at = tile_of(q)
        grad = gssd_ref[:, at].astype(BF16)
        scaled = scaled_ref[:, at]
        total = jnp.zeros((tokens, LANE), F32)
        for i in range(heads_tile):
            h = q * heads_tile + i
            gap = jnp.minimum(cumt_ref[h : h + 1, :] - cum_ref[:, h : h + 1], 0.0)
            decay = jnp.exp2(gap)
            mixed = decay * scores
            picked = jnp.where(lane_head == i, scaled, jnp.zeros_like(scaled))
            gmixed = dot_nt(picked, grad)
            total = total + jnp.where(lane_head == i, dot_nn(mixed.astype(BF16), grad), 0.0)
            product = gmixed * mixed
            sums_ref[h : h + 1, :] = jnp.sum(product, axis=0, keepdims=True)
            gcum_ref[:, h : h + 1] = -jnp.sum(product, axis=1, keepdims=True)
            gscores = gscores + gmixed * decay
        gscaled_ref[:, at] = total
    gscores = jnp.where(mask, gscores, 0.0)
    gbc_ref[:, :LANE] = dot_nn(gscores.astype(BF16), bc_ref[:, LANE:])
    gbc_ref[:, LANE:] = dot_nn(gscores.T.astype(BF16), bc_ref[:, :LANE])
    gcum_ref[...] = gcum_ref[...] + sums_ref[...].T


def inter_grad_kernel(
    inner, heads_tile, places, count, state_ref, scaled_ref, value_ref, gssd_ref, gscaled_ref, bc_ref, gbc_ref, gcum_ref,
    step_ref, lead_ref, carry_ref, z_ref, conv_ref, aux_ref, small_ref, ggain_ref, *refs,
):
    taps_ref, heads_ref, _, _ = views(small_ref, places)
    messages = refs[:count]
    gpre_ref, gstep_ref, gtaps_ref, em_ref, leadu_ref, cg_ref, gain_ref, lose_ref, gsize_ref = refs[count:]
    tokens = scaled_ref.shape[0]
    width = conv_ref.shape[1]
    aux = aux_ref[...]
    adjoint = enter_states([m[...] for m in messages])
    adjoint_low = adjoint.astype(BF16)
    state = state_ref[...]
    from_adjoint = dot_nn(bc_ref[:, :LANE], adjoint_low)
    from_state = dot_nn(bc_ref[:, LANE:], state)
    overlap = jnp.sum(adjoint * state.astype(F32), axis=0, keepdims=True)
    lane_head = lane_heads(tokens, heads_tile)
    lane_row = lane_heads(1, heads_tile)
    step = step_ref[...]
    lead = lead_ref[...]
    carry = carry_ref[...]
    em_ref[0:8, :] = jnp.zeros((8, LANE), F32)
    em_ref[8 + tokens :, :] = jnp.zeros((8, LANE), F32)
    gpre_ref[0:8, :] = jnp.zeros((8, width), F32)
    gtaps_ref[...] = jnp.zeros(gtaps_ref.shape, F32)

    def through_conv(q, grad):
        at = tile_of(q)
        conv = conv_ref[:, at]
        sig = sigmoid(conv)
        e = grad * (sig * (1.0 + conv * (1.0 - sig)))
        gtaps_ref[4:5, at] = jnp.sum(e, axis=0, keepdims=True)
        gtaps_ref[3:4, at] = jnp.sum(e * z_ref[LEAD:, at], axis=0, keepdims=True)
        total = None
        for j in range(3):
            masked = aux[:, j : j + 1] * e
            shifted = z_ref[LEAD - 3 + j : LEAD - 3 + j + tokens, at]
            gtaps_ref[j : j + 1, at] = jnp.sum(masked * shifted, axis=0, keepdims=True)
            em_ref[8 : 8 + tokens, :] = masked
            term = taps_ref[j : j + 1, at] * em_ref[3 - j : 11 - j + tokens, :]
            total = term if total is None else total + term
        gpre_ref[8:LEAD, at] = total[0:8, :]
        gpre_ref[LEAD:, at] = total[8:, :] + taps_ref[3:4, at] * e

    for q in range(inner // LANE):
        at = tile_of(q)
        scaled = scaled_ref[:, at].astype(F32)
        grad = gssd_ref[:, at]
        value = value_ref[:, at]
        leads = spread(lead, q, heads_tile, lane_head)
        carries = spread(carry, q, heads_tile, lane_head)
        pushed = leads * from_adjoint[:, at]
        gscaled = gscaled_ref[:, at] + pushed
        carried = carries * grad
        leadu_ref[:, at] = (leads * scaled).astype(BF16)
        cg_ref[:, at] = carried.astype(BF16)
        gain_ref[:, at] = (carried * from_state[:, at]).astype(BF16)
        lose_ref[:, at] = (scaled * pushed).astype(BF16)
        gsize_ref[:, at] = (gscaled * value).astype(BF16)
        gtaps_ref[5:6, at] = jnp.sum(grad * value, axis=0, keepdims=True)
        gvalue = spread(step, q, heads_tile, lane_head) * gscaled
        gvalue = gvalue + spread(heads_ref[2:3, :], q, heads_tile, lane_row) * grad
        through_conv(q, gvalue)
    gb = gbc_ref[:, :LANE] + dot_nt(leadu_ref[...], adjoint_low)
    gc = gbc_ref[:, LANE:] + dot_nt(cg_ref[...], state)
    through_conv(inner // LANE, gb)
    through_conv(inner // LANE + 1, gc)
    head_of = lax.broadcasted_iota(jnp.int32, (inner, LANE), 0) // (LANE // heads_tile)
    pick = (head_of == lax.broadcasted_iota(jnp.int32, (inner, LANE), 1)).astype(BF16)
    lose = dot_nn(lose_ref[...], pick)
    gcum = gcum_ref[...] + dot_nn(gain_ref[...], pick) - lose
    high, low = split_pair(overlap)
    ends = dot_nn(jnp.broadcast_to(high, (8, inner)), pick) + dot_nn(jnp.broadcast_to(low, (8, inner)), pick)
    last = carry[tokens - 1 : tokens, :] * ends[0:1, :] + jnp.sum(lose, axis=0, keepdims=True)
    row_of = lax.broadcasted_iota(jnp.int32, (tokens, LANE), 0)
    gcum = gcum + jnp.where(row_of == tokens - 1, last, 0.0)
    rows = lax.broadcasted_iota(jnp.int32, (tokens, tokens), 0)
    cols = lax.broadcasted_iota(jnp.int32, (tokens, tokens), 1)
    grate = dot_exact((rows <= cols).astype(F32), gcum)
    speed = jnp.exp(heads_ref[1:2, :])
    gsize = dot_nn(gsize_ref[...], pick) - speed * grate
    raw = z_ref[LEAD:, width:] + heads_ref[0:1, :]
    graw = gsize * sigmoid(raw)
    gstep_ref[...] = graw.astype(BF16)
    gtaps_ref[6:7, :inner] = ggain_ref[0:1, :]
    gtaps_ref[7:8, 0:LANE] = jnp.sum(graw, axis=0, keepdims=True)
    gtaps_ref[7:8, LANE : 2 * LANE] = jnp.sum(grate * (-speed * step), axis=0, keepdims=True)


def give_b_kernel(
    core_ref, ggate_ref, normed_ref, g_out_ref, branch_ref,
    other_b_ref, gg_mine_ref, gg_other_ref, normed_t_ref, g_out_t_ref,
):
    width = g_out_ref.shape[1]
    half = ggate_ref.shape[1] // 2
    core = core_ref[0]
    gg_mine_ref[...] = ggate_ref[:, pl.ds(pl.multiple_of(core * half, LANE), half)]
    gg_other_ref[...] = ggate_ref[:, pl.ds(pl.multiple_of((1 - core) * half, LANE), half)]
    block = width // BLOCKS
    for i in range(BLOCKS):
        at = slice(i * block, (i + 1) * block)
        normed_t_ref[at, :] = normed_ref[LEAD:, at].astype(F32).T.astype(BF16)
        g_out_t_ref[at, :] = g_out_ref[:, at].astype(F32).T.astype(BF16)
    other_b_ref[:, :half] = dot_nn(normed_t_ref[...], gg_other_ref[...]).astype(BF16)
    branch = branch_ref[:, pl.ds(pl.multiple_of((1 - core) * half, LANE), half)]
    other_b_ref[:, half:] = dot_nn(g_out_t_ref[...], branch).astype(BF16)


def keep_b_kernel(core_ref, normed_t_ref, g_out_t_ref, branch_ref, gg_mine_ref, their_ref, *refs):
    size = normed_t_ref.shape[0] // len(refs)
    half = gg_mine_ref.shape[1]
    branch = branch_ref[:, pl.ds(pl.multiple_of(core_ref[0] * half, LANE), half)]
    for i, ref in enumerate(refs):
        at = slice(i * size, (i + 1) * size)
        part = dot_nn(normed_t_ref[at, :], gg_mine_ref[...]) + their_ref[at, :half].astype(F32)
        ref[:, :half] = part.astype(BF16)
        part = dot_nn(g_out_t_ref[at, :], branch) + their_ref[at, half:].astype(F32)
        ref[:, half:] = part.astype(BF16)


def taps_rows(taps, wide):
    left, right = taps[:, :wide], taps[:, wide:]
    rows = []
    for part in (left, right):
        high = part.astype(BF16).astype(F32)
        rows += [high, part - high]
    return jnp.concatenate(rows, axis=0).astype(BF16)


def gain_rows(gain, wide):
    high = gain.astype(BF16).astype(F32)
    index = lax.broadcasted_iota(jnp.int32, (16, wide), 0)
    out = jnp.zeros((16, wide), F32)
    count = -(-gain.shape[1] // wide)
    for i in range(count):
        for base, part in ((0, high), (8, gain - high)):
            piece = part[:, i * wide : (i + 1) * wide]
            if piece.shape[1] < wide:
                piece = jnp.concatenate([piece, jnp.zeros((1, wide - piece.shape[1]), F32)], axis=1)
            out = jnp.where(index == base + i, piece, out)
    return out.astype(BF16)


def give_a_kernel(
    core_ref, gpre_ref, next_ref, gstep_ref, normed_t_ref, gtaps_ref, other_a_ref, ga_mine_ref, ga_other_ref, glow_ref
):
    tokens, width = glow_ref.shape
    inner = width - 2 * LANE
    half = inner // 2
    core = core_ref[0]
    cut = tokens - LEAD
    glow_ref[:cut, :] = gpre_ref[LEAD : LEAD + cut, :].astype(BF16)
    glow_ref[cut:, :] = (gpre_ref[LEAD + cut :, :] + next_ref[...]).astype(BF16)
    for ga_ref, place in ((ga_mine_ref, core), (ga_other_ref, 1 - core)):
        ga_ref[:, :half] = glow_ref[:, pl.ds(pl.multiple_of(place * half, LANE), half)]
        ga_ref[:, half:] = glow_ref[:, pl.ds(pl.multiple_of(inner + place * LANE, LANE), LANE)]
    rows, wide = normed_t_ref.shape[0], other_a_ref.shape[1]
    other_a_ref[:rows, :] = dot_nn(normed_t_ref[...], ga_other_ref[...]).astype(BF16)
    steps = step_grads(gstep_ref, normed_t_ref)
    for i in range(rows // wide):
        other_a_ref[rows + STEPS * i : rows + STEPS * (i + 1), :] = steps[:, i * wide : (i + 1) * wide].astype(BF16)
    other_a_ref[rows + STEPS * (rows // wide) :, :] = taps_rows(gtaps_ref[...], wide)


def step_grads(gstep_ref, normed_t_ref):
    return dot_nt(gstep_ref[...].astype(F32).T[0:STEPS, :].astype(BF16), normed_t_ref[...])


def keep_a_kernel(normed_t_ref, ga_mine_ref, gstep_ref, their_ref, gtaps_ref, ggain_ref, *refs):
    rows = normed_t_ref.shape[0]
    size = rows // len(refs)
    wide = ga_mine_ref.shape[1]
    groups = [
        their_ref[rows + STEPS * i : rows + STEPS * (i + 1), :].astype(F32) for i in range(rows // wide + TAPS_ROWS // STEPS)
    ]
    steps = step_grads(gstep_ref, normed_t_ref) + jnp.concatenate(groups[: rows // wide], axis=1)
    taps = jnp.concatenate([t[0:8] + t[8:16] for t in groups[rows // wide :]], axis=1)[:, : gtaps_ref.shape[1]]
    small = taps_rows(taps + gtaps_ref[...], wide)
    gain = gain_rows(ggain_ref[0:1, :], wide)
    below = size + STEPS
    for i, ref in enumerate(refs):
        at = slice(i * size, (i + 1) * size)
        ref[:size, :] = (dot_nn(normed_t_ref[at, :], ga_mine_ref[...]) + their_ref[at, :].astype(F32)).astype(BF16)
        ref[size:below, :] = jnp.zeros((STEPS, wide), BF16)
        ref[size:below, :size] = steps[:, at].astype(BF16)
        ref[below : below + TAPS_ROWS, :] = small
        ref[below + TAPS_ROWS :, :] = gain


def pull_kernel(ga_mine_ref, ga_other_ref, gstep_ref, gg_mine_ref, gg_other_ref, x_ref, scale_ref, *refs):
    mine_a, other_a, mine_b, other_b = (refs[i * BLOCKS : (i + 1) * BLOCKS] for i in range(4))
    msg_ref, ggain_ref = refs[4 * BLOCKS :]
    half = gg_mine_ref.shape[1]
    block = mine_b[0].shape[0]
    scale = scale_ref[:, 0:1]
    ggain_ref[...] = jnp.zeros(ggain_ref.shape, F32)
    for i in range(BLOCKS):
        at = slice(i * block, (i + 1) * block)
        part = dot_nt(ga_mine_ref[...], mine_a[i][:block, :])
        part = part + dot_nt(ga_other_ref[...], other_a[i][:block, :])
        part = part + dot_nn(gstep_ref[:, :STEPS], mine_a[i][block:, :block])
        part = part + dot_nt(gg_mine_ref[...], mine_b[i][:, :half])
        part = part + dot_nt(gg_other_ref[...], other_b[i][:, :half])
        msg_ref[:, at] = part.astype(BF16)
        ggain_ref[0:1, at] = jnp.sum(part * (x_ref[:, at].astype(F32) * scale), axis=0, keepdims=True)


def leave_kernel(norm_width, places, below, ordered, row_ref, full_ref, x_ref, scale_ref, small_ref, g_out_ref, *refs):
    gain_ref = views(small_ref, places)[2]
    if below:
        raw_ref, grad_ref, low_ref, norm_ref = refs
    else:
        (grad_ref,) = refs
    tokens, width = x_ref.shape
    scale = scale_ref[:, 0:1]
    x = x_ref[...].astype(F32)
    pulled = full_ref[...].astype(F32) * gain_ref[0:1, :]
    slope = jnp.sum(pulled * x, axis=1, keepdims=True) * (scale * scale * scale / width)
    grad = g_out_ref[...].astype(F32) + scale * pulled - x * slope
    if ordered:
        block = width // BLOCKS
        for i in range(BLOCKS):
            start = pl.multiple_of((row_ref[0] ^ i) * block, LANE)
            grad_ref[:, pl.ds(start, block)] = grad[:, i * block : (i + 1) * block]
    else:
        grad_ref[...] = grad
    if below:
        low = grad.astype(BF16)
        low_ref[...] = low
        dots = jnp.sum(low.astype(F32) * raw_ref[:, :width].astype(F32), axis=1, keepdims=True)
        squares = raw_ref[:, width : width + 1].astype(F32) + raw_ref[:, width + 1 : width + 2].astype(F32)
        lanes = lax.broadcasted_iota(jnp.int32, (tokens, LANE), 1)
        norm_ref[...] = jnp.where(lanes == 0, lax.rsqrt(squares / norm_width + EPSILON), dots)


def permute(block, axis, route):
    return lax.ppermute(block, axis, route)


def from_before(block, count, distance):
    return permute(block, "row", [(i, i + distance) for i in range(count - distance)])


def from_after(block, count, distance):
    return permute(block, "row", [(i + distance, i) for i in range(count - distance)])


def swapped(block):
    return permute(block, "pipe", [(0, 1), (1, 0)])


def exchanged(blocks, axis):
    return lax.all_to_all(blocks, axis, 0, 0)


def spread_out(block, axis):
    count = lax.axis_size(axis)
    return exchanged(jnp.broadcast_to(block[None], (count,) + block.shape), axis).reshape(
        (count * block.shape[0],) + block.shape[1:]
    )


def parts_sum(block, axis):
    count = lax.axis_size(axis)
    parts = exchanged(block.reshape((count, block.shape[0] // count) + block.shape[1:]), axis)
    return jnp.sum(parts.astype(F32), axis=0)


def direct_sum(block, axis):
    parts = [block] + [sent_to(block, axis, b) for b in range(1, lax.axis_size(axis))]
    parts = [p.astype(F32) for p in parts]
    while len(parts) > 1:
        parts = [parts[i] + parts[i + 1] for i in range(0, len(parts), 2)]
    return parts[0]


def sent_to(block, axis, flip):
    count = lax.axis_size(axis)
    return permute(block, axis, [(i, i ^ flip) for i in range(count)])


def relative_order(block, dim, axis, place=None):
    count = lax.axis_size(axis)
    size = block.shape[dim] // count
    place = lax.axis_index(axis) if place is None else place
    return jnp.concatenate(
        [lax.dynamic_slice_in_dim(block, (place ^ b) * size, size, dim) for b in range(count)], axis=dim
    )


class Phases:
    def __init__(self, token):
        self.token = token

    def hold(self, value):
        return lax.optimization_barrier((value, self.token))[0]

    def close(self, *values):
        self.token = lax.optimization_barrier((self.token,) + tuple(jax.tree.leaves(values)))[0]


def col_gather(block):
    return lax.all_gather(block, "col", axis=0, tiled=True)


def after(block, *others):
    return lax.optimization_barrier((block,) + others)[0]


def local(
    inputs, cotangent, segment_ids, batch_order, norm_gain, gate_proj, value_proj, step_proj, state_proj,
    conv_value, conv_value_bias, conv_state, conv_state_bias, step_bias, decay_log, skip_gain, gate_gain, out_proj,
):
    core = lax.axis_index("pipe")
    first = core == 0
    core_id = core.reshape(1).astype(jnp.int32)
    rows = lax.axis_size("row")
    row = lax.axis_index("row")
    tokens, width = inputs.shape[1], inputs.shape[2]
    inner = gate_proj.shape[2]
    heads = step_proj.shape[2]
    states = state_proj.shape[2] // 2
    heads_tile = LANE // (inner // heads)
    half = inner // 2
    conv_width = inner + 2 * states
    norm_width = inner * lax.axis_size("col")
    reach = max(rows // 2, 1)
    distances = range(1, reach + 1)
    group = rows // BLOCKS

    def pick_mine(a, b):
        return jnp.where(first, a, b)

    phases = Phases(core_id)
    hold, close = phases.hold, phases.close

    shard = gate_proj.shape[1]
    a_width, b_width = half + states, inner
    own_a, away_a = on_chip(pack_a_kernel, (shaped((shard + STEPS, a_width), BF16),) * 2)(
        core_id, value_proj[0], state_proj[0], step_proj[0]
    )
    close(away_a)
    take_a = swapped(hold(away_a))
    own_b, away_b = on_chip(pack_b_kernel, (shaped((shard, b_width), BF16),) * 2)(core_id, hold(gate_proj[0]), out_proj[0])
    close(take_a, away_b)

    def blocks_of(pieces):
        if pieces[0].shape[0] > shard and group > 1:
            made = []
            for i in range(BLOCKS):
                part = pieces[i * group : (i + 1) * group]
                steps = jnp.concatenate([p[shard:, :shard] for p in part], axis=1)
                steps = jnp.pad(steps, ((0, 0), (0, a_width - steps.shape[1])))
                made.append(jnp.concatenate([p[:shard] for p in part] + [steps], axis=0))
            return made
        return [jnp.concatenate(pieces[i * group : (i + 1) * group], axis=0) for i in range(BLOCKS)]

    near = 3 if rows == BLOCKS else rows

    def sent_near(block):
        return [block] + [sent_to(block, "row", b) for b in range(1, near)]

    def passed_on(pieces):
        if rows != BLOCKS:
            return []
        cut = -(-pieces[0].shape[0] // 32) * 16
        return [jnp.concatenate([sent_to(pieces[1][:cut], "row", 2), sent_to(pieces[2][cut:], "row", 1)], axis=0)]

    def both_cores(mine):
        return mine, [swapped(p) for p in mine]

    piece_a0 = hold(pick_mine(own_a, take_a))
    pieces_a0 = sent_near(piece_a0)
    take_b = swapped(hold(away_b))
    piece_b0 = pick_mine(own_b, take_b)

    taps_own = jnp.concatenate(
        [
            jnp.concatenate([hold(conv_value[0]), conv_state[0]], axis=1),
            jnp.concatenate([conv_value_bias, conv_state_bias], axis=1),
            jnp.zeros((3, conv_width), F32),
        ],
        axis=0,
    )
    heads_own = jnp.pad(jnp.concatenate([hold(step_bias), decay_log, skip_gain], axis=0), ((0, 5), (0, LANE - heads)))
    gains_own = jnp.concatenate([relative_order(hold(norm_gain), 1, "row"), gate_gain], axis=1)
    gains_own = jnp.pad(gains_own, ((0, 7), (0, 0)))
    small = jnp.concatenate([taps_own, heads_own, gains_own], axis=1)
    small_other = swapped(small)
    params = (pick_mine(small, small_other), pick_mine(small_other, small))
    places = (slice(0, conv_width), slice(conv_width, conv_width + LANE))
    places += (slice(conv_width + LANE, conv_width + LANE + width), slice(conv_width + LANE + width, small.shape[1]))

    source = hold(batch_order)[core]
    layer_in = relative_order(inputs[source], 1, "row")
    seg = jnp.broadcast_to(segment_ids[source].astype(F32)[:, None], (tokens, LANE))
    sent_rows = jnp.concatenate([layer_in[tokens - LEAD :], seg[tokens - LEAD :].astype(BF16)], axis=1)
    got_rows = from_before(sent_rows, rows, 1)
    other_order = row ^ jnp.maximum(row - 1, 0)
    before0 = relative_order(got_rows[:, :width], 1, "row", other_order)
    seg_before = jnp.where(row == 0, -1.0, got_rows[:, width:].astype(F32))
    g_out1 = relative_order(hold(cotangent)[core], 1, "row")
    close(pieces_a0, piece_b0, params, layer_in, seg, before0, seg_before, g_out1)

    long = tokens + LEAD
    message_shape = shaped((states + SMALL_ROWS, inner), BF16)
    entered = (
        shaped((long, width), BF16), shaped((tokens, LANE)), shaped((long, conv_width + LANE)),
        shaped((tokens, conv_width)), shaped((tokens, inner)), shaped((tokens, inner), BF16),
        shaped((tokens, 2 * states), BF16), shaped((tokens, LANE)), shaped((tokens, LANE)), shaped((LANE, tokens)),
        shaped((tokens, LANE)), shaped((tokens, LANE)), message_shape,
    )
    enter = [
        on_chip(
            functools.partial(enter_first_kernel, inner, heads_tile, places),
            (shaped((tokens, LANE)), shaped((8, tokens))) + entered,
            [pltpu.VMEM((long, LANE), F32), pltpu.VMEM((tokens, inner), BF16)],
        ),
        on_chip(
            functools.partial(enter_kernel, inner, heads_tile, places), entered, [pltpu.VMEM((tokens, inner), BF16)]
        ),
    ]
    intra = on_chip(functools.partial(intra_kernel, inner, heads_tile, places), shaped((tokens, inner)))
    gate_product = on_chip(functools.partial(wide_kernel, 0, LEAD), shaped((tokens, inner)))
    branch_product = on_chip(functools.partial(wide_kernel, half, 0), shaped((tokens, inner)))
    gates = [
        on_chip(
            functools.partial(gate_kernel, inner, heads_tile, places, reach, with_grad),
            (shaped((tokens, inner)), shaped((states, inner), BF16))
            + ((shaped((tokens, width), BF16), shaped((8, tokens))) if with_grad else (shaped((tokens, width + LANE), BF16),)),
            [pltpu.VMEM((tokens, inner), BF16)],
        )
        for with_grad in (False, True)
    ]
    ungate = on_chip(
        functools.partial(ungate_kernel, inner, heads_tile, places, norm_width),
        (
            shaped((tokens, inner)), shaped((tokens, inner), BF16), shaped((tokens, inner), BF16), message_shape,
            shaped((8, inner)),
        ),
        [pltpu.VMEM((tokens, inner), BF16)],
    )
    intra_grad = on_chip(
        functools.partial(intra_grad_kernel, inner, heads_tile),
        (shaped((tokens, inner)), shaped((tokens, 2 * states)), shaped((tokens, LANE))),
        [pltpu.VMEM((LANE, tokens), F32)],
    )
    inter_grad = on_chip(
        functools.partial(inter_grad_kernel, inner, heads_tile, places, reach),
        (shaped((long, conv_width)), shaped((tokens, LANE), BF16), shaped((8, conv_width))),
        [pltpu.VMEM((tokens + 16, LANE), F32)] + [pltpu.VMEM((tokens, inner), BF16)] * 5,
    )
    pull = on_chip(pull_kernel, (shaped((tokens, width), BF16), shaped((8, width))))
    weight_t = shaped((width, tokens), BF16)
    give_a = on_chip(
        give_a_kernel,
        (shaped((width + STEPS * (width // a_width) + TAPS_ROWS, a_width), BF16),) + (shaped((tokens, a_width), BF16),) * 2,
        [pltpu.VMEM((tokens, conv_width), BF16)],
    )
    give_b = on_chip(
        give_b_kernel,
        (shaped((width, b_width), BF16), shaped((tokens, half), BF16), shaped((tokens, half), BF16), weight_t, weight_t),
    )
    keep_a = on_chip(keep_a_kernel, (shaped((shard + STEPS + SMALL, a_width), BF16),) * rows)
    keep_b = on_chip(keep_b_kernel, (shaped((shard, b_width), BF16),) * rows)
    row_id = row.reshape(1).astype(jnp.int32)
    ordered = rows == BLOCKS and shard % LANE == 0
    leave = [
        on_chip(functools.partial(leave_kernel, norm_width, places, False, ordered), shaped((tokens, width))),
        on_chip(
            functools.partial(leave_kernel, norm_width, places, True, ordered),
            (shaped((tokens, width)), shaped((tokens, width), BF16), shaped((tokens, LANE))),
        ),
    ]

    def in_order(grad):
        return grad if ordered else relative_order(grad, 1, "row")

    pieces_a0 = [hold(p) for p in pieces_a0]
    pieces_b0 = sent_near(hold(piece_b0))
    pieces_a0 += passed_on(pieces_a0)
    close(pieces_a0, pieces_b0)
    weights_a0 = both_cores(blocks_of(pieces_a0))
    pieces_b0 = [hold(p) for p in pieces_b0]
    pieces_b0 += passed_on(pieces_b0)
    aux, seg_t, *made0 = enter[0](
        core_id, hold(layer_in), before0, params[0], seg, seg_before, *weights_a0[0], *weights_a0[1]
    )
    normed0, scale0, z0, conv0, value0, scaled0, bc0, step0, cum0, cumt0, lead0, carry0, message0 = made0
    close(message0, pieces_b0)
    messages0 = [from_before(hold(message0), rows, d) for d in distances]
    weights_b0 = both_cores([hold(w) for w in blocks_of(pieces_b0)])
    inside0 = intra(hold(scaled0), value0, bc0, cum0, cumt0, aux, seg_t, params[0])
    close(messages0, inside0, weights_b0)
    gate0 = gate_product(core_id, hold(normed0), *weights_b0[0], *weights_b0[1])
    ssd0, state0, partial0 = gates[0](
        core_id, inside0, bc0, carry0, gate0, params[0], *messages0, *weights_b0[0], *weights_b0[1]
    )
    close(partial0)
    pieces_a1 = sent_near(hold(pick_mine(take_a, own_a)))
    pieces_b1 = sent_near(hold(pick_mine(take_b, own_b)))
    own0 = parts_sum(hold(partial0), "col")
    square = own0[:, width : width + 1] + own0[:, width + 1 : width + 2]
    rest = square - square.astype(BF16).astype(F32)
    lanes = lax.broadcasted_iota(jnp.int32, own0.shape, 1)
    own0 = jnp.where(lanes == width, square, jnp.where(lanes == width + 1, rest, own0)).astype(BF16)
    close(own0, pieces_a1, pieces_b1)
    pieces_a1, pieces_b1 = [hold(p) for p in pieces_a1], [hold(p) for p in pieces_b1]
    pieces_a1 += passed_on(pieces_a1)
    pieces_b1 += passed_on(pieces_b1)
    full0 = col_gather(hold(own0))
    weights_a1 = both_cores(blocks_of(pieces_a1))
    close(full0, weights_a1, pieces_b1)
    full0 = hold(full0)
    squares0 = full0[:, width : width + 1].astype(F32) + full0[:, width + 1 : width + 2].astype(F32)
    rho0 = lax.rsqrt(squares0 / norm_width + EPSILON)
    x1 = (layer_in.astype(F32) + rho0 * full0[:, :width].astype(F32)).astype(BF16)

    before1 = relative_order(from_before(x1[tokens - LEAD :], rows, 1), 1, "row", other_order)
    close(x1, before1)
    weights_b1 = both_cores([hold(w) for w in blocks_of(pieces_b1)])
    made1 = enter[1](core_id, hold(x1), before1, params[1], aux, *weights_a1[0], *weights_a1[1])
    normed1, scale1, z1, conv1, value1, scaled1, bc1, step1, cum1, cumt1, lead1, carry1, message1 = made1
    close(message1, weights_b1)
    messages1 = [from_before(hold(message1), rows, d) for d in distances]
    inside1 = intra(hold(scaled1), value1, bc1, cum1, cumt1, aux, seg_t, params[1])
    gate1 = gate_product(core_id, hold(normed1), *weights_b1[0], *weights_b1[1])
    close(messages1, inside1, gate1)
    gbranch1 = branch_product(core_id, hold(g_out1), *weights_b1[0], *weights_b1[1])
    ssd1, state1, partial1, sums1 = gates[1](
        core_id, inside1, bc1, carry1, gate1, params[1], *messages1, *weights_b1[0], *weights_b1[1], gbranch1
    )
    totals1 = direct_sum(sums1, "col")
    close(totals1)
    rho1 = lax.rsqrt(totals1[0] / norm_width + EPSILON)[:, None]
    norm1 = jnp.pad(jnp.concatenate([rho1, totals1[1][:, None]], axis=1), ((0, 0), (0, LANE - 2)))

    def scan_back(layer, gbranch, norm, gate, ssd, state, made, beside):
        _, scale, z, conv, value, scaled, bc, step, cum, cumt, lead, carry, _ = made
        gssd, ggate, branch, message, ggain = ungate(gbranch, norm, gate, ssd, params[layer], carry, bc)
        close(message)
        messages = [from_after(hold(message), rows, d) for d in distances]
        gscaled, gbc, gcum = intra_grad(scaled, hold(gssd), bc, cum, cumt, aux, seg_t)
        close(messages, gscaled, beside("intra"))
        gpre, gstep, gtaps = inter_grad(
            state, scaled, value, gssd, hold(gscaled), bc, gbc, gcum, step, lead, carry, z, conv, aux, params[layer],
            ggain, *messages,
        )
        close(gpre)
        return gpre, gstep, gtaps, ggate, branch

    def reduce_back(scanned, normed, scale, x, g_out, weights_a, weights_b, beside):
        gpre, gstep, gtaps, ggate, branch = scanned
        from_next = from_after(hold(gpre[:LEAD]), rows, 1)
        other_b, gg_mine, gg_other, normed_t, g_out_t = give_b(core_id, hold(ggate), normed, g_out, branch)
        close(from_next, other_b, beside("halo"))
        their_b = swapped(hold(other_b))
        other_a, ga_mine, ga_other = give_a(core_id, gpre, hold(from_next), gstep, normed_t, gtaps)
        close(their_b, other_a, beside("give"))
        their_a = swapped(hold(other_a))
        partial, ggain = pull(
            hold(ga_mine), ga_other, gstep, gg_mine, gg_other, x, scale,
            *weights_a[0], *weights_a[1], *weights_b[0], *weights_b[1],
        )
        close(their_a, partial, beside("pull"))
        ggain = hold(ggain)
        ggain = relative_order(ggain + swapped(ggain), 1, "row")
        kept_b = keep_b(core_id, hold(normed_t), g_out_t, branch, gg_mine, their_b)
        kept_a = keep_a(normed_t, ga_mine, gstep, their_a, gtaps, ggain)
        close(kept_a, kept_b, beside("keep"))
        def sends(blocks, which):
            return [sent_to(hold(blocks[b]), "row", b) for b in which]

        early, late = range(1, near), range(near, rows)
        got_a, got_b = sends(kept_a, early), sends(kept_b, early)
        own = parts_sum(hold(partial), "col").astype(BF16)
        close(own, got_a, got_b, beside("scatter"))
        got_a += sends(kept_a, late)
        got_b += sends(kept_b, late)
        full = col_gather(hold(own))
        close(full, got_a, got_b)

        def total(mine, got):
            return functools.reduce(lambda u, v: u + v.astype(F32), got, hold(mine).astype(F32))

        share_a, share_b = total(kept_a[0], got_a), total(kept_b[0], got_b)
        return hold(full), share_a, share_b

    places_of = lax.broadcasted_iota(jnp.int32, (2, 1, 1), 0)

    def both_batches(below, above, place):
        mine, theirs = pick_mine(below, above), swapped(pick_mine(above, below))
        return jnp.where(places_of == place, mine[None], theirs[None])

    def settled(own, others):
        mine = pick_mine(own, others).astype(BF16)
        theirs = swapped(pick_mine(others, own).astype(BF16))
        return pick_mine(mine, theirs).astype(F32), pick_mine(theirs, mine).astype(F32)

    def state_part(share):
        return share[:shard, half : half + states].astype(BF16)

    cols = lax.axis_size("col")
    col = lax.axis_index("col")
    chunk = tokens // cols
    slots = ("intra", "halo", "pull")
    parts1 = [lax.dynamic_slice_in_dim(hold(partial1), (col ^ b) * chunk, chunk, 0) for b in range(cols)]
    received = {1: [], 0: []}
    store = {}

    def exchange(layer, name, sources):
        if name not in slots:
            return ()
        at = slots.index(name)
        mine = range(1 + at, cols) if name == slots[-1] else range(1 + at, min(2 + at, cols))
        got = [sent_to(hold(sources[b]), "col", b) for b in mine]
        received[layer] += got
        return got

    def beside1(name):
        return exchange(1, name, parts1)

    def beside0(name):
        got = list(exchange(0, name, [store["chunk"]] * cols))
        if name == "give":
            store["state"] = hold(store["state"])
            store["state_got"] = sent_to(store["state"], "col", 1)
            got.append(store["state_got"])
        if name == "keep":
            total = store["state"].astype(F32) + hold(store["state_got"]).astype(F32)
            reach_out = 2
            while reach_out < cols:
                total = total.astype(BF16)
                total = total.astype(F32) + sent_to(total, "col", reach_out).astype(F32)
                reach_out *= 2
            store["state"] = total
            got.append(total)
        if name == "scatter":
            raw1 = relative_order(jnp.concatenate([store["chunk"]] + received[0], axis=0), 0, "col")
            x2 = (hold(x1).astype(F32) + rho1 * raw1.astype(F32)).astype(BF16)
            store["outputs"] = both_batches(relative_order(x1, 1, "row"), relative_order(x2, 1, "row"), core)
            got.append(store["outputs"])
        return got

    scanned1 = scan_back(1, gbranch1, norm1, gate1, ssd1, state1, made1, beside1)
    grad_full1, share_a1, share_b1 = reduce_back(
        scanned1, normed1, scale1, x1, g_out1, weights_a1, weights_b1, beside1
    )
    store["chunk"] = functools.reduce(lambda u, v: u + v.astype(F32), received[1], parts1[0].astype(F32)).astype(BF16)
    store["state"] = state_part(share_a1)
    g_in1, g_out0, norm0 = leave[1](row_id, grad_full1, x1, scale1, params[1], g_out1, full0)
    gbranch0 = branch_product(core_id, g_out0, *weights_b0[0], *weights_b0[1])
    scanned0 = scan_back(0, gbranch0, norm0, gate0, ssd0, state0, made0, beside0)
    grad_full0, share_a0, share_b0 = reduce_back(
        scanned0, normed0, scale0, layer_in, g_out0, weights_a0, weights_b0, beside0
    )
    g_in0 = leave[0](row_id, grad_full0, layer_in, scale0, params[0], g_out0)
    close(g_in0)
    layer_outputs = store["outputs"]
    input_grads = both_batches(in_order(hold(g_in0)), in_order(g_in1), jnp.where(first, batch_order[0], core))

    small_sums = pick_mine(share_a0[shard + STEPS :], share_a1[shard + STEPS :])
    vec = jnp.concatenate([small_sums[0:8] + small_sums[8:16], small_sums[16:24] + small_sums[24:32]], axis=1)
    vec = vec[:, :conv_width]
    gain_sum = small_sums[TAPS_ROWS : TAPS_ROWS + 8] + small_sums[TAPS_ROWS + 8 :]
    partial_sums = jnp.concatenate([vec[:, inner:], gain_sum], axis=1)
    tiles = partial_sums.shape[1] // LANE
    high, low = split_pair(partial_sums)
    both = jnp.concatenate([high, low], axis=0)
    message = jnp.concatenate([hold(state_part(share_a0))] + [both[:, tile_of(i)] for i in range(tiles)], axis=0)
    summed = direct_sum(message, "col")
    state_sum0, rest_sum = summed[:shard], summed[shard:].reshape(tiles, 16, LANE)
    rest_sum = rest_sum[:, 0:8] + rest_sum[:, 8:16]
    vec_state = jnp.concatenate([rest_sum[i] for i in range(2)], axis=1)
    ggain_in = jnp.concatenate([rest_sum[i] for i in range(2, tiles)], axis=1)
    ggain_in = ggain_in[: -(-width // a_width)].reshape(1, -1)[:, :width]
    d_skip = vec[5, :inner].reshape(heads, inner // heads).sum(axis=1)

    a_low, a_high = settled(share_a0[: shard + STEPS], share_a1[: shard + STEPS])
    s_low, s_high = settled(state_sum0, store["state"])
    b_low, b_high = settled(share_b0, share_b1)
    d_value = jnp.concatenate([a_low[:shard, :half], a_high[:shard, :half]], axis=1)
    d_state = jnp.concatenate([s_low, s_high], axis=1)
    d_step = a_low[shard : shard + heads, :shard].T
    d_gate = jnp.concatenate([b_low[:, :half], b_high[:, :half]], axis=1)
    d_out = jnp.concatenate([b_low[:, half:], b_high[:, half:]], axis=1).T

    return (
        layer_outputs[None],
        input_grads[None],
        ggain_in,
        d_gate[None],
        d_value[None],
        d_step[None],
        d_state[None],
        vec[None, 0:4, :inner],
        vec[4:5, :inner],
        vec_state[None, 0:4],
        vec_state[4:5],
        vec[7:8, :heads],
        vec[7:8, LANE : LANE + heads],
        d_skip[None],
        vec[6:7, :inner],
        d_out[None],
    )


def solution(mesh):
    in_specs = (
        P(None, "row", None),
        P(None, "row", None),
        P(None, "row"),
        P(),
        P("pipe", None),
        P("pipe", "row", "col"),
        P("pipe", "row", "col"),
        P("pipe", "row", "col"),
        P("pipe", "row", None),
        P("pipe", None, "col"),
        P("pipe", "col"),
        P("pipe", None, None),
        P("pipe", None),
        P("pipe", "col"),
        P("pipe", "col"),
        P("pipe", "col"),
        P("pipe", "col"),
        P("pipe", "col", "row"),
    )
    out_specs = (
        P("pipe", None, "row", None),
        P("pipe", None, "row", None),
        P("pipe", None),
        P("pipe", "row", "col"),
        P("pipe", "row", "col"),
        P("pipe", "row", "col"),
        P("pipe", "row", None),
        P("pipe", None, "col"),
        P("pipe", "col"),
        P("pipe", None, None),
        P("pipe", None),
        P("pipe", "col"),
        P("pipe", "col"),
        P("pipe", "col"),
        P("pipe", "col"),
        P("pipe", "col", "row"),
    )
    return jax.shard_map(local, mesh=mesh, in_specs=in_specs, out_specs=out_specs, check_vma=False)
```

```python
import functools
import math

import jax
import jax.numpy as jnp
from jax import lax
from jax.experimental import pallas as pl
from jax.experimental.pallas import tpu as pltpu
from jax.sharding import PartitionSpec as P

EPSILON = 1e-05
LOG2E = math.log2(math.e)
LANE = 128
F32 = jnp.float32
BF16 = jnp.bfloat16
SMALL_ROWS = 16
LEAD = 16
VMEM_MIB = 16
TAPS_ROWS = 32
SMALL = 48
STEPS = 16
BLOCKS = 4


def dot_nn(a, b):
    return lax.dot_general(a, b, (((1,), (0,)), ((), ())), preferred_element_type=F32)


def dot_nt(a, b):
    return lax.dot_general(a, b, (((1,), (1,)), ((), ())), preferred_element_type=F32)


def dot_tn(a, b):
    return lax.dot_general(a, b, (((0,), (0,)), ((), ())), preferred_element_type=F32)


def dot_exact(a, b):
    return lax.dot_general(
        a, b, (((1,), (0,)), ((), ())), precision=lax.Precision.HIGHEST, preferred_element_type=F32
    )


def sigmoid(v):
    return 1.0 / (1.0 + jnp.exp(-v))


def split_pair(v):
    high = v.astype(BF16)
    return high, (v - high.astype(F32)).astype(BF16)


def on_chip(kernel, out_shapes, scratch=(), far_in=(), far_out=()):
    whole = pl.BlockSpec(memory_space=pltpu.VMEM)
    scalar = pl.BlockSpec(memory_space=pltpu.SMEM)
    single = not isinstance(out_shapes, tuple)
    shapes = (out_shapes,) if single else out_shapes
    shapes = tuple(pltpu.HBM(o.shape, o.dtype) if i in far_out else o for i, o in enumerate(shapes))

    def call(*operands):
        operands = [
            pltpu.with_memory_space_constraint(o, pltpu.HBM) if i in far_in else o for i, o in enumerate(operands)
        ]
        return pl.pallas_call(
            kernel,
            out_shape=shapes[0] if single else shapes,
            in_specs=[scalar if o.dtype == jnp.int32 else whole for o in operands],
            out_specs=whole if single else (whole,) * len(shapes),
            scratch_shapes=scratch,
            compiler_params=pltpu.CompilerParams(vmem_limit_bytes=VMEM_MIB * 1024 * 1024),
        )(*operands)

    return call


def shaped(shape, dtype=F32):
    return jax.ShapeDtypeStruct(shape, dtype)


def tile_of(q):
    return slice(q * LANE, (q + 1) * LANE)


def spread(columns, q, heads_tile, lane_head):
    first = q * heads_tile
    out = columns[:, first : first + 1]
    for i in range(1, heads_tile):
        out = jnp.where(lane_head == i, columns[:, first + i : first + i + 1], out)
    return out


def lane_heads(rows, heads_tile):
    lanes = lax.broadcasted_iota(jnp.int32, (rows, LANE), 1)
    return lanes // (LANE // heads_tile)


def tri_mask(tokens, seg_col, seg_row, transposed):
    first = lax.broadcasted_iota(jnp.int32, (tokens, tokens), 0)
    second = lax.broadcasted_iota(jnp.int32, (tokens, tokens), 1)
    order = first <= second if transposed else first >= second
    return order & (seg_col == seg_row)


def pack_a_kernel(core_ref, value_ref, state_ref, step_ref, keep_ref, give_ref):
    shard, half = value_ref.shape[0], value_ref.shape[1] // 2
    heads = step_ref.shape[1]
    step = jnp.concatenate([step_ref[...].astype(F32), jnp.zeros((shard, LANE - heads), F32)], axis=1).T
    core = core_ref[0]
    for ref, place in ((keep_ref, core), (give_ref, 1 - core)):
        ref[:shard, :half] = value_ref[:, pl.ds(pl.multiple_of(place * half, LANE), half)]
        ref[:shard, half:] = state_ref[:, pl.ds(pl.multiple_of(place * LANE, LANE), LANE)]
        ref[shard:, :] = jnp.zeros((STEPS, ref.shape[1]), BF16)
        ref[shard:, :shard] = step[0:STEPS, :].astype(BF16)


def pack_b_kernel(core_ref, gate_ref, out_ref, keep_ref, give_ref):
    half = gate_ref.shape[1] // 2
    core = core_ref[0]
    for ref, place in ((keep_ref, core), (give_ref, 1 - core)):
        ref[:, :half] = gate_ref[:, pl.ds(pl.multiple_of(place * half, LANE), half)]
        ref[:, half:] = out_ref[pl.ds(pl.multiple_of(place * half, LANE), half), :].astype(F32).T.astype(BF16)


def enter_kernel(
    inner, heads_tile, places, core_ref, x_ref, before_ref, small_ref, aux_ref, *refs,
):
    taps_ref, heads_ref, gain_ref, _ = views(small_ref, places)
    mine, other = refs[:BLOCKS], refs[BLOCKS : 2 * BLOCKS]
    (
        normed_ref, scale_ref, z_ref, conv_ref, value_ref, scaled_ref, bc_ref, step_ref, cum_ref, cumt_ref, lead_ref,
        carry_ref, msg_ref, leadu_ref,
    ) = refs[2 * BLOCKS :]
    tokens, width = x_ref.shape
    half = inner // 2
    conv_width = conv_ref.shape[1]
    for ref, at in ((before_ref, slice(0, LEAD)), (x_ref, slice(LEAD, LEAD + tokens))):
        x = ref[...].astype(F32)
        scale = lax.rsqrt(jnp.mean(x * x, axis=1, keepdims=True) + EPSILON)
        normed_ref[at, :] = (x * scale * gain_ref[0:1, :]).astype(BF16)
    scale_ref[...] = jnp.broadcast_to(scale, scale_ref.shape)
    core = core_ref[0]
    block = width // BLOCKS
    step = None
    for pieces, place in ((mine, core), (other, 1 - core)):
        z = None
        for i in range(BLOCKS):
            normed = normed_ref[:, i * block : (i + 1) * block]
            term = dot_nn(normed, pieces[i][:block, :])
            z = term if z is None else z + term
            if pieces is mine:
                term = dot_nt(normed, pieces[i][block:, :block])
                step = term if step is None else step + term
        z_ref[:, pl.ds(pl.multiple_of(place * half, LANE), half)] = z[:, :half]
        z_ref[:, pl.ds(pl.multiple_of(inner + place * LANE, LANE), LANE)] = z[:, half:]
    z_ref[:, conv_width:] = jnp.zeros((z_ref.shape[0], LANE), F32)
    z_ref[:, conv_width : conv_width + STEPS] = step
    aux = aux_ref[...]
    raw = z_ref[LEAD:, conv_width:] + heads_ref[0:1, :]
    step = jnp.maximum(raw, 0.0) + jnp.log1p(jnp.exp(-jnp.abs(raw)))
    rates = -step * jnp.exp(heads_ref[1:2, :])
    rows = lax.broadcasted_iota(jnp.int32, (tokens, tokens), 0)
    cols = lax.broadcasted_iota(jnp.int32, (tokens, tokens), 1)
    cum = dot_exact((rows >= cols).astype(F32), rates) * LOG2E
    lead = aux[:, 5:6] * jnp.exp2(cum[tokens - 1 : tokens, :] - cum)
    carry = aux[:, 4:5] * jnp.exp2(cum)
    step_ref[...] = step
    cum_ref[...] = cum
    cumt_ref[...] = cum.T
    lead_ref[...] = lead
    carry_ref[...] = carry
    lane_head = lane_heads(tokens, heads_tile)
    for q in range(conv_width // LANE):
        at = tile_of(q)
        acc = taps_ref[4:5, at] + taps_ref[3:4, at] * z_ref[LEAD:, at]
        for j in range(3):
            shifted = z_ref[LEAD - 3 + j : LEAD - 3 + j + tokens, at]
            acc = acc + taps_ref[j : j + 1, at] * (aux[:, j : j + 1] * shifted)
        conv_ref[:, at] = acc
        value = acc * sigmoid(acc)
        if q < inner // LANE:
            value_ref[:, at] = value
            scaled = spread(step, q, heads_tile, lane_head) * value
            scaled_ref[:, at] = scaled.astype(BF16)
            leadu_ref[:, at] = (spread(lead, q, heads_tile, lane_head) * scaled).astype(BF16)
        else:
            bc_ref[:, tile_of(q - inner // LANE)] = value.astype(BF16)
    msg_ref[0:LANE, :] = dot_tn(bc_ref[:, :LANE], leadu_ref[...]).astype(BF16)
    put_through(msg_ref, carry[tokens - 1 : tokens, :], inner, heads_tile)


def enter_first_kernel(
    inner, heads_tile, places, core_ref, x_ref, before_ref, small_ref, seg_ref, seg_before_ref, *refs,
):
    weights, refs = refs[: 2 * BLOCKS], refs[2 * BLOCKS :]
    aux_ref, segt_ref, *made, seg_ext_ref, leadu_ref = refs
    tokens = x_ref.shape[0]
    seg = seg_ref[...]
    seg_ext_ref[0:LEAD, :] = seg_before_ref[...]
    seg_ext_ref[LEAD:, :] = seg
    lanes = lax.broadcasted_iota(jnp.int32, (tokens, LANE), 1)
    flags = jnp.where(lanes == 3, seg, 0.0)
    for j in range(3):
        same = (seg_ext_ref[LEAD - 3 + j : LEAD - 3 + j + tokens, :] == seg).astype(F32)
        flags = jnp.where(lanes == j, same, flags)
    flags = jnp.where(lanes == 4, (seg == seg_ext_ref[LEAD - 1 : LEAD, :]).astype(F32), flags)
    flags = jnp.where(lanes == 5, (seg == seg[tokens - 1 :, :]).astype(F32), flags)
    aux_ref[...] = flags
    segt_ref[...] = seg.T[0:8, :]
    enter_kernel(
        inner, heads_tile, places, core_ref, x_ref, before_ref, small_ref, aux_ref, *weights, *made, leadu_ref
    )


def views(ref, places):
    return tuple(ref.at[:, p] for p in places)


def put_through(msg_ref, last, inner, heads_tile):
    msg_ref[LANE:, :] = jnp.zeros((SMALL_ROWS, inner), BF16)
    lane_row = lane_heads(1, heads_tile)
    for q in range(inner // LANE):
        high, low = split_pair(spread(last, q, heads_tile, lane_row))
        msg_ref[LANE : LANE + 1, tile_of(q)] = high
        msg_ref[LANE + 1 : LANE + 2, tile_of(q)] = low


def wide_kernel(offset, lead, core_ref, a_ref, *refs):
    mine, other = refs[:BLOCKS], refs[BLOCKS : 2 * BLOCKS]
    out_ref = refs[2 * BLOCKS]
    core = core_ref[0]
    half = out_ref.shape[1] // 2
    block = a_ref.shape[1] // BLOCKS
    for pieces, place in ((mine, core), (other, 1 - core)):
        total = None
        for i in range(BLOCKS):
            term = dot_nn(a_ref[lead:, i * block : (i + 1) * block], pieces[i][:, offset : offset + half])
            total = term if total is None else total + term
        out_ref[:, pl.ds(pl.multiple_of(place * half, LANE), half)] = total


def intra_kernel(
    inner, heads_tile, places, scaled_ref, value_ref, bc_ref, cum_ref, cumt_ref, aux_ref, segt_ref, small_ref,
    out_ref,
):
    heads_ref = views(small_ref, places)[1]
    tokens = scaled_ref.shape[0]
    scores = dot_nt(bc_ref[:, LANE:], bc_ref[:, :LANE])
    scores = jnp.where(tri_mask(tokens, aux_ref[:, 3:4], segt_ref[0:1, :], False), scores, 0.0)
    lane_head = lane_heads(tokens, heads_tile)
    lane_row = lane_heads(1, heads_tile)
    for q in range(inner // LANE):
        at = tile_of(q)
        total = spread(heads_ref[2:3, :], q, heads_tile, lane_row) * value_ref[:, at]
        scaled = scaled_ref[:, at]
        for i in range(heads_tile):
            h = q * heads_tile + i
            gap = jnp.minimum(cum_ref[:, h : h + 1] - cumt_ref[h : h + 1, :], 0.0)
            mixed = (jnp.exp2(gap) * scores).astype(BF16)
            total = total + jnp.where(lane_head == i, dot_nn(mixed, scaled), 0.0)
        out_ref[:, at] = total


def enter_states(messages):
    state = None
    for message in reversed(messages):
        own = message[0:LANE, :].astype(F32)
        through = message[LANE : LANE + 1, :].astype(F32) + message[LANE + 1 : LANE + 2, :].astype(F32)
        state = own if state is None else own + through * state
    return state


def gate_kernel(
    inner, heads_tile, places, count, with_grad, core_ref, intra_ref, bc_ref, carry_ref, gate_ref, small_ref, *refs
):
    gain_ref = views(small_ref, places)[3]
    messages = refs[:count]
    mine, other = refs[count : count + BLOCKS], refs[count + BLOCKS : count + 2 * BLOCKS]
    refs = refs[count + 2 * BLOCKS :]
    if with_grad:
        branch_grad_ref, refs = refs[0], refs[1:]
        ssd_ref, state_ref, msg_ref, sums_ref, gated_ref = refs
    else:
        ssd_ref, state_ref, msg_ref, gated_ref = refs
    tokens = intra_ref.shape[0]
    state = enter_states([m[...] for m in messages]).astype(BF16)
    state_ref[...] = state
    inter = dot_nn(bc_ref[:, LANE:], state)
    lane_head = lane_heads(tokens, heads_tile)
    carry = carry_ref[...]
    squares = jnp.zeros((tokens, LANE), F32)
    products = jnp.zeros((tokens, LANE), F32)
    for q in range(inner // LANE):
        at = tile_of(q)
        ssd = intra_ref[:, at] + spread(carry, q, heads_tile, lane_head) * inter[:, at]
        ssd_ref[:, at] = ssd
        gate = gate_ref[:, at]
        gated = ssd * (gate * sigmoid(gate))
        squares = squares + gated * gated
        scaled = gated * gain_ref[0:1, at]
        gated_ref[:, at] = scaled.astype(BF16)
        if with_grad:
            products = products + scaled * branch_grad_ref[:, at]
    half = inner // 2
    core = core_ref[0]
    low = gated_ref[:, pl.ds(pl.multiple_of(core * half, LANE), half)]
    high = gated_ref[:, pl.ds(pl.multiple_of((1 - core) * half, LANE), half)]
    block = mine[0].shape[0]
    for i in range(BLOCKS):
        part = dot_nt(low, mine[i][:, half:]) + dot_nt(high, other[i][:, half:])
        msg_ref[:, i * block : (i + 1) * block] = part.astype(BF16)
    total = jnp.sum(squares, axis=1, keepdims=True)
    lanes = lax.broadcasted_iota(jnp.int32, (tokens, LANE), 1)
    if with_grad:
        packed = jnp.where(lanes == 0, total, 0.0)
        packed = packed + jnp.where(lanes == 1, jnp.sum(products, axis=1, keepdims=True), 0.0)
        sums_ref[...] = packed.T[0:8, :]
    else:
        rest = total - total.astype(BF16).astype(F32)
        packed = jnp.where(lanes == 0, total, jnp.where(lanes == 1, rest, 0.0))
        msg_ref[:, BLOCKS * block :] = packed.astype(BF16)


def ungate_kernel(
    inner, heads_tile, places, norm_width, branch_grad_ref, norm_ref, gate_ref, ssd_ref, small_ref, carry_ref, bc_ref,
    gssd_ref, ggate_ref, branch_ref, msg_ref, ggain_ref, cg_ref,
):
    gain_ref = views(small_ref, places)[3]
    tokens = branch_grad_ref.shape[0]
    rho = norm_ref[:, 0:1]
    pull = norm_ref[:, 1:2] * (rho * rho * rho / norm_width)
    lane_head = lane_heads(tokens, heads_tile)
    carry = carry_ref[...]
    ggain_ref[...] = jnp.zeros(ggain_ref.shape, F32)
    for q in range(inner // LANE):
        at = tile_of(q)
        gate = gate_ref[:, at]
        sig = sigmoid(gate)
        ssd = ssd_ref[:, at]
        gated = ssd * (gate * sig)
        grad = branch_grad_ref[:, at]
        gain = gain_ref[0:1, at]
        normed = gated * rho
        ggain_ref[0:1, at] = jnp.sum(grad * normed, axis=0, keepdims=True)
        branch_ref[:, at] = (normed * gain).astype(BF16)
        ggated = rho * (gain * grad) - gated * pull
        gssd = ggated * (gate * sig)
        gssd_ref[:, at] = gssd
        ggate_ref[:, at] = (ggated * ssd * (sig * (1.0 + gate * (1.0 - sig)))).astype(BF16)
        cg_ref[:, at] = (spread(carry, q, heads_tile, lane_head) * gssd).astype(BF16)
    msg_ref[0:LANE, :] = dot_tn(bc_ref[:, LANE:], cg_ref[...]).astype(BF16)
    put_through(msg_ref, carry[tokens - 1 : tokens, :], inner, heads_tile)


def intra_grad_kernel(
    inner, heads_tile, scaled_ref, gssd_ref, bc_ref, cum_ref, cumt_ref, aux_ref, segt_ref,
    gscaled_ref, gbc_ref, gcum_ref, sums_ref,
):
    tokens = scaled_ref.shape[0]
    mask = tri_mask(tokens, aux_ref[:, 3:4], segt_ref[0:1, :], True)
    scores = jnp.where(mask, dot_nt(bc_ref[:, :LANE], bc_ref[:, LANE:]), 0.0)
    lane_head = lane_heads(tokens, heads_tile)
    gscores = jnp.zeros((tokens, tokens), F32)
    gcum_ref[...] = jnp.zeros(gcum_ref.shape, F32)
    sums_ref[...] = jnp.zeros(sums_ref.shape, F32)
    for q in range(inner // LANE):
        at = tile_of(q)
        grad = gssd_ref[:, at].astype(BF16)
        scaled = scaled_ref[:, at]
        total = jnp.zeros((tokens, LANE), F32)
        for i in range(heads_tile):
            h = q * heads_tile + i
            gap = jnp.minimum(cumt_ref[h : h + 1, :] - cum_ref[:, h : h + 1], 0.0)
            decay = jnp.exp2(gap)
            mixed = decay * scores
            picked = jnp.where(lane_head == i, scaled, jnp.zeros_like(scaled))
            gmixed = dot_nt(picked, grad)
            total = total + jnp.where(lane_head == i, dot_nn(mixed.astype(BF16), grad), 0.0)
            product = gmixed * mixed
            sums_ref[h : h + 1, :] = jnp.sum(product, axis=0, keepdims=True)
            gcum_ref[:, h : h + 1] = -jnp.sum(product, axis=1, keepdims=True)
            gscores = gscores + gmixed * decay
        gscaled_ref[:, at] = total
    gscores = jnp.where(mask, gscores, 0.0)
    gbc_ref[:, :LANE] = dot_nn(gscores.astype(BF16), bc_ref[:, LANE:])
    gbc_ref[:, LANE:] = dot_nn(gscores.T.astype(BF16), bc_ref[:, :LANE])
    gcum_ref[...] = gcum_ref[...] + sums_ref[...].T


def inter_grad_kernel(
    inner, heads_tile, places, count, state_ref, scaled_ref, value_ref, gssd_ref, gscaled_ref, bc_ref, gbc_ref, gcum_ref,
    step_ref, lead_ref, carry_ref, z_ref, conv_ref, aux_ref, small_ref, ggain_ref, *refs,
):
    taps_ref, heads_ref, _, _ = views(small_ref, places)
    messages = refs[:count]
    gpre_ref, gstep_ref, gtaps_ref, em_ref, leadu_ref, cg_ref, gain_ref, lose_ref, gsize_ref = refs[count:]
    tokens = scaled_ref.shape[0]
    width = conv_ref.shape[1]
    aux = aux_ref[...]
    adjoint = enter_states([m[...] for m in messages])
    adjoint_low = adjoint.astype(BF16)
    state = state_ref[...]
    from_adjoint = dot_nn(bc_ref[:, :LANE], adjoint_low)
    from_state = dot_nn(bc_ref[:, LANE:], state)
    overlap = jnp.sum(adjoint * state.astype(F32), axis=0, keepdims=True)
    lane_head = lane_heads(tokens, heads_tile)
    lane_row = lane_heads(1, heads_tile)
    step = step_ref[...]
    lead = lead_ref[...]
    carry = carry_ref[...]
    em_ref[0:8, :] = jnp.zeros((8, LANE), F32)
    em_ref[8 + tokens :, :] = jnp.zeros((8, LANE), F32)
    gpre_ref[0:8, :] = jnp.zeros((8, width), F32)
    gtaps_ref[...] = jnp.zeros(gtaps_ref.shape, F32)

    def through_conv(q, grad):
        at = tile_of(q)
        conv = conv_ref[:, at]
        sig = sigmoid(conv)
        e = grad * (sig * (1.0 + conv * (1.0 - sig)))
        gtaps_ref[4:5, at] = jnp.sum(e, axis=0, keepdims=True)
        gtaps_ref[3:4, at] = jnp.sum(e * z_ref[LEAD:, at], axis=0, keepdims=True)
        total = None
        for j in range(3):
            masked = aux[:, j : j + 1] * e
            shifted = z_ref[LEAD - 3 + j : LEAD - 3 + j + tokens, at]
            gtaps_ref[j : j + 1, at] = jnp.sum(masked * shifted, axis=0, keepdims=True)
            em_ref[8 : 8 + tokens, :] = masked
            term = taps_ref[j : j + 1, at] * em_ref[3 - j : 11 - j + tokens, :]
            total = term if total is None else total + term
        gpre_ref[8:LEAD, at] = total[0:8, :]
        gpre_ref[LEAD:, at] = total[8:, :] + taps_ref[3:4, at] * e

    for q in range(inner // LANE):
        at = tile_of(q)
        scaled = scaled_ref[:, at].astype(F32)
        grad = gssd_ref[:, at]
        value = value_ref[:, at]
        leads = spread(lead, q, heads_tile, lane_head)
        carries = spread(carry, q, heads_tile, lane_head)
        pushed = leads * from_adjoint[:, at]
        gscaled = gscaled_ref[:, at] + pushed
        carried = carries * grad
        leadu_ref[:, at] = (leads * scaled).astype(BF16)
        cg_ref[:, at] = carried.astype(BF16)
        gain_ref[:, at] = (carried * from_state[:, at]).astype(BF16)
        lose_ref[:, at] = (scaled * pushed).astype(BF16)
        gsize_ref[:, at] = (gscaled * value).astype(BF16)
        gtaps_ref[5:6, at] = jnp.sum(grad * value, axis=0, keepdims=True)
        gvalue = spread(step, q, heads_tile, lane_head) * gscaled
        gvalue = gvalue + spread(heads_ref[2:3, :], q, heads_tile, lane_row) * grad
        through_conv(q, gvalue)
    gb = gbc_ref[:, :LANE] + dot_nt(leadu_ref[...], adjoint_low)
    gc = gbc_ref[:, LANE:] + dot_nt(cg_ref[...], state)
    through_conv(inner // LANE, gb)
    through_conv(inner // LANE + 1, gc)
    head_of = lax.broadcasted_iota(jnp.int32, (inner, LANE), 0) // (LANE // heads_tile)
    pick = (head_of == lax.broadcasted_iota(jnp.int32, (inner, LANE), 1)).astype(BF16)
    lose = dot_nn(lose_ref[...], pick)
    gcum = gcum_ref[...] + dot_nn(gain_ref[...], pick) - lose
    high, low = split_pair(overlap)
    ends = dot_nn(jnp.broadcast_to(high, (8, inner)), pick) + dot_nn(jnp.broadcast_to(low, (8, inner)), pick)
    last = carry[tokens - 1 : tokens, :] * ends[0:1, :] + jnp.sum(lose, axis=0, keepdims=True)
    row_of = lax.broadcasted_iota(jnp.int32, (tokens, LANE), 0)
    gcum = gcum + jnp.where(row_of == tokens - 1, last, 0.0)
    rows = lax.broadcasted_iota(jnp.int32, (tokens, tokens), 0)
    cols = lax.broadcasted_iota(jnp.int32, (tokens, tokens), 1)
    grate = dot_exact((rows <= cols).astype(F32), gcum)
    speed = jnp.exp(heads_ref[1:2, :])
    gsize = dot_nn(gsize_ref[...], pick) - speed * grate
    raw = z_ref[LEAD:, width:] + heads_ref[0:1, :]
    graw = gsize * sigmoid(raw)
    gstep_ref[...] = graw.astype(BF16)
    gtaps_ref[6:7, :inner] = ggain_ref[0:1, :]
    gtaps_ref[7:8, 0:LANE] = jnp.sum(graw, axis=0, keepdims=True)
    gtaps_ref[7:8, LANE : 2 * LANE] = jnp.sum(grate * (-speed * step), axis=0, keepdims=True)


def give_b_kernel(
    core_ref, ggate_ref, normed_ref, g_out_ref, branch_ref,
    other_b_ref, gg_mine_ref, gg_other_ref, normed_t_ref, g_out_t_ref,
):
    width = g_out_ref.shape[1]
    half = ggate_ref.shape[1] // 2
    core = core_ref[0]
    gg_mine_ref[...] = ggate_ref[:, pl.ds(pl.multiple_of(core * half, LANE), half)]
    gg_other_ref[...] = ggate_ref[:, pl.ds(pl.multiple_of((1 - core) * half, LANE), half)]
    block = width // BLOCKS
    for i in range(BLOCKS):
        at = slice(i * block, (i + 1) * block)
        normed_t_ref[at, :] = normed_ref[LEAD:, at].astype(F32).T.astype(BF16)
        g_out_t_ref[at, :] = g_out_ref[:, at].astype(F32).T.astype(BF16)
    other_b_ref[:, :half] = dot_nn(normed_t_ref[...], gg_other_ref[...]).astype(BF16)
    branch = branch_ref[:, pl.ds(pl.multiple_of((1 - core) * half, LANE), half)]
    other_b_ref[:, half:] = dot_nn(g_out_t_ref[...], branch).astype(BF16)


def keep_b_kernel(core_ref, normed_t_ref, g_out_t_ref, branch_ref, gg_mine_ref, their_ref, *refs):
    size = normed_t_ref.shape[0] // len(refs)
    half = gg_mine_ref.shape[1]
    branch = branch_ref[:, pl.ds(pl.multiple_of(core_ref[0] * half, LANE), half)]
    for i, ref in enumerate(refs):
        at = slice(i * size, (i + 1) * size)
        part = dot_nn(normed_t_ref[at, :], gg_mine_ref[...]) + their_ref[at, :half].astype(F32)
        ref[:, :half] = part.astype(BF16)
        part = dot_nn(g_out_t_ref[at, :], branch) + their_ref[at, half:].astype(F32)
        ref[:, half:] = part.astype(BF16)


def taps_rows(taps, wide):
    left, right = taps[:, :wide], taps[:, wide:]
    rows = []
    for part in (left, right):
        high = part.astype(BF16).astype(F32)
        rows += [high, part - high]
    return jnp.concatenate(rows, axis=0).astype(BF16)


def gain_rows(gain, wide):
    high = gain.astype(BF16).astype(F32)
    index = lax.broadcasted_iota(jnp.int32, (16, wide), 0)
    out = jnp.zeros((16, wide), F32)
    count = -(-gain.shape[1] // wide)
    for i in range(count):
        for base, part in ((0, high), (8, gain - high)):
            piece = part[:, i * wide : (i + 1) * wide]
            if piece.shape[1] < wide:
                piece = jnp.concatenate([piece, jnp.zeros((1, wide - piece.shape[1]), F32)], axis=1)
            out = jnp.where(index == base + i, piece, out)
    return out.astype(BF16)


def give_a_kernel(
    core_ref, gpre_ref, next_ref, gstep_ref, normed_t_ref, gtaps_ref, other_a_ref, ga_mine_ref, ga_other_ref, glow_ref
):
    tokens, width = glow_ref.shape
    inner = width - 2 * LANE
    half = inner // 2
    core = core_ref[0]
    cut = tokens - LEAD
    glow_ref[:cut, :] = gpre_ref[LEAD : LEAD + cut, :].astype(BF16)
    glow_ref[cut:, :] = (gpre_ref[LEAD + cut :, :] + next_ref[...]).astype(BF16)
    for ga_ref, place in ((ga_mine_ref, core), (ga_other_ref, 1 - core)):
        ga_ref[:, :half] = glow_ref[:, pl.ds(pl.multiple_of(place * half, LANE), half)]
        ga_ref[:, half:] = glow_ref[:, pl.ds(pl.multiple_of(inner + place * LANE, LANE), LANE)]
    rows, wide = normed_t_ref.shape[0], other_a_ref.shape[1]
    other_a_ref[:rows, :] = dot_nn(normed_t_ref[...], ga_other_ref[...]).astype(BF16)
    steps = step_grads(gstep_ref, normed_t_ref)
    for i in range(rows // wide):
        other_a_ref[rows + STEPS * i : rows + STEPS * (i + 1), :] = steps[:, i * wide : (i + 1) * wide].astype(BF16)
    other_a_ref[rows + STEPS * (rows // wide) :, :] = taps_rows(gtaps_ref[...], wide)


def step_grads(gstep_ref, normed_t_ref):
    return dot_nt(gstep_ref[...].astype(F32).T[0:STEPS, :].astype(BF16), normed_t_ref[...])


def keep_a_kernel(normed_t_ref, ga_mine_ref, gstep_ref, their_ref, gtaps_ref, ggain_ref, *refs):
    rows = normed_t_ref.shape[0]
    size = rows // len(refs)
    wide = ga_mine_ref.shape[1]
    groups = [
        their_ref[rows + STEPS * i : rows + STEPS * (i + 1), :].astype(F32) for i in range(rows // wide + TAPS_ROWS // STEPS)
    ]
    steps = step_grads(gstep_ref, normed_t_ref) + jnp.concatenate(groups[: rows // wide], axis=1)
    taps = jnp.concatenate([t[0:8] + t[8:16] for t in groups[rows // wide :]], axis=1)[:, : gtaps_ref.shape[1]]
    small = taps_rows(taps + gtaps_ref[...], wide)
    gain = gain_rows(ggain_ref[0:1, :], wide)
    below = size + STEPS
    for i, ref in enumerate(refs):
        at = slice(i * size, (i + 1) * size)
        ref[:size, :] = (dot_nn(normed_t_ref[at, :], ga_mine_ref[...]) + their_ref[at, :].astype(F32)).astype(BF16)
        ref[size:below, :] = jnp.zeros((STEPS, wide), BF16)
        ref[size:below, :size] = steps[:, at].astype(BF16)
        ref[below : below + TAPS_ROWS, :] = small
        ref[below + TAPS_ROWS :, :] = gain


def pull_kernel(ga_mine_ref, ga_other_ref, gstep_ref, gg_mine_ref, gg_other_ref, x_ref, scale_ref, *refs):
    mine_a, other_a, mine_b, other_b = (refs[i * BLOCKS : (i + 1) * BLOCKS] for i in range(4))
    msg_ref, ggain_ref = refs[4 * BLOCKS :]
    half = gg_mine_ref.shape[1]
    block = mine_b[0].shape[0]
    scale = scale_ref[:, 0:1]
    ggain_ref[...] = jnp.zeros(ggain_ref.shape, F32)
    for i in range(BLOCKS):
        at = slice(i * block, (i + 1) * block)
        part = dot_nt(ga_mine_ref[...], mine_a[i][:block, :])
        part = part + dot_nt(ga_other_ref[...], other_a[i][:block, :])
        part = part + dot_nn(gstep_ref[:, :STEPS], mine_a[i][block:, :block])
        part = part + dot_nt(gg_mine_ref[...], mine_b[i][:, :half])
        part = part + dot_nt(gg_other_ref[...], other_b[i][:, :half])
        msg_ref[:, at] = part.astype(BF16)
        ggain_ref[0:1, at] = jnp.sum(part * (x_ref[:, at].astype(F32) * scale), axis=0, keepdims=True)


def leave_kernel(norm_width, places, below, ordered, ids_ref, full_ref, x_ref, scale_ref, small_ref, g_out_ref, *refs):
    gain_ref = views(small_ref, places)[2]
    tokens, width = x_ref.shape
    scale = scale_ref[:, 0:1]
    x = x_ref[...].astype(F32)
    pulled = full_ref[...].astype(F32) * gain_ref[0:1, :]
    slope = jnp.sum(pulled * x, axis=1, keepdims=True) * (scale * scale * scale / width)
    grad = g_out_ref[...].astype(F32) + scale * pulled - x * slope
    core = ids_ref[0]

    def put(ref):
        put_blocks(ordered, ids_ref[1], ref, slice(None), grad)

    if below:
        raw_ref, grad_ref, low_ref, norm_ref = refs
        put(grad_ref)
        low = grad.astype(BF16)
        low_ref[...] = low
        dots = jnp.sum(low.astype(F32) * raw_ref[:, :width].astype(F32), axis=1, keepdims=True)
        squares = raw_ref[:, width : width + 1].astype(F32) + raw_ref[:, width + 1 : width + 2].astype(F32)
        lanes = lax.broadcasted_iota(jnp.int32, (tokens, LANE), 1)
        norm_ref[...] = jnp.where(lanes == 0, lax.rsqrt(squares / norm_width + EPSILON), dots)
        return
    above_ref, mine_ref, give_ref = refs

    @pl.when(core == 0)
    def _():
        put(mine_ref)
        give_ref[...] = above_ref[...]

    @pl.when(core != 0)
    def _():
        put(give_ref)
        mine_ref[...] = above_ref[...]


def put_blocks(ordered, row, ref, at, value):
    block = value.shape[1] // BLOCKS
    for i in range(BLOCKS):
        part = value[:, i * block : (i + 1) * block]
        if ordered:
            ref[at, pl.ds(pl.multiple_of((row ^ i) * block, LANE), block)] = part
        else:
            ref[at, i * block : (i + 1) * block] = part


def outputs_kernel(ordered, ids_ref, x_ref, norm_ref, *refs):
    chunks, (mine_ref, give_ref) = refs[:-2], refs[-2:]
    size = chunks[0].shape[0]
    for b, chunk in enumerate(chunks):
        at = pl.ds(pl.multiple_of((ids_ref[2] ^ b) * size, size), size)
        below = x_ref[at, :]
        above = (below.astype(F32) + norm_ref[at, 0:1] * chunk[...].astype(F32)).astype(BF16)
        for first, second, chosen in ((mine_ref, give_ref, 0), (give_ref, mine_ref, 1)):

            @pl.when(ids_ref[0] == chosen)
            def _():
                put_blocks(ordered, ids_ref[1], first, at, below)
                put_blocks(ordered, ids_ref[1], second, at, above)


def stack_kernel(place_ref, mine_ref, their_ref, out_ref):
    out_ref[place_ref[0]] = mine_ref[...]
    out_ref[1 - place_ref[0]] = their_ref[...]


def sum_kernel(inner, states, heads_tile, ids_ref, share_a_ref, share_b_ref, *refs):
    mine_a_ref, give_a_ref, mine_b_ref, give_b_ref, msg_ref, taps_ref, bias_ref, gain_ref, heads_ref = refs[-9:]
    pieces = refs[:-9]
    count = len(pieces) // 2
    a = functools.reduce(lambda u, v: u + v, [p[...].astype(F32) for p in pieces[:count]])
    b = functools.reduce(lambda u, v: u + v, [p[...].astype(F32) for p in pieces[count:]])
    shard = mine_b_ref.shape[0]
    half = inner // 2
    below = shard + STEPS
    msg_ref[:shard, :] = a[:shard, half:].astype(BF16)

    def small(part):
        vec = jnp.concatenate([part[0:8] + part[8:16], part[16:24] + part[24:32]], axis=1)
        taps_ref[...] = vec[0:4, :inner]
        bias_ref[...] = vec[4:5, :inner]
        gain_ref[...] = vec[6:7, :inner]
        head_of = lax.broadcasted_iota(jnp.int32, (inner, LANE), 0) // (LANE // heads_tile)
        pick = (head_of == lax.broadcasted_iota(jnp.int32, (inner, LANE), 1)).astype(F32)
        heads_ref[0:1, :] = vec[7:8, 0:LANE]
        heads_ref[1:2, :] = vec[7:8, LANE : 2 * LANE]
        heads_ref[2:8, :] = dot_exact(vec[:, :inner], pick)[2:8, :]
        rest = jnp.concatenate(
            [vec[:, inner : inner + 2 * states], part[TAPS_ROWS : TAPS_ROWS + 8] + part[TAPS_ROWS + 8 :]], axis=1
        )
        high = rest.astype(BF16).astype(F32)
        both = jnp.concatenate([high, rest - high], axis=0).astype(BF16)
        for i in range(rest.shape[1] // LANE):
            msg_ref[shard + 16 * i : shard + 16 * (i + 1), :] = both[:, tile_of(i)]

    @pl.when(ids_ref[0] == 0)
    def _():
        mine_a_ref[...] = a[:below].astype(BF16)
        give_a_ref[...] = share_a_ref[:below, :].astype(BF16)
        mine_b_ref[...] = b.astype(BF16)
        give_b_ref[...] = share_b_ref[...].astype(BF16)
        small(a[below:])

    @pl.when(ids_ref[0] != 0)
    def _():
        mine_a_ref[...] = share_a_ref[:below, :].astype(BF16)
        give_a_ref[...] = a[:below].astype(BF16)
        mine_b_ref[...] = share_b_ref[...].astype(BF16)
        give_b_ref[...] = b.astype(BF16)
        small(share_a_ref[below:, :])


def col_kernel(states, ids_ref, state_ref, *refs):
    mine_ref, give_ref, taps_ref, bias_ref, gain_ref = refs[-5:]
    parts = [r[...].astype(F32) for r in refs[:-5]]
    while len(parts) > 1:
        parts = [parts[i] + parts[i + 1] for i in range(0, len(parts), 2)]
    shard = mine_ref.shape[0]
    own, rest = parts[0][:shard].astype(BF16), parts[0][shard:]
    tiles = [rest[16 * i : 16 * i + 8] + rest[16 * i + 8 : 16 * (i + 1)] for i in range(rest.shape[0] // 16)]
    count = 2 * states // LANE
    for i in range(count):
        taps_ref[:, tile_of(i)] = tiles[i][0:4]
        bias_ref[:, tile_of(i)] = tiles[i][4:5]
    wide = len(tiles) - count
    for i in range(gain_ref.shape[1] // LANE):
        gain_ref[:, tile_of(i)] = tiles[count + i % wide][i // wide : i // wide + 1]
    for first, second, chosen in ((mine_ref, give_ref, 0), (give_ref, mine_ref, 1)):

        @pl.when(ids_ref[0] == chosen)
        def _():
            first[...] = own
            second[...] = state_ref[...].astype(BF16)


def join_kernel(ids_ref, mine_a_ref, their_a_ref, mine_b_ref, their_b_ref, value_ref, step_ref, gate_ref, out_ref):
    shard, half = value_ref.shape[0], value_ref.shape[1] // 2
    core = ids_ref[0]
    for a_ref, b_ref, place in ((mine_a_ref, mine_b_ref, core), (their_a_ref, their_b_ref, 1 - core)):
        at = pl.ds(pl.multiple_of(place * half, LANE), half)
        value_ref[:, at] = a_ref[:shard, :half].astype(F32)
        gate_ref[:, at] = b_ref[:, :half].astype(F32)
        out_ref[at, :] = b_ref[:, half:].astype(F32).T
    step_ref[...] = mine_a_ref[shard:, :shard].astype(F32).T[:, : step_ref.shape[1]]


def permute(block, axis, route):
    return lax.ppermute(block, axis, route)


def from_before(block, count, distance):
    return permute(block, "row", [(i, i + distance) for i in range(count - distance)])


def from_after(block, count, distance):
    return permute(block, "row", [(i + distance, i) for i in range(count - distance)])


def swapped(block):
    return permute(block, "pipe", [(0, 1), (1, 0)])


def exchanged(blocks, axis):
    return lax.all_to_all(blocks, axis, 0, 0)


def spread_out(block, axis):
    count = lax.axis_size(axis)
    return exchanged(jnp.broadcast_to(block[None], (count,) + block.shape), axis).reshape(
        (count * block.shape[0],) + block.shape[1:]
    )


def parts_sum(block, axis):
    count = lax.axis_size(axis)
    parts = exchanged(block.reshape((count, block.shape[0] // count) + block.shape[1:]), axis)
    return jnp.sum(parts.astype(F32), axis=0)


def direct_sum(block, axis):
    parts = [block] + [sent_to(block, axis, b) for b in range(1, lax.axis_size(axis))]
    parts = [p.astype(F32) for p in parts]
    while len(parts) > 1:
        parts = [parts[i] + parts[i + 1] for i in range(0, len(parts), 2)]
    return parts[0]


def sent_to(block, axis, flip):
    count = lax.axis_size(axis)
    return permute(block, axis, [(i, i ^ flip) for i in range(count)])


def relative_order(block, dim, axis, place=None):
    count = lax.axis_size(axis)
    size = block.shape[dim] // count
    place = lax.axis_index(axis) if place is None else place
    return jnp.concatenate(
        [lax.dynamic_slice_in_dim(block, (place ^ b) * size, size, dim) for b in range(count)], axis=dim
    )


class Phases:
    def __init__(self, token):
        self.token = token

    def hold(self, value):
        return lax.optimization_barrier((value, self.token))[0]

    def close(self, *values):
        self.token = lax.optimization_barrier((self.token,) + tuple(jax.tree.leaves(values)))[0]


def col_gather(block):
    return lax.all_gather(block, "col", axis=0, tiled=True)


def after(block, *others):
    return lax.optimization_barrier((block,) + others)[0]


def local(
    inputs, cotangent, segment_ids, batch_order, norm_gain, gate_proj, value_proj, step_proj, state_proj,
    conv_value, conv_value_bias, conv_state, conv_state_bias, step_bias, decay_log, skip_gain, gate_gain, out_proj,
):
    core = lax.axis_index("pipe")
    first = core == 0
    core_id = core.reshape(1).astype(jnp.int32)
    rows = lax.axis_size("row")
    row = lax.axis_index("row")
    tokens, width = inputs.shape[1], inputs.shape[2]
    inner = gate_proj.shape[2]
    heads = step_proj.shape[2]
    states = state_proj.shape[2] // 2
    heads_tile = LANE // (inner // heads)
    half = inner // 2
    conv_width = inner + 2 * states
    norm_width = inner * lax.axis_size("col")
    reach = max(rows // 2, 1)
    distances = range(1, reach + 1)
    group = rows // BLOCKS

    def pick_mine(a, b):
        return jnp.where(first, a, b)

    phases = Phases(core_id)
    hold, close = phases.hold, phases.close

    shard = gate_proj.shape[1]
    a_width, b_width = half + states, inner
    own_a, away_a = on_chip(pack_a_kernel, (shaped((shard + STEPS, a_width), BF16),) * 2, far_in=(1, 2, 3))(
        core_id, value_proj[0], state_proj[0], step_proj[0]
    )
    close(away_a)
    take_a = swapped(hold(away_a))
    own_b, away_b = on_chip(pack_b_kernel, (shaped((shard, b_width), BF16),) * 2, far_in=(1, 2))(core_id, hold(gate_proj[0]), out_proj[0])
    close(take_a, away_b)

    def blocks_of(pieces):
        if pieces[0].shape[0] > shard and group > 1:
            made = []
            for i in range(BLOCKS):
                part = pieces[i * group : (i + 1) * group]
                steps = jnp.concatenate([p[shard:, :shard] for p in part], axis=1)
                steps = jnp.pad(steps, ((0, 0), (0, a_width - steps.shape[1])))
                made.append(jnp.concatenate([p[:shard] for p in part] + [steps], axis=0))
            return made
        return [jnp.concatenate(pieces[i * group : (i + 1) * group], axis=0) for i in range(BLOCKS)]

    near = 3 if rows == BLOCKS else rows

    def sent_near(block):
        return [block] + [sent_to(block, "row", b) for b in range(1, near)]

    def passed_on(pieces):
        if rows != BLOCKS:
            return []
        cut = -(-pieces[0].shape[0] // 32) * 16
        return [jnp.concatenate([sent_to(pieces[1][:cut], "row", 2), sent_to(pieces[2][cut:], "row", 1)], axis=0)]

    def both_cores(mine):
        return mine, [swapped(p) for p in mine]

    piece_a0 = hold(pick_mine(own_a, take_a))
    pieces_a0 = sent_near(piece_a0)
    take_b = swapped(hold(away_b))
    piece_b0 = pick_mine(own_b, take_b)

    taps_own = jnp.concatenate(
        [
            jnp.concatenate([hold(conv_value[0]), conv_state[0]], axis=1),
            jnp.concatenate([conv_value_bias, conv_state_bias], axis=1),
            jnp.zeros((3, conv_width), F32),
        ],
        axis=0,
    )
    heads_own = jnp.pad(jnp.concatenate([hold(step_bias), decay_log, skip_gain], axis=0), ((0, 5), (0, LANE - heads)))
    gains_own = jnp.concatenate([relative_order(hold(norm_gain), 1, "row"), gate_gain], axis=1)
    gains_own = jnp.pad(gains_own, ((0, 7), (0, 0)))
    small = jnp.concatenate([taps_own, heads_own, gains_own], axis=1)
    small_other = swapped(small)
    params = (pick_mine(small, small_other), pick_mine(small_other, small))
    places = (slice(0, conv_width), slice(conv_width, conv_width + LANE))
    places += (slice(conv_width + LANE, conv_width + LANE + width), slice(conv_width + LANE + width, small.shape[1]))

    source = hold(batch_order)[core]
    layer_in = relative_order(inputs[source], 1, "row")
    seg = jnp.broadcast_to(segment_ids[source].astype(F32)[:, None], (tokens, LANE))
    sent_rows = jnp.concatenate([layer_in[tokens - LEAD :], seg[tokens - LEAD :].astype(BF16)], axis=1)
    got_rows = from_before(sent_rows, rows, 1)
    other_order = row ^ jnp.maximum(row - 1, 0)
    before0 = relative_order(got_rows[:, :width], 1, "row", other_order)
    seg_before = jnp.where(row == 0, -1.0, got_rows[:, width:].astype(F32))
    g_out1 = relative_order(hold(cotangent)[core], 1, "row")
    close(pieces_a0, piece_b0, params, layer_in, seg, before0, seg_before, g_out1)

    long = tokens + LEAD
    message_shape = shaped((states + SMALL_ROWS, inner), BF16)
    entered = (
        shaped((long, width), BF16), shaped((tokens, LANE)), shaped((long, conv_width + LANE)),
        shaped((tokens, conv_width)), shaped((tokens, inner)), shaped((tokens, inner), BF16),
        shaped((tokens, 2 * states), BF16), shaped((tokens, LANE)), shaped((tokens, LANE)), shaped((LANE, tokens)),
        shaped((tokens, LANE)), shaped((tokens, LANE)), message_shape,
    )
    enter = [
        on_chip(
            functools.partial(enter_first_kernel, inner, heads_tile, places),
            (shaped((tokens, LANE)), shaped((8, tokens))) + entered,
            [pltpu.VMEM((long, LANE), F32), pltpu.VMEM((tokens, inner), BF16)],
        ),
        on_chip(
            functools.partial(enter_kernel, inner, heads_tile, places), entered, [pltpu.VMEM((tokens, inner), BF16)]
        ),
    ]
    intra = on_chip(functools.partial(intra_kernel, inner, heads_tile, places), shaped((tokens, inner)))
    gate_product = on_chip(functools.partial(wide_kernel, 0, LEAD), shaped((tokens, inner)))
    branch_product = on_chip(functools.partial(wide_kernel, half, 0), shaped((tokens, inner)))
    gates = [
        on_chip(
            functools.partial(gate_kernel, inner, heads_tile, places, reach, with_grad),
            (shaped((tokens, inner)), shaped((states, inner), BF16))
            + ((shaped((tokens, width), BF16), shaped((8, tokens))) if with_grad else (shaped((tokens, width + LANE), BF16),)),
            [pltpu.VMEM((tokens, inner), BF16)],
        )
        for with_grad in (False, True)
    ]
    ungates = [on_chip(
        functools.partial(ungate_kernel, inner, heads_tile, places, norm_width),
        (
            shaped((tokens, inner)), shaped((tokens, inner), BF16), shaped((tokens, inner), BF16), message_shape,
            shaped((8, inner)),
        ),
        [pltpu.VMEM((tokens, inner), BF16)],
        far_in=far,
    ) for far in ((), (0, 2, 3, 4, 5, 6))]
    intra_grad = on_chip(
        functools.partial(intra_grad_kernel, inner, heads_tile),
        (shaped((tokens, inner)), shaped((tokens, 2 * states)), shaped((tokens, LANE))),
        [pltpu.VMEM((LANE, tokens), F32)],
    )
    inter_grad = on_chip(
        functools.partial(inter_grad_kernel, inner, heads_tile, places, reach),
        (shaped((long, conv_width)), shaped((tokens, LANE), BF16), shaped((8, conv_width))),
        [pltpu.VMEM((tokens + 16, LANE), F32)] + [pltpu.VMEM((tokens, inner), BF16)] * 5,
    )
    pull = on_chip(pull_kernel, (shaped((tokens, width), BF16), shaped((8, width))))
    weight_t = shaped((width, tokens), BF16)
    give_a = on_chip(
        give_a_kernel,
        (shaped((width + STEPS * (width // a_width) + TAPS_ROWS, a_width), BF16),) + (shaped((tokens, a_width), BF16),) * 2,
        [pltpu.VMEM((tokens, conv_width), BF16)],
    )
    give_b = on_chip(
        give_b_kernel,
        (shaped((width, b_width), BF16), shaped((tokens, half), BF16), shaped((tokens, half), BF16), weight_t, weight_t),
    )
    keep_a = on_chip(keep_a_kernel, (shaped((shard + STEPS + SMALL, a_width), BF16),) * rows, far_out=range(1, rows))
    keep_b = on_chip(keep_b_kernel, (shaped((shard, b_width), BF16),) * rows, far_out=range(1, rows))
    ids = jnp.stack([core, row, lax.axis_index("col")]).astype(jnp.int32)
    ordered = rows == BLOCKS and shard % LANE == 0
    leave = [
        on_chip(
            functools.partial(leave_kernel, norm_width, places, False, ordered), (shaped((tokens, width)),) * 2,
            far_in=(3, 4, 6), far_out=(0, 1),
        ),
        on_chip(
            functools.partial(leave_kernel, norm_width, places, True, ordered),
            (shaped((tokens, width)), shaped((tokens, width), BF16), shaped((tokens, LANE))),
            far_in=(3, 4, 6), far_out=(0,),
        ),
    ]

    pieces_a0 = [hold(p) for p in pieces_a0]
    pieces_a0 += passed_on(pieces_a0)
    close(pieces_a0)
    weights_a0 = both_cores(blocks_of(pieces_a0))
    pieces_b0 = sent_near(hold(piece_b0))
    aux, seg_t, *made0 = enter[0](
        core_id, hold(layer_in), before0, params[0], seg, seg_before, *weights_a0[0], *weights_a0[1]
    )
    normed0, scale0, z0, conv0, value0, scaled0, bc0, step0, cum0, cumt0, lead0, carry0, message0 = made0
    close(message0, pieces_b0)
    messages0 = [from_before(hold(message0), rows, d) for d in distances]
    pieces_b0 = [hold(p) for p in pieces_b0]
    pieces_b0 += passed_on(pieces_b0)
    weights_b0 = both_cores(blocks_of(pieces_b0))
    inside0 = intra(hold(scaled0), value0, bc0, cum0, cumt0, aux, seg_t, params[0])
    close(messages0, inside0, weights_b0)
    gate0 = gate_product(core_id, hold(normed0), *weights_b0[0], *weights_b0[1])
    ssd0, state0, partial0 = gates[0](
        core_id, inside0, bc0, carry0, gate0, params[0], *messages0, *weights_b0[0], *weights_b0[1]
    )
    close(partial0)
    pieces_a1 = sent_near(hold(pick_mine(take_a, own_a)))
    pieces_b1 = sent_near(hold(pick_mine(take_b, own_b)))
    own0 = parts_sum(hold(partial0), "col")
    square = own0[:, width : width + 1] + own0[:, width + 1 : width + 2]
    rest = square - square.astype(BF16).astype(F32)
    lanes = lax.broadcasted_iota(jnp.int32, own0.shape, 1)
    own0 = jnp.where(lanes == width, square, jnp.where(lanes == width + 1, rest, own0)).astype(BF16)
    close(own0, pieces_a1, pieces_b1)
    pieces_a1, pieces_b1 = [hold(p) for p in pieces_a1], [hold(p) for p in pieces_b1]
    pieces_a1 += [sent_to(pieces_a1[0], "row", b) for b in range(near, rows)]
    pieces_b1 += [sent_to(pieces_b1[0], "row", b) for b in range(near, rows)]
    full0 = col_gather(hold(own0))
    blocks_a1 = blocks_of(pieces_a1)
    ready = near if rows == BLOCKS else 0
    others_a1 = [swapped(w) for w in blocks_a1[:ready]]
    close(full0, blocks_a1, others_a1, pieces_b1)
    weights_a1 = (blocks_a1, others_a1 + [swapped(hold(w)) for w in blocks_a1[ready:]])
    full0 = hold(full0)
    squares0 = full0[:, width : width + 1].astype(F32) + full0[:, width + 1 : width + 2].astype(F32)
    rho0 = lax.rsqrt(squares0 / norm_width + EPSILON)
    x1 = (layer_in.astype(F32) + rho0 * full0[:, :width].astype(F32)).astype(BF16)

    before1 = relative_order(from_before(x1[tokens - LEAD :], rows, 1), 1, "row", other_order)
    close(x1, before1)
    weights_b1 = both_cores([hold(w) for w in blocks_of(pieces_b1)])
    made1 = enter[1](core_id, hold(x1), before1, params[1], aux, *weights_a1[0], *weights_a1[1])
    normed1, scale1, z1, conv1, value1, scaled1, bc1, step1, cum1, cumt1, lead1, carry1, message1 = made1
    close(message1, weights_b1)
    messages1 = [from_before(hold(message1), rows, d) for d in distances]
    inside1 = intra(hold(scaled1), value1, bc1, cum1, cumt1, aux, seg_t, params[1])
    gate1 = gate_product(core_id, hold(normed1), *weights_b1[0], *weights_b1[1])
    close(messages1, inside1, gate1)
    gbranch1 = branch_product(core_id, hold(g_out1), *weights_b1[0], *weights_b1[1])
    ssd1, state1, partial1, sums1 = gates[1](
        core_id, inside1, bc1, carry1, gate1, params[1], *messages1, *weights_b1[0], *weights_b1[1], gbranch1
    )
    totals1 = direct_sum(sums1, "col")
    close(totals1)
    rho1 = lax.rsqrt(totals1[0] / norm_width + EPSILON)[:, None]
    norm1 = jnp.pad(jnp.concatenate([rho1, totals1[1][:, None]], axis=1), ((0, 0), (0, LANE - 2)))

    def scan_back(layer, gbranch, norm, gate, ssd, state, made, beside):
        _, scale, z, conv, value, scaled, bc, step, cum, cumt, lead, carry, _ = made
        gssd, ggate, branch, message, ggain = ungates[layer](gbranch, norm, gate, ssd, params[layer], carry, bc)
        close(message)
        messages = [from_after(hold(message), rows, d) for d in distances]
        gscaled, gbc, gcum = intra_grad(scaled, hold(gssd), bc, cum, cumt, aux, seg_t)
        close(messages, gscaled, beside("intra"))
        gpre, gstep, gtaps = inter_grad(
            state, scaled, value, gssd, hold(gscaled), bc, gbc, gcum, step, lead, carry, z, conv, aux, params[layer],
            ggain, *messages,
        )
        close(gpre, beside("inter"))
        return gpre, gstep, gtaps, ggate, branch

    def reduce_back(scanned, normed, scale, x, g_out, weights_a, weights_b, beside):
        gpre, gstep, gtaps, ggate, branch = scanned
        from_next = from_after(hold(gpre[:LEAD]), rows, 1)
        other_b, gg_mine, gg_other, normed_t, g_out_t = give_b(core_id, hold(ggate), normed, g_out, branch)
        kept_b = keep_b(core_id, normed_t, g_out_t, branch, gg_mine, swapped(other_b))
        close(from_next, kept_b, beside("halo"))
        other_a, ga_mine, ga_other = give_a(core_id, gpre, hold(from_next), gstep, normed_t, gtaps)
        close(other_a)
        their_a = swapped(hold(other_a))
        partial, ggain = pull(
            hold(ga_mine), ga_other, gstep, gg_mine, gg_other, x, scale,
            *weights_a[0], *weights_a[1], *weights_b[0], *weights_b[1],
        )
        close(their_a, partial, beside("pull"))
        ggain = hold(ggain)
        ggain = relative_order(ggain + swapped(ggain), 1, "row")
        kept_a = keep_a(normed_t, hold(ga_mine), gstep, their_a, gtaps, ggain)
        close(kept_a, beside("keep"))

        def sends(blocks, which):
            return [sent_to(hold(blocks[b]), "row", b) for b in which]

        early, late = range(1, near), range(near, rows)
        got_a, got_b = sends(kept_a, early), sends(kept_b, early)
        own = parts_sum(hold(partial), "col").astype(BF16)
        close(own, got_a, got_b, beside("scatter"))
        got_a += sends(kept_a, late)
        got_b += sends(kept_b, late)
        full = col_gather(hold(own))
        close(full, got_a, got_b)

        return hold(full), [hold(kept_a[0])] + got_a, [hold(kept_b[0])] + got_b

    def total(pieces):
        return functools.reduce(lambda u, v: u + v.astype(F32), pieces[1:], pieces[0].astype(F32))

    stack = on_chip(stack_kernel, shaped((2, tokens, width)), far_in=(1, 2), far_out=(0,))
    stack_low = on_chip(stack_kernel, shaped((2, tokens, width), BF16), far_out=(0,))

    def in_order_both(pair):
        return pair if ordered else relative_order(pair, 2, "row")

    cols = lax.axis_size("col")
    col = lax.axis_index("col")
    chunk = tokens // cols
    slots = ("intra", "halo", "pull")
    parts1 = [lax.dynamic_slice_in_dim(hold(partial1), (col ^ b) * chunk, chunk, 0) for b in range(cols)]
    received = {1: [], 0: []}
    store = {}

    def exchange(layer, name, sources):
        if name not in slots:
            return ()
        at = slots.index(name)
        mine = range(1 + at, cols) if name == slots[-1] else range(1 + at, min(2 + at, cols))
        got = [sent_to(hold(sources[b]), "col", b) for b in mine]
        received[layer] += got
        return got

    def beside1(name):
        return exchange(1, name, parts1)

    def beside0(name):
        got = list(exchange(0, name, [store["chunk"]] * cols))
        if name == "halo":
            got.append(store["shares"])
        if name == "intra":
            store["state"] = hold(total([p[:shard, half:] for p in store["pieces"]]).astype(BF16))
            store["state_got"] = sent_to(store["state"], "col", 1)
            got.append(store["state_got"])
        if name == "inter":
            summed = store["state"].astype(F32) + hold(store["state_got"]).astype(F32)
            step_out = 2
            while step_out < cols:
                summed = summed.astype(BF16)
                summed = summed.astype(F32) + sent_to(summed, "col", step_out).astype(F32)
                step_out *= 2
            store["state"] = summed
            got.append(summed)
        if name == "scatter":
            made = on_chip(functools.partial(outputs_kernel, ordered), (shaped((tokens, width), BF16),) * 2)(
                ids, hold(x1), norm1, store["chunk"], *received[0]
            )
            store["outputs"] = in_order_both(stack_low(core_id, made[0], swapped(made[1])))
            got.append(store["outputs"])
        return got

    scanned1 = scan_back(1, gbranch1, norm1, gate1, ssd1, state1, made1, beside1)
    grad_full1, pieces_a, pieces_b = reduce_back(
        scanned1, normed1, scale1, x1, g_out1, weights_a1, weights_b1, beside1
    )
    store["chunk"] = functools.reduce(lambda u, v: u + v.astype(F32), received[1], parts1[0].astype(F32)).astype(BF16)
    share_a1, share_b1 = total(pieces_a), total(pieces_b)
    store["pieces"] = pieces_a
    store["shares"] = (share_a1, share_b1)
    g_in1, g_out0, norm0 = leave[1](ids, grad_full1, x1, scale1, params[1], g_out1, full0)
    gbranch0 = branch_product(core_id, g_out0, *weights_b0[0], *weights_b0[1])
    scanned0 = scan_back(0, gbranch0, norm0, gate0, ssd0, state0, made0, beside0)
    grad_full0, pieces_a, pieces_b = reduce_back(
        scanned0, normed0, scale0, layer_in, g_out0, weights_a0, weights_b0, beside0
    )
    tiles = (2 * states + a_width) // LANE
    mine_a, give_a_, mine_b, give_b_, message, d_cv, d_cvb, d_gain, d_heads = on_chip(
        functools.partial(sum_kernel, inner, states, heads_tile),
        (shaped((shard + STEPS, a_width), BF16),) * 2
        + (shaped((shard, b_width), BF16),) * 2
        + (shaped((shard + 16 * tiles, LANE), BF16), shaped((4, inner)), shaped((1, inner)), shaped((1, inner)), shaped((8, LANE))),
        far_in=(1, 2), far_out=(0, 1, 2, 3),
    )(ids, share_a1, share_b1, *[hold(p) for p in pieces_a], *pieces_b)
    close(message)
    messages = [hold(message)] + [sent_to(hold(message), "col", b) for b in range(1, cols)]
    their_a, their_b = swapped(hold(give_a_)), swapped(hold(give_b_))
    mine, give = leave[0](ids, hold(grad_full0), layer_in, scale0, params[0], g_out0, g_in1)
    close(mine, their_a, their_b)
    other_grad = swapped(hold(give))
    d_value, d_step, d_gate, d_out = on_chip(
        join_kernel, (shaped((shard, inner)), shaped((shard, heads)), shaped((shard, inner)), shaped((inner, shard))),
        far_in=(1, 2, 3, 4), far_out=(0, 1, 2, 3),
    )(ids, hold(mine_a), their_a, mine_b, their_b)
    place = jnp.where(first, batch_order[0], core).reshape(1).astype(jnp.int32)
    close(messages, d_value, other_grad)
    mine_s, give_s, d_cs, d_csb, d_norm = on_chip(
        functools.partial(col_kernel, states),
        (shaped((shard, states), BF16),) * 2 + (shaped((4, 2 * states)), shaped((1, 2 * states)), shaped((1, width))),
    )(ids, store["state"], *[hold(m) for m in messages])
    their_s = swapped(give_s)
    input_grads = in_order_both(stack(place, mine, hold(other_grad)))
    d_state = jnp.concatenate([pick_mine(mine_s, their_s), pick_mine(their_s, mine_s)], axis=1).astype(F32)

    return (
        store["outputs"][None],
        input_grads[None],
        d_norm,
        d_gate[None],
        d_value[None],
        d_step[None],
        d_state[None],
        d_cv[None],
        d_cvb,
        d_cs[None],
        d_csb,
        d_heads[0:1, :heads],
        d_heads[1:2, :heads],
        d_heads[5:6, :heads],
        d_gain,
        d_out[None],
    )


def solution(mesh):
    in_specs = (
        P(None, "row", None),
        P(None, "row", None),
        P(None, "row"),
        P(),
        P("pipe", None),
        P("pipe", "row", "col"),
        P("pipe", "row", "col"),
        P("pipe", "row", "col"),
        P("pipe", "row", None),
        P("pipe", None, "col"),
        P("pipe", "col"),
        P("pipe", None, None),
        P("pipe", None),
        P("pipe", "col"),
        P("pipe", "col"),
        P("pipe", "col"),
        P("pipe", "col"),
        P("pipe", "col", "row"),
    )
    out_specs = (
        P("pipe", None, "row", None),
        P("pipe", None, "row", None),
        P("pipe", None),
        P("pipe", "row", "col"),
        P("pipe", "row", "col"),
        P("pipe", "row", "col"),
        P("pipe", "row", None),
        P("pipe", None, "col"),
        P("pipe", "col"),
        P("pipe", None, None),
        P("pipe", None),
        P("pipe", "col"),
        P("pipe", "col"),
        P("pipe", "col"),
        P("pipe", "col"),
        P("pipe", "col", "row"),
    )
    return jax.shard_map(local, mesh=mesh, in_specs=in_specs, out_specs=out_specs, check_vma=False)
```

```python
import functools
import math

import jax
import jax.numpy as jnp
from jax import lax
from jax.experimental import pallas as pl
from jax.experimental.pallas import tpu as pltpu
from jax.sharding import PartitionSpec as P

EPSILON = 1e-05
LOG2E = math.log2(math.e)
LANE = 128
F32 = jnp.float32
BF16 = jnp.bfloat16
SMALL_ROWS = 16
LEAD = 16
VMEM_MIB = 16
TAPS_ROWS = 32
SMALL = 48
STEPS = 16
BLOCKS = 4


def dot_nn(a, b):
    return lax.dot_general(a, b, (((1,), (0,)), ((), ())), preferred_element_type=F32)


def dot_nt(a, b):
    return lax.dot_general(a, b, (((1,), (1,)), ((), ())), preferred_element_type=F32)


def dot_tn(a, b):
    return lax.dot_general(a, b, (((0,), (0,)), ((), ())), preferred_element_type=F32)


def dot_exact(a, b):
    return lax.dot_general(
        a, b, (((1,), (0,)), ((), ())), precision=lax.Precision.HIGHEST, preferred_element_type=F32
    )


def sigmoid(v):
    return 1.0 / (1.0 + jnp.exp(-v))


def split_pair(v):
    high = v.astype(BF16)
    return high, (v - high.astype(F32)).astype(BF16)


def on_chip(kernel, out_shapes, scratch=(), far_in=(), far_out=()):
    whole = pl.BlockSpec(memory_space=pltpu.VMEM)
    scalar = pl.BlockSpec(memory_space=pltpu.SMEM)
    single = not isinstance(out_shapes, tuple)
    shapes = (out_shapes,) if single else out_shapes
    shapes = tuple(pltpu.HBM(o.shape, o.dtype) if i in far_out else o for i, o in enumerate(shapes))

    def call(*operands):
        operands = [
            pltpu.with_memory_space_constraint(o, pltpu.HBM) if i in far_in else o for i, o in enumerate(operands)
        ]
        return pl.pallas_call(
            kernel,
            out_shape=shapes[0] if single else shapes,
            in_specs=[scalar if o.dtype == jnp.int32 else whole for o in operands],
            out_specs=whole if single else (whole,) * len(shapes),
            scratch_shapes=scratch,
            compiler_params=pltpu.CompilerParams(vmem_limit_bytes=VMEM_MIB * 1024 * 1024),
        )(*operands)

    return call


def shaped(shape, dtype=F32):
    return jax.ShapeDtypeStruct(shape, dtype)


def tile_of(q):
    return slice(q * LANE, (q + 1) * LANE)


def spread(columns, q, heads_tile, lane_head):
    first = q * heads_tile
    out = columns[:, first : first + 1]
    for i in range(1, heads_tile):
        out = jnp.where(lane_head == i, columns[:, first + i : first + i + 1], out)
    return out


def lane_heads(rows, heads_tile):
    lanes = lax.broadcasted_iota(jnp.int32, (rows, LANE), 1)
    return lanes // (LANE // heads_tile)


def tri_mask(tokens, seg_col, seg_row, transposed):
    first = lax.broadcasted_iota(jnp.int32, (tokens, tokens), 0)
    second = lax.broadcasted_iota(jnp.int32, (tokens, tokens), 1)
    order = first <= second if transposed else first >= second
    return order & (seg_col == seg_row)


def pack_a_kernel(core_ref, value_ref, state_ref, step_ref, keep_ref, give_ref):
    shard, half = value_ref.shape[0], value_ref.shape[1] // 2
    heads = step_ref.shape[0]
    core = core_ref[0]
    for ref, place in ((keep_ref, core), (give_ref, 1 - core)):
        ref[:shard, :half] = value_ref[:, pl.ds(pl.multiple_of(place * half, LANE), half)]
        ref[:shard, half:] = state_ref[:, pl.ds(pl.multiple_of(place * LANE, LANE), LANE)]
        ref[shard:, :] = jnp.zeros((STEPS, ref.shape[1]), BF16)
        ref[shard : shard + heads, :shard] = step_ref[...]


def pack_b_kernel(core_ref, gate_ref, out_ref, keep_ref, give_ref):
    half = gate_ref.shape[1] // 2
    core = core_ref[0]
    for ref, place in ((keep_ref, core), (give_ref, 1 - core)):
        ref[:, :half] = gate_ref[:, pl.ds(pl.multiple_of(place * half, LANE), half)]
        ref[:, half:] = out_ref[pl.ds(pl.multiple_of(place * half, LANE), half), :].astype(F32).T.astype(BF16)


def enter_kernel(
    inner, heads_tile, places, core_ref, x_ref, before_ref, small_ref, aux_ref, *refs,
):
    taps_ref, heads_ref, gain_ref, _ = views(small_ref, places)
    mine, other = refs[:BLOCKS], refs[BLOCKS : 2 * BLOCKS]
    (
        normed_ref, scale_ref, z_ref, conv_ref, value_ref, scaled_ref, bc_ref, step_ref, cum_ref, cumt_ref, lead_ref,
        carry_ref, msg_ref, leadu_ref,
    ) = refs[2 * BLOCKS :]
    tokens, width = x_ref.shape
    half = inner // 2
    conv_width = conv_ref.shape[1]
    for ref, at in ((before_ref, slice(0, LEAD)), (x_ref, slice(LEAD, LEAD + tokens))):
        x = ref[...].astype(F32)
        scale = lax.rsqrt(jnp.mean(x * x, axis=1, keepdims=True) + EPSILON)
        normed_ref[at, :] = (x * scale * gain_ref[0:1, :]).astype(BF16)
    scale_ref[...] = jnp.broadcast_to(scale, scale_ref.shape)
    core = core_ref[0]
    block = width // BLOCKS
    step = None
    for pieces, place in ((mine, core), (other, 1 - core)):
        z = None
        for i in range(BLOCKS):
            normed = normed_ref[:, i * block : (i + 1) * block]
            term = dot_nn(normed, pieces[i][:block, :])
            z = term if z is None else z + term
            if pieces is mine:
                term = dot_nt(normed, pieces[i][block:, :block])
                step = term if step is None else step + term
        z_ref[:, pl.ds(pl.multiple_of(place * half, LANE), half)] = z[:, :half]
        z_ref[:, pl.ds(pl.multiple_of(inner + place * LANE, LANE), LANE)] = z[:, half:]
    z_ref[:, conv_width:] = jnp.zeros((z_ref.shape[0], LANE), F32)
    z_ref[:, conv_width : conv_width + STEPS] = step
    aux = aux_ref[...]
    raw = z_ref[LEAD:, conv_width:] + heads_ref[0:1, :]
    step = jnp.maximum(raw, 0.0) + jnp.log1p(jnp.exp(-jnp.abs(raw)))
    rates = -step * jnp.exp(heads_ref[1:2, :])
    rows = lax.broadcasted_iota(jnp.int32, (tokens, tokens), 0)
    cols = lax.broadcasted_iota(jnp.int32, (tokens, tokens), 1)
    cum = dot_exact((rows >= cols).astype(F32), rates) * LOG2E
    lead = aux[:, 5:6] * jnp.exp2(cum[tokens - 1 : tokens, :] - cum)
    carry = aux[:, 4:5] * jnp.exp2(cum)
    step_ref[...] = step
    cum_ref[...] = cum
    cumt_ref[...] = cum.T
    lead_ref[...] = lead
    carry_ref[...] = carry
    lane_head = lane_heads(tokens, heads_tile)
    for q in range(conv_width // LANE):
        at = tile_of(q)
        acc = taps_ref[4:5, at] + taps_ref[3:4, at] * z_ref[LEAD:, at]
        for j in range(3):
            shifted = z_ref[LEAD - 3 + j : LEAD - 3 + j + tokens, at]
            acc = acc + taps_ref[j : j + 1, at] * (aux[:, j : j + 1] * shifted)
        conv_ref[:, at] = acc
        value = acc * sigmoid(acc)
        if q < inner // LANE:
            value_ref[:, at] = value
            scaled = spread(step, q, heads_tile, lane_head) * value
            scaled_ref[:, at] = scaled.astype(BF16)
            leadu_ref[:, at] = (spread(lead, q, heads_tile, lane_head) * scaled).astype(BF16)
        else:
            bc_ref[:, tile_of(q - inner // LANE)] = value.astype(BF16)
    msg_ref[0:LANE, :] = dot_tn(bc_ref[:, :LANE], leadu_ref[...]).astype(BF16)
    put_through(msg_ref, carry[tokens - 1 : tokens, :], inner, heads_tile)


def enter_first_kernel(
    inner, heads_tile, places, core_ref, x_ref, before_ref, small_ref, seg_ref, seg_before_ref, *refs,
):
    weights, refs = refs[: 2 * BLOCKS], refs[2 * BLOCKS :]
    aux_ref, segt_ref, *made, seg_ext_ref, leadu_ref = refs
    tokens = x_ref.shape[0]
    seg = seg_ref[...]
    seg_ext_ref[0:LEAD, :] = seg_before_ref[...]
    seg_ext_ref[LEAD:, :] = seg
    lanes = lax.broadcasted_iota(jnp.int32, (tokens, LANE), 1)
    flags = jnp.where(lanes == 3, seg, 0.0)
    for j in range(3):
        same = (seg_ext_ref[LEAD - 3 + j : LEAD - 3 + j + tokens, :] == seg).astype(F32)
        flags = jnp.where(lanes == j, same, flags)
    flags = jnp.where(lanes == 4, (seg == seg_ext_ref[LEAD - 1 : LEAD, :]).astype(F32), flags)
    flags = jnp.where(lanes == 5, (seg == seg[tokens - 1 :, :]).astype(F32), flags)
    aux_ref[...] = flags
    segt_ref[...] = seg.T[0:8, :]
    enter_kernel(
        inner, heads_tile, places, core_ref, x_ref, before_ref, small_ref, aux_ref, *weights, *made, leadu_ref
    )


def views(ref, places):
    return tuple(ref.at[:, p] for p in places)


def put_through(msg_ref, last, inner, heads_tile):
    msg_ref[LANE:, :] = jnp.zeros((SMALL_ROWS, inner), BF16)
    lane_row = lane_heads(1, heads_tile)
    for q in range(inner // LANE):
        high, low = split_pair(spread(last, q, heads_tile, lane_row))
        msg_ref[LANE : LANE + 1, tile_of(q)] = high
        msg_ref[LANE + 1 : LANE + 2, tile_of(q)] = low


def wide_kernel(offset, lead, core_ref, a_ref, *refs):
    mine, other = refs[:BLOCKS], refs[BLOCKS : 2 * BLOCKS]
    out_ref = refs[2 * BLOCKS]
    core = core_ref[0]
    half = out_ref.shape[1] // 2
    block = a_ref.shape[1] // BLOCKS
    for pieces, place in ((mine, core), (other, 1 - core)):
        total = None
        for i in range(BLOCKS):
            term = dot_nn(a_ref[lead:, i * block : (i + 1) * block], pieces[i][:, offset : offset + half])
            total = term if total is None else total + term
        out_ref[:, pl.ds(pl.multiple_of(place * half, LANE), half)] = total


def intra_kernel(
    inner, heads_tile, places, scaled_ref, value_ref, bc_ref, cum_ref, cumt_ref, aux_ref, segt_ref, small_ref,
    out_ref,
):
    heads_ref = views(small_ref, places)[1]
    tokens = scaled_ref.shape[0]
    scores = dot_nt(bc_ref[:, LANE:], bc_ref[:, :LANE])
    scores = jnp.where(tri_mask(tokens, aux_ref[:, 3:4], segt_ref[0:1, :], False), scores, 0.0)
    lane_head = lane_heads(tokens, heads_tile)
    lane_row = lane_heads(1, heads_tile)
    for q in range(inner // LANE):
        at = tile_of(q)
        total = spread(heads_ref[2:3, :], q, heads_tile, lane_row) * value_ref[:, at]
        scaled = scaled_ref[:, at]
        for i in range(heads_tile):
            h = q * heads_tile + i
            gap = jnp.minimum(cum_ref[:, h : h + 1] - cumt_ref[h : h + 1, :], 0.0)
            mixed = (jnp.exp2(gap) * scores).astype(BF16)
            total = total + jnp.where(lane_head == i, dot_nn(mixed, scaled), 0.0)
        out_ref[:, at] = total


def enter_states(messages):
    state = None
    for message in reversed(messages):
        own = message[0:LANE, :].astype(F32)
        through = message[LANE : LANE + 1, :].astype(F32) + message[LANE + 1 : LANE + 2, :].astype(F32)
        state = own if state is None else own + through * state
    return state


def gate_kernel(
    inner, heads_tile, places, count, with_grad, core_ref, intra_ref, bc_ref, carry_ref, gate_ref, small_ref, *refs
):
    gain_ref = views(small_ref, places)[3]
    messages = refs[:count]
    mine, other = refs[count : count + BLOCKS], refs[count + BLOCKS : count + 2 * BLOCKS]
    refs = refs[count + 2 * BLOCKS :]
    if with_grad:
        branch_grad_ref, refs = refs[0], refs[1:]
        ssd_ref, state_ref, msg_ref, sums_ref, gated_ref = refs
    else:
        ssd_ref, state_ref, msg_ref, gated_ref = refs
    tokens = intra_ref.shape[0]
    state = enter_states([m[...] for m in messages]).astype(BF16)
    state_ref[...] = state
    inter = dot_nn(bc_ref[:, LANE:], state)
    lane_head = lane_heads(tokens, heads_tile)
    carry = carry_ref[...]
    squares = jnp.zeros((tokens, LANE), F32)
    products = jnp.zeros((tokens, LANE), F32)
    for q in range(inner // LANE):
        at = tile_of(q)
        ssd = intra_ref[:, at] + spread(carry, q, heads_tile, lane_head) * inter[:, at]
        ssd_ref[:, at] = ssd
        gate = gate_ref[:, at]
        gated = ssd * (gate * sigmoid(gate))
        squares = squares + gated * gated
        scaled = gated * gain_ref[0:1, at]
        gated_ref[:, at] = scaled.astype(BF16)
        if with_grad:
            products = products + scaled * branch_grad_ref[:, at]
    half = inner // 2
    core = core_ref[0]
    low = gated_ref[:, pl.ds(pl.multiple_of(core * half, LANE), half)]
    high = gated_ref[:, pl.ds(pl.multiple_of((1 - core) * half, LANE), half)]
    block = mine[0].shape[0]
    for i in range(BLOCKS):
        part = dot_nt(low, mine[i][:, half:]) + dot_nt(high, other[i][:, half:])
        msg_ref[:, i * block : (i + 1) * block] = part.astype(BF16)
    total = jnp.sum(squares, axis=1, keepdims=True)
    lanes = lax.broadcasted_iota(jnp.int32, (tokens, LANE), 1)
    if with_grad:
        packed = jnp.where(lanes == 0, total, 0.0)
        packed = packed + jnp.where(lanes == 1, jnp.sum(products, axis=1, keepdims=True), 0.0)
        sums_ref[...] = packed.T[0:8, :]
    else:
        rest = total - total.astype(BF16).astype(F32)
        packed = jnp.where(lanes == 0, total, jnp.where(lanes == 1, rest, 0.0))
        msg_ref[:, BLOCKS * block :] = packed.astype(BF16)


def norm_kernel(norm_width, *refs):
    parts = [r[...] for r in refs[:-1]]
    while len(parts) > 1:
        parts = [parts[i] + parts[i + 1] for i in range(0, len(parts), 2)]
    total = parts[0]
    rows = lax.broadcasted_iota(jnp.int32, total.shape, 0)
    total = jnp.where(rows == 0, lax.rsqrt(total / norm_width + EPSILON), total)
    total = jnp.concatenate([total, jnp.zeros((LANE - total.shape[0], total.shape[1]), F32)], axis=0)
    refs[-1][...] = total.T


def ungate_kernel(
    inner, heads_tile, places, norm_width, branch_grad_ref, norm_ref, gate_ref, ssd_ref, small_ref, carry_ref, bc_ref,
    gssd_ref, ggate_ref, branch_ref, msg_ref, ggain_ref, cg_ref,
):
    gain_ref = views(small_ref, places)[3]
    tokens = branch_grad_ref.shape[0]
    rho = norm_ref[:, 0:1]
    pull = norm_ref[:, 1:2] * (rho * rho * rho / norm_width)
    lane_head = lane_heads(tokens, heads_tile)
    carry = carry_ref[...]
    ggain_ref[...] = jnp.zeros(ggain_ref.shape, F32)
    for q in range(inner // LANE):
        at = tile_of(q)
        gate = gate_ref[:, at]
        sig = sigmoid(gate)
        ssd = ssd_ref[:, at]
        gated = ssd * (gate * sig)
        grad = branch_grad_ref[:, at]
        gain = gain_ref[0:1, at]
        normed = gated * rho
        ggain_ref[0:1, at] = jnp.sum(grad * normed, axis=0, keepdims=True)
        branch_ref[:, at] = (normed * gain).astype(BF16)
        ggated = rho * (gain * grad) - gated * pull
        gssd = ggated * (gate * sig)
        gssd_ref[:, at] = gssd
        ggate_ref[:, at] = (ggated * ssd * (sig * (1.0 + gate * (1.0 - sig)))).astype(BF16)
        cg_ref[:, at] = (spread(carry, q, heads_tile, lane_head) * gssd).astype(BF16)
    msg_ref[0:LANE, :] = dot_tn(bc_ref[:, LANE:], cg_ref[...]).astype(BF16)
    put_through(msg_ref, carry[tokens - 1 : tokens, :], inner, heads_tile)


def intra_grad_kernel(
    inner, heads_tile, scaled_ref, gssd_ref, bc_ref, cum_ref, cumt_ref, aux_ref, segt_ref,
    gscaled_ref, gbc_ref, gcum_ref, sums_ref,
):
    tokens = scaled_ref.shape[0]
    mask = tri_mask(tokens, aux_ref[:, 3:4], segt_ref[0:1, :], True)
    scores = jnp.where(mask, dot_nt(bc_ref[:, :LANE], bc_ref[:, LANE:]), 0.0)
    lane_head = lane_heads(tokens, heads_tile)
    gscores = jnp.zeros((tokens, tokens), F32)
    gcum_ref[...] = jnp.zeros(gcum_ref.shape, F32)
    sums_ref[...] = jnp.zeros(sums_ref.shape, F32)
    for q in range(inner // LANE):
        at = tile_of(q)
        grad = gssd_ref[:, at].astype(BF16)
        scaled = scaled_ref[:, at]
        total = jnp.zeros((tokens, LANE), F32)
        for i in range(heads_tile):
            h = q * heads_tile + i
            gap = jnp.minimum(cumt_ref[h : h + 1, :] - cum_ref[:, h : h + 1], 0.0)
            decay = jnp.exp2(gap)
            mixed = decay * scores
            picked = jnp.where(lane_head == i, scaled, jnp.zeros_like(scaled))
            gmixed = dot_nt(picked, grad)
            total = total + jnp.where(lane_head == i, dot_nn(mixed.astype(BF16), grad), 0.0)
            product = gmixed * mixed
            sums_ref[h : h + 1, :] = jnp.sum(product, axis=0, keepdims=True)
            gcum_ref[:, h : h + 1] = -jnp.sum(product, axis=1, keepdims=True)
            gscores = gscores + gmixed * decay
        gscaled_ref[:, at] = total
    gscores = jnp.where(mask, gscores, 0.0)
    gbc_ref[:, :LANE] = dot_nn(gscores.astype(BF16), bc_ref[:, LANE:])
    gbc_ref[:, LANE:] = dot_nn(gscores.T.astype(BF16), bc_ref[:, :LANE])
    gcum_ref[...] = gcum_ref[...] + sums_ref[...].T


def inter_grad_kernel(
    inner, heads_tile, places, count, state_ref, scaled_ref, value_ref, gssd_ref, gscaled_ref, bc_ref, gbc_ref, gcum_ref,
    step_ref, lead_ref, carry_ref, z_ref, conv_ref, aux_ref, small_ref, ggain_ref, *refs,
):
    taps_ref, heads_ref, _, _ = views(small_ref, places)
    messages = refs[:count]
    gpre_ref, gstep_ref, gtaps_ref, em_ref, leadu_ref, cg_ref, gain_ref, lose_ref, gsize_ref = refs[count:]
    tokens = scaled_ref.shape[0]
    width = conv_ref.shape[1]
    aux = aux_ref[...]
    adjoint = enter_states([m[...] for m in messages])
    adjoint_low = adjoint.astype(BF16)
    state = state_ref[...]
    from_adjoint = dot_nn(bc_ref[:, :LANE], adjoint_low)
    from_state = dot_nn(bc_ref[:, LANE:], state)
    overlap = jnp.sum(adjoint * state.astype(F32), axis=0, keepdims=True)
    lane_head = lane_heads(tokens, heads_tile)
    lane_row = lane_heads(1, heads_tile)
    step = step_ref[...]
    lead = lead_ref[...]
    carry = carry_ref[...]
    em_ref[0:8, :] = jnp.zeros((8, LANE), F32)
    em_ref[8 + tokens :, :] = jnp.zeros((8, LANE), F32)
    gpre_ref[0:8, :] = jnp.zeros((8, width), F32)
    gtaps_ref[...] = jnp.zeros(gtaps_ref.shape, F32)

    def through_conv(q, grad):
        at = tile_of(q)
        conv = conv_ref[:, at]
        sig = sigmoid(conv)
        e = grad * (sig * (1.0 + conv * (1.0 - sig)))
        gtaps_ref[4:5, at] = jnp.sum(e, axis=0, keepdims=True)
        gtaps_ref[3:4, at] = jnp.sum(e * z_ref[LEAD:, at], axis=0, keepdims=True)
        total = None
        for j in range(3):
            masked = aux[:, j : j + 1] * e
            shifted = z_ref[LEAD - 3 + j : LEAD - 3 + j + tokens, at]
            gtaps_ref[j : j + 1, at] = jnp.sum(masked * shifted, axis=0, keepdims=True)
            em_ref[8 : 8 + tokens, :] = masked
            term = taps_ref[j : j + 1, at] * em_ref[3 - j : 11 - j + tokens, :]
            total = term if total is None else total + term
        gpre_ref[8:LEAD, at] = total[0:8, :]
        gpre_ref[LEAD:, at] = total[8:, :] + taps_ref[3:4, at] * e

    for q in range(inner // LANE):
        at = tile_of(q)
        scaled = scaled_ref[:, at].astype(F32)
        grad = gssd_ref[:, at]
        value = value_ref[:, at]
        leads = spread(lead, q, heads_tile, lane_head)
        carries = spread(carry, q, heads_tile, lane_head)
        pushed = leads * from_adjoint[:, at]
        gscaled = gscaled_ref[:, at] + pushed
        carried = carries * grad
        leadu_ref[:, at] = (leads * scaled).astype(BF16)
        cg_ref[:, at] = carried.astype(BF16)
        gain_ref[:, at] = (carried * from_state[:, at]).astype(BF16)
        lose_ref[:, at] = (scaled * pushed).astype(BF16)
        gsize_ref[:, at] = (gscaled * value).astype(BF16)
        gtaps_ref[5:6, at] = jnp.sum(grad * value, axis=0, keepdims=True)
        gvalue = spread(step, q, heads_tile, lane_head) * gscaled
        gvalue = gvalue + spread(heads_ref[2:3, :], q, heads_tile, lane_row) * grad
        through_conv(q, gvalue)
    gb = gbc_ref[:, :LANE] + dot_nt(leadu_ref[...], adjoint_low)
    gc = gbc_ref[:, LANE:] + dot_nt(cg_ref[...], state)
    through_conv(inner // LANE, gb)
    through_conv(inner // LANE + 1, gc)
    head_of = lax.broadcasted_iota(jnp.int32, (inner, LANE), 0) // (LANE // heads_tile)
    pick = (head_of == lax.broadcasted_iota(jnp.int32, (inner, LANE), 1)).astype(BF16)
    lose = dot_nn(lose_ref[...], pick)
    gcum = gcum_ref[...] + dot_nn(gain_ref[...], pick) - lose
    high, low = split_pair(overlap)
    ends = dot_nn(jnp.broadcast_to(high, (8, inner)), pick) + dot_nn(jnp.broadcast_to(low, (8, inner)), pick)
    last = carry[tokens - 1 : tokens, :] * ends[0:1, :] + jnp.sum(lose, axis=0, keepdims=True)
    row_of = lax.broadcasted_iota(jnp.int32, (tokens, LANE), 0)
    gcum = gcum + jnp.where(row_of == tokens - 1, last, 0.0)
    rows = lax.broadcasted_iota(jnp.int32, (tokens, tokens), 0)
    cols = lax.broadcasted_iota(jnp.int32, (tokens, tokens), 1)
    grate = dot_exact((rows <= cols).astype(F32), gcum)
    speed = jnp.exp(heads_ref[1:2, :])
    gsize = dot_nn(gsize_ref[...], pick) - speed * grate
    raw = z_ref[LEAD:, width:] + heads_ref[0:1, :]
    graw = gsize * sigmoid(raw)
    gstep_ref[...] = graw.astype(BF16)
    gtaps_ref[6:7, :inner] = ggain_ref[0:1, :]
    gtaps_ref[7:8, 0:LANE] = jnp.sum(graw, axis=0, keepdims=True)
    gtaps_ref[7:8, LANE : 2 * LANE] = jnp.sum(grate * (-speed * step), axis=0, keepdims=True)


def give_b_kernel(
    core_ref, ggate_ref, normed_ref, g_out_ref, branch_ref,
    other_b_ref, gg_mine_ref, gg_other_ref, normed_t_ref, g_out_t_ref,
):
    width = g_out_ref.shape[1]
    half = ggate_ref.shape[1] // 2
    core = core_ref[0]
    gg_mine_ref[...] = ggate_ref[:, pl.ds(pl.multiple_of(core * half, LANE), half)]
    gg_other_ref[...] = ggate_ref[:, pl.ds(pl.multiple_of((1 - core) * half, LANE), half)]
    block = width // BLOCKS
    for i in range(BLOCKS):
        at = slice(i * block, (i + 1) * block)
        normed_t_ref[at, :] = normed_ref[LEAD:, at].astype(F32).T.astype(BF16)
        g_out_t_ref[at, :] = g_out_ref[:, at].astype(F32).T.astype(BF16)
    other_b_ref[:, :half] = dot_nn(normed_t_ref[...], gg_other_ref[...]).astype(BF16)
    branch = branch_ref[:, pl.ds(pl.multiple_of((1 - core) * half, LANE), half)]
    other_b_ref[:, half:] = dot_nn(g_out_t_ref[...], branch).astype(BF16)


def keep_b_kernel(core_ref, normed_t_ref, g_out_t_ref, branch_ref, gg_mine_ref, their_ref, *refs):
    size = normed_t_ref.shape[0] // len(refs)
    half = gg_mine_ref.shape[1]
    branch = branch_ref[:, pl.ds(pl.multiple_of(core_ref[0] * half, LANE), half)]
    for i, ref in enumerate(refs):
        at = slice(i * size, (i + 1) * size)
        part = dot_nn(normed_t_ref[at, :], gg_mine_ref[...]) + their_ref[at, :half].astype(F32)
        ref[:, :half] = part.astype(BF16)
        part = dot_nn(g_out_t_ref[at, :], branch) + their_ref[at, half:].astype(F32)
        ref[:, half:] = part.astype(BF16)


def taps_rows(taps, wide):
    left, right = taps[:, :wide], taps[:, wide:]
    rows = []
    for part in (left, right):
        high = part.astype(BF16).astype(F32)
        rows += [high, part - high]
    return jnp.concatenate(rows, axis=0).astype(BF16)


def gain_rows(gain, wide):
    high = gain.astype(BF16).astype(F32)
    index = lax.broadcasted_iota(jnp.int32, (16, wide), 0)
    out = jnp.zeros((16, wide), F32)
    count = -(-gain.shape[1] // wide)
    for i in range(count):
        for base, part in ((0, high), (8, gain - high)):
            piece = part[:, i * wide : (i + 1) * wide]
            if piece.shape[1] < wide:
                piece = jnp.concatenate([piece, jnp.zeros((1, wide - piece.shape[1]), F32)], axis=1)
            out = jnp.where(index == base + i, piece, out)
    return out.astype(BF16)


def give_a_kernel(
    core_ref, gpre_ref, next_ref, gstep_ref, normed_t_ref, gtaps_ref, other_a_ref, ga_mine_ref, ga_other_ref, glow_ref
):
    tokens, width = glow_ref.shape
    inner = width - 2 * LANE
    half = inner // 2
    core = core_ref[0]
    cut = tokens - LEAD
    glow_ref[:cut, :] = gpre_ref[LEAD : LEAD + cut, :].astype(BF16)
    glow_ref[cut:, :] = (gpre_ref[LEAD + cut :, :] + next_ref[...]).astype(BF16)
    for ga_ref, place in ((ga_mine_ref, core), (ga_other_ref, 1 - core)):
        ga_ref[:, :half] = glow_ref[:, pl.ds(pl.multiple_of(place * half, LANE), half)]
        ga_ref[:, half:] = glow_ref[:, pl.ds(pl.multiple_of(inner + place * LANE, LANE), LANE)]
    rows, wide = normed_t_ref.shape[0], other_a_ref.shape[1]
    other_a_ref[:rows, :] = dot_nn(normed_t_ref[...], ga_other_ref[...]).astype(BF16)
    steps = step_grads(gstep_ref, normed_t_ref)
    for i in range(rows // wide):
        other_a_ref[rows + STEPS * i : rows + STEPS * (i + 1), :] = steps[:, i * wide : (i + 1) * wide].astype(BF16)
    other_a_ref[rows + STEPS * (rows // wide) :, :] = taps_rows(gtaps_ref[...], wide)


def step_grads(gstep_ref, normed_t_ref):
    return dot_nt(gstep_ref[...].astype(F32).T[0:STEPS, :].astype(BF16), normed_t_ref[...])


def keep_a_kernel(normed_t_ref, ga_mine_ref, gstep_ref, their_ref, gtaps_ref, ggain_ref, *refs):
    rows = normed_t_ref.shape[0]
    size = rows // len(refs)
    wide = ga_mine_ref.shape[1]
    groups = [
        their_ref[rows + STEPS * i : rows + STEPS * (i + 1), :].astype(F32) for i in range(rows // wide + TAPS_ROWS // STEPS)
    ]
    steps = step_grads(gstep_ref, normed_t_ref) + jnp.concatenate(groups[: rows // wide], axis=1)
    taps = jnp.concatenate([t[0:8] + t[8:16] for t in groups[rows // wide :]], axis=1)[:, : gtaps_ref.shape[1]]
    small = taps_rows(taps + gtaps_ref[...], wide)
    gain = gain_rows(ggain_ref[0:1, :], wide)
    below = size + STEPS
    for i, ref in enumerate(refs):
        at = slice(i * size, (i + 1) * size)
        ref[:size, :] = (dot_nn(normed_t_ref[at, :], ga_mine_ref[...]) + their_ref[at, :].astype(F32)).astype(BF16)
        ref[size:below, :] = jnp.zeros((STEPS, wide), BF16)
        ref[size:below, :size] = steps[:, at].astype(BF16)
        ref[below : below + TAPS_ROWS, :] = small
        ref[below + TAPS_ROWS :, :] = gain


def pull_kernel(ga_mine_ref, ga_other_ref, gstep_ref, gg_mine_ref, gg_other_ref, x_ref, scale_ref, *refs):
    mine_a, other_a, mine_b, other_b = (refs[i * BLOCKS : (i + 1) * BLOCKS] for i in range(4))
    msg_ref, ggain_ref = refs[4 * BLOCKS :]
    half = gg_mine_ref.shape[1]
    block = mine_b[0].shape[0]
    scale = scale_ref[:, 0:1]
    ggain_ref[...] = jnp.zeros(ggain_ref.shape, F32)
    for i in range(BLOCKS):
        at = slice(i * block, (i + 1) * block)
        part = dot_nt(ga_mine_ref[...], mine_a[i][:block, :])
        part = part + dot_nt(ga_other_ref[...], other_a[i][:block, :])
        part = part + dot_nn(gstep_ref[:, :STEPS], mine_a[i][block:, :block])
        part = part + dot_nt(gg_mine_ref[...], mine_b[i][:, :half])
        part = part + dot_nt(gg_other_ref[...], other_b[i][:, :half])
        msg_ref[:, at] = part.astype(BF16)
        ggain_ref[0:1, at] = jnp.sum(part * (x_ref[:, at].astype(F32) * scale), axis=0, keepdims=True)


def leave_kernel(norm_width, places, below, ordered, ids_ref, full_ref, x_ref, scale_ref, small_ref, g_out_ref, *refs):
    gain_ref = views(small_ref, places)[2]
    tokens, width = x_ref.shape
    scale = scale_ref[:, 0:1]
    x = x_ref[...].astype(F32)
    pulled = full_ref[...].astype(F32) * gain_ref[0:1, :]
    slope = jnp.sum(pulled * x, axis=1, keepdims=True) * (scale * scale * scale / width)
    grad = g_out_ref[...].astype(F32) + scale * pulled - x * slope
    core = ids_ref[0]

    def put(ref):
        put_blocks(ordered, ids_ref[1], ref, slice(None), grad)

    if below:
        raw_ref, grad_ref, low_ref, norm_ref = refs
        put(grad_ref)
        low = grad.astype(BF16)
        low_ref[...] = low
        dots = jnp.sum(low.astype(F32) * raw_ref[:, :width].astype(F32), axis=1, keepdims=True)
        squares = raw_ref[:, width : width + 1].astype(F32) + raw_ref[:, width + 1 : width + 2].astype(F32)
        lanes = lax.broadcasted_iota(jnp.int32, (tokens, LANE), 1)
        norm_ref[...] = jnp.where(lanes == 0, lax.rsqrt(squares / norm_width + EPSILON), dots)
        return
    above_ref, mine_ref, give_ref = refs

    @pl.when(core == 0)
    def _():
        put(mine_ref)
        give_ref[...] = above_ref[...]

    @pl.when(core != 0)
    def _():
        put(give_ref)
        mine_ref[...] = above_ref[...]


def put_blocks(ordered, row, ref, at, value):
    block = value.shape[1] // BLOCKS
    for i in range(BLOCKS):
        part = value[:, i * block : (i + 1) * block]
        if ordered:
            ref[at, pl.ds(pl.multiple_of((row ^ i) * block, LANE), block)] = part
        else:
            ref[at, i * block : (i + 1) * block] = part


def outputs_kernel(ordered, ids_ref, x_ref, norm_ref, *refs):
    chunks, (mine_ref, give_ref) = refs[:-2], refs[-2:]
    size = chunks[0].shape[0]
    for b, chunk in enumerate(chunks):
        at = pl.ds(pl.multiple_of((ids_ref[2] ^ b) * size, size), size)
        below = x_ref[at, :]
        above = (below.astype(F32) + norm_ref[at, 0:1] * chunk[...].astype(F32)).astype(BF16)
        for first, second, chosen in ((mine_ref, give_ref, 0), (give_ref, mine_ref, 1)):

            @pl.when(ids_ref[0] == chosen)
            def _():
                put_blocks(ordered, ids_ref[1], first, at, below)
                put_blocks(ordered, ids_ref[1], second, at, above)


def stack_kernel(place_ref, mine_ref, their_ref, out_ref):
    out_ref[place_ref[0]] = mine_ref[...]
    out_ref[1 - place_ref[0]] = their_ref[...]


def sum_kernel(inner, states, heads_tile, ids_ref, share_a_ref, share_b_ref, *refs):
    mine_a_ref, give_a_ref, mine_b_ref, give_b_ref, msg_ref, taps_ref, bias_ref, gain_ref, heads_ref = refs[-9:]
    pieces = refs[:-9]
    count = len(pieces) // 2
    a = functools.reduce(lambda u, v: u + v, [p[...].astype(F32) for p in pieces[:count]])
    b = functools.reduce(lambda u, v: u + v, [p[...].astype(F32) for p in pieces[count:]])
    shard = mine_b_ref.shape[0]
    half = inner // 2
    below = shard + STEPS
    msg_ref[:shard, :] = a[:shard, half:].astype(BF16)

    def small(part):
        vec = jnp.concatenate([part[0:8] + part[8:16], part[16:24] + part[24:32]], axis=1)
        taps_ref[...] = vec[0:4, :inner]
        bias_ref[...] = vec[4:5, :inner]
        gain_ref[...] = vec[6:7, :inner]
        head_of = lax.broadcasted_iota(jnp.int32, (inner, LANE), 0) // (LANE // heads_tile)
        pick = (head_of == lax.broadcasted_iota(jnp.int32, (inner, LANE), 1)).astype(F32)
        heads_ref[0:1, :] = vec[7:8, 0:LANE]
        heads_ref[1:2, :] = vec[7:8, LANE : 2 * LANE]
        heads_ref[2:8, :] = dot_exact(vec[:, :inner], pick)[2:8, :]
        rest = jnp.concatenate(
            [vec[:, inner : inner + 2 * states], part[TAPS_ROWS : TAPS_ROWS + 8] + part[TAPS_ROWS + 8 :]], axis=1
        )
        high = rest.astype(BF16).astype(F32)
        both = jnp.concatenate([high, rest - high], axis=0).astype(BF16)
        for i in range(rest.shape[1] // LANE):
            msg_ref[shard + 16 * i : shard + 16 * (i + 1), :] = both[:, tile_of(i)]

    @pl.when(ids_ref[0] == 0)
    def _():
        mine_a_ref[...] = a[:below].astype(BF16)
        give_a_ref[...] = share_a_ref[:below, :].astype(BF16)
        mine_b_ref[...] = b.astype(BF16)
        give_b_ref[...] = share_b_ref[...].astype(BF16)
        small(a[below:])

    @pl.when(ids_ref[0] != 0)
    def _():
        mine_a_ref[...] = share_a_ref[:below, :].astype(BF16)
        give_a_ref[...] = a[:below].astype(BF16)
        mine_b_ref[...] = share_b_ref[...].astype(BF16)
        give_b_ref[...] = b.astype(BF16)
        small(share_a_ref[below:, :])


def col_kernel(states, ids_ref, state_ref, *refs):
    mine_ref, give_ref, taps_ref, bias_ref, gain_ref = refs[-5:]
    parts = [r[...].astype(F32) for r in refs[:-5]]
    while len(parts) > 1:
        parts = [parts[i] + parts[i + 1] for i in range(0, len(parts), 2)]
    shard = mine_ref.shape[0]
    own, rest = parts[0][:shard].astype(BF16), parts[0][shard:]
    tiles = [rest[16 * i : 16 * i + 8] + rest[16 * i + 8 : 16 * (i + 1)] for i in range(rest.shape[0] // 16)]
    count = 2 * states // LANE
    for i in range(count):
        taps_ref[:, tile_of(i)] = tiles[i][0:4]
        bias_ref[:, tile_of(i)] = tiles[i][4:5]
    wide = len(tiles) - count
    for i in range(gain_ref.shape[1] // LANE):
        gain_ref[:, tile_of(i)] = tiles[count + i % wide][i // wide : i // wide + 1]
    for first, second, chosen in ((mine_ref, give_ref, 0), (give_ref, mine_ref, 1)):

        @pl.when(ids_ref[0] == chosen)
        def _():
            first[...] = own
            second[...] = state_ref[...].astype(BF16)


def join_kernel(ids_ref, mine_a_ref, their_a_ref, mine_b_ref, their_b_ref, value_ref, step_ref, gate_ref, out_ref):
    shard, half = value_ref.shape[0], value_ref.shape[1] // 2
    core = ids_ref[0]
    for a_ref, b_ref, place in ((mine_a_ref, mine_b_ref, core), (their_a_ref, their_b_ref, 1 - core)):
        at = pl.ds(pl.multiple_of(place * half, LANE), half)
        value_ref[:, at] = a_ref[:shard, :half].astype(F32)
        gate_ref[:, at] = b_ref[:, :half].astype(F32)
        out_ref[at, :] = b_ref[:, half:].astype(F32).T
    step_ref[...] = mine_a_ref[shard:, :shard].astype(F32)[: step_ref.shape[0], :]


def permute(block, axis, route):
    return lax.ppermute(block, axis, route)


def from_before(block, count, distance):
    return permute(block, "row", [(i, i + distance) for i in range(count - distance)])


def from_after(block, count, distance):
    return permute(block, "row", [(i + distance, i) for i in range(count - distance)])


def swapped(block):
    return permute(block, "pipe", [(0, 1), (1, 0)])


def exchanged(blocks, axis):
    return lax.all_to_all(blocks, axis, 0, 0)


def spread_out(block, axis):
    count = lax.axis_size(axis)
    return exchanged(jnp.broadcast_to(block[None], (count,) + block.shape), axis).reshape(
        (count * block.shape[0],) + block.shape[1:]
    )


def parts_sum(block, axis):
    count = lax.axis_size(axis)
    parts = exchanged(block.reshape((count, block.shape[0] // count) + block.shape[1:]), axis)
    return jnp.sum(parts.astype(F32), axis=0)


def sent_to(block, axis, flip):
    count = lax.axis_size(axis)
    return permute(block, axis, [(i, i ^ flip) for i in range(count)])


def relative_order(block, dim, axis, place=None):
    count = lax.axis_size(axis)
    size = block.shape[dim] // count
    place = lax.axis_index(axis) if place is None else place
    return jnp.concatenate(
        [lax.dynamic_slice_in_dim(block, (place ^ b) * size, size, dim) for b in range(count)], axis=dim
    )


class Phases:
    def __init__(self, token):
        self.token = token

    def hold(self, value):
        return lax.optimization_barrier((value, self.token))[0]

    def close(self, *values):
        self.token = lax.optimization_barrier((self.token,) + tuple(jax.tree.leaves(values)))[0]


def col_gather(block):
    return lax.all_gather(block, "col", axis=0, tiled=True)


def after(block, *others):
    return lax.optimization_barrier((block,) + others)[0]


def local(
    inputs, cotangent, segment_ids, batch_order, norm_gain, gate_proj, value_proj, step_proj, state_proj,
    conv_value, conv_value_bias, conv_state, conv_state_bias, step_bias, decay_log, skip_gain, gate_gain, out_proj,
):
    core = lax.axis_index("pipe")
    first = core == 0
    core_id = core.reshape(1).astype(jnp.int32)
    rows = lax.axis_size("row")
    row = lax.axis_index("row")
    tokens, width = inputs.shape[1], inputs.shape[2]
    inner = gate_proj.shape[2]
    heads = step_proj.shape[2]
    states = state_proj.shape[2] // 2
    heads_tile = LANE // (inner // heads)
    half = inner // 2
    conv_width = inner + 2 * states
    norm_width = inner * lax.axis_size("col")
    reach = max(rows // 2, 1)
    distances = range(1, reach + 1)
    group = rows // BLOCKS

    def pick_mine(a, b):
        return jnp.where(first, a, b)

    phases = Phases(core_id)
    hold, close = phases.hold, phases.close

    shard = gate_proj.shape[1]
    a_width, b_width = half + states, inner
    own_a, away_a = on_chip(pack_a_kernel, (shaped((shard + STEPS, a_width), BF16),) * 2, far_in=(1, 2, 3))(
        core_id, value_proj[0], state_proj[0], step_proj[0].T
    )
    close(away_a)
    take_a = swapped(hold(away_a))
    own_b, away_b = on_chip(pack_b_kernel, (shaped((shard, b_width), BF16),) * 2, far_in=(1, 2))(core_id, hold(gate_proj[0]), out_proj[0])
    close(take_a, away_b)

    def blocks_of(pieces):
        if pieces[0].shape[0] > shard and group > 1:
            made = []
            for i in range(BLOCKS):
                part = pieces[i * group : (i + 1) * group]
                steps = jnp.concatenate([p[shard:, :shard] for p in part], axis=1)
                steps = jnp.pad(steps, ((0, 0), (0, a_width - steps.shape[1])))
                made.append(jnp.concatenate([p[:shard] for p in part] + [steps], axis=0))
            return made
        return [jnp.concatenate(pieces[i * group : (i + 1) * group], axis=0) for i in range(BLOCKS)]

    near = 3 if rows == BLOCKS else rows

    def sent_near(block):
        return [block] + [sent_to(block, "row", b) for b in range(1, near)]

    def passed_on(pieces):
        if rows != BLOCKS:
            return []
        cut = -(-pieces[0].shape[0] // 32) * 16
        return [jnp.concatenate([sent_to(pieces[1][:cut], "row", 2), sent_to(pieces[2][cut:], "row", 1)], axis=0)]

    def both_cores(mine):
        return mine, [swapped(p) for p in mine]

    piece_a0 = hold(pick_mine(own_a, take_a))
    pieces_a0 = sent_near(piece_a0)
    take_b = swapped(hold(away_b))
    piece_b0 = pick_mine(own_b, take_b)

    taps_own = jnp.concatenate(
        [
            jnp.concatenate([hold(conv_value[0]), conv_state[0]], axis=1),
            jnp.concatenate([conv_value_bias, conv_state_bias], axis=1),
            jnp.zeros((3, conv_width), F32),
        ],
        axis=0,
    )
    heads_own = jnp.pad(jnp.concatenate([hold(step_bias), decay_log, skip_gain], axis=0), ((0, 5), (0, LANE - heads)))
    gains_own = jnp.concatenate([relative_order(hold(norm_gain), 1, "row"), gate_gain], axis=1)
    gains_own = jnp.pad(gains_own, ((0, 7), (0, 0)))
    small = jnp.concatenate([taps_own, heads_own, gains_own], axis=1)
    small_other = swapped(small)
    params = (pick_mine(small, small_other), pick_mine(small_other, small))
    places = (slice(0, conv_width), slice(conv_width, conv_width + LANE))
    places += (slice(conv_width + LANE, conv_width + LANE + width), slice(conv_width + LANE + width, small.shape[1]))

    source = hold(batch_order)[core]
    layer_in = relative_order(inputs[source], 1, "row")
    seg = jnp.broadcast_to(segment_ids[source].astype(F32)[:, None], (tokens, LANE))
    sent_rows = jnp.concatenate([layer_in[tokens - LEAD :], seg[tokens - LEAD :].astype(BF16)], axis=1)
    got_rows = from_before(sent_rows, rows, 1)
    other_order = row ^ jnp.maximum(row - 1, 0)
    before0 = relative_order(got_rows[:, :width], 1, "row", other_order)
    seg_before = jnp.where(row == 0, -1.0, got_rows[:, width:].astype(F32))
    g_out1 = relative_order(hold(cotangent)[core], 1, "row")
    close(pieces_a0, piece_b0, params, layer_in, seg, before0, seg_before, g_out1)

    long = tokens + LEAD
    message_shape = shaped((states + SMALL_ROWS, inner), BF16)
    entered = (
        shaped((long, width), BF16), shaped((tokens, LANE)), shaped((long, conv_width + LANE)),
        shaped((tokens, conv_width)), shaped((tokens, inner)), shaped((tokens, inner), BF16),
        shaped((tokens, 2 * states), BF16), shaped((tokens, LANE)), shaped((tokens, LANE)), shaped((LANE, tokens)),
        shaped((tokens, LANE)), shaped((tokens, LANE)), message_shape,
    )
    enter = [
        on_chip(
            functools.partial(enter_first_kernel, inner, heads_tile, places),
            (shaped((tokens, LANE)), shaped((8, tokens))) + entered,
            [pltpu.VMEM((long, LANE), F32), pltpu.VMEM((tokens, inner), BF16)],
        ),
        on_chip(
            functools.partial(enter_kernel, inner, heads_tile, places), entered, [pltpu.VMEM((tokens, inner), BF16)]
        ),
    ]
    intra = on_chip(functools.partial(intra_kernel, inner, heads_tile, places), shaped((tokens, inner)))
    gate_product = on_chip(functools.partial(wide_kernel, 0, LEAD), shaped((tokens, inner)))
    branch_product = on_chip(functools.partial(wide_kernel, half, 0), shaped((tokens, inner)))
    gates = [
        on_chip(
            functools.partial(gate_kernel, inner, heads_tile, places, reach, with_grad),
            (shaped((tokens, inner)), shaped((states, inner), BF16))
            + ((shaped((tokens, width), BF16), shaped((8, tokens))) if with_grad else (shaped((tokens, width + LANE), BF16),)),
            [pltpu.VMEM((tokens, inner), BF16)],
        )
        for with_grad in (False, True)
    ]
    ungates = [on_chip(
        functools.partial(ungate_kernel, inner, heads_tile, places, norm_width),
        (
            shaped((tokens, inner)), shaped((tokens, inner), BF16), shaped((tokens, inner), BF16), message_shape,
            shaped((8, inner)),
        ),
        [pltpu.VMEM((tokens, inner), BF16)],
        far_in=far,
    ) for far in ((), (0, 2, 3, 4, 5, 6))]
    intra_grad = on_chip(
        functools.partial(intra_grad_kernel, inner, heads_tile),
        (shaped((tokens, inner)), shaped((tokens, 2 * states)), shaped((tokens, LANE))),
        [pltpu.VMEM((LANE, tokens), F32)],
    )
    inter_grad = on_chip(
        functools.partial(inter_grad_kernel, inner, heads_tile, places, reach),
        (shaped((long, conv_width)), shaped((tokens, LANE), BF16), shaped((8, conv_width))),
        [pltpu.VMEM((tokens + 16, LANE), F32)] + [pltpu.VMEM((tokens, inner), BF16)] * 5,
    )
    pull = on_chip(pull_kernel, (shaped((tokens, width), BF16), shaped((8, width))))
    weight_t = shaped((width, tokens), BF16)
    give_a = on_chip(
        give_a_kernel,
        (shaped((width + STEPS * (width // a_width) + TAPS_ROWS, a_width), BF16),) + (shaped((tokens, a_width), BF16),) * 2,
        [pltpu.VMEM((tokens, conv_width), BF16)],
    )
    give_b = on_chip(
        give_b_kernel,
        (shaped((width, b_width), BF16), shaped((tokens, half), BF16), shaped((tokens, half), BF16), weight_t, weight_t),
    )
    keep_a = on_chip(keep_a_kernel, (shaped((shard + STEPS + SMALL, a_width), BF16),) * rows, far_out=range(1, rows))
    keep_b = on_chip(keep_b_kernel, (shaped((shard, b_width), BF16),) * rows, far_out=range(1, rows))
    ids = jnp.stack([core, row, lax.axis_index("col")]).astype(jnp.int32)
    ordered = rows == BLOCKS and shard % LANE == 0
    leave = [
        on_chip(
            functools.partial(leave_kernel, norm_width, places, False, ordered), (shaped((tokens, width)),) * 2,
            far_in=(3, 4, 6), far_out=(0, 1),
        ),
        on_chip(
            functools.partial(leave_kernel, norm_width, places, True, ordered),
            (shaped((tokens, width)), shaped((tokens, width), BF16), shaped((tokens, LANE))),
            far_in=(3, 4, 6), far_out=(0,),
        ),
    ]

    pieces_a0 = [hold(p) for p in pieces_a0]
    pieces_a0 += passed_on(pieces_a0)
    close(pieces_a0)
    weights_a0 = both_cores(blocks_of(pieces_a0))
    pieces_b0 = sent_near(hold(piece_b0))
    aux, seg_t, *made0 = enter[0](
        core_id, hold(layer_in), before0, params[0], seg, seg_before, *weights_a0[0], *weights_a0[1]
    )
    normed0, scale0, z0, conv0, value0, scaled0, bc0, step0, cum0, cumt0, lead0, carry0, message0 = made0
    close(message0, pieces_b0)
    messages0 = [from_before(hold(message0), rows, d) for d in distances]
    inside0 = intra(hold(scaled0), value0, bc0, cum0, cumt0, aux, seg_t, params[0])
    close(messages0, inside0)
    pieces_b0 = [hold(p) for p in pieces_b0]
    pieces_b0 += passed_on(pieces_b0)
    weights_b0 = both_cores(blocks_of(pieces_b0))
    close(weights_b0)
    gate0 = gate_product(core_id, hold(normed0), *weights_b0[0], *weights_b0[1])
    ssd0, state0, partial0 = gates[0](
        core_id, inside0, bc0, carry0, gate0, params[0], *messages0, *weights_b0[0], *weights_b0[1]
    )
    close(partial0)
    pieces_a1 = sent_near(hold(pick_mine(take_a, own_a)))
    pieces_b1 = sent_near(hold(pick_mine(take_b, own_b)))
    own0 = parts_sum(hold(partial0), "col")
    square = own0[:, width : width + 1] + own0[:, width + 1 : width + 2]
    rest = square - square.astype(BF16).astype(F32)
    lanes = lax.broadcasted_iota(jnp.int32, own0.shape, 1)
    own0 = jnp.where(lanes == width, square, jnp.where(lanes == width + 1, rest, own0)).astype(BF16)
    close(own0, pieces_a1, pieces_b1)
    pieces_a1, pieces_b1 = [hold(p) for p in pieces_a1], [hold(p) for p in pieces_b1]
    pieces_a1 += [sent_to(pieces_a1[0], "row", b) for b in range(near, rows)]
    pieces_b1 += [sent_to(pieces_b1[0], "row", b) for b in range(near, rows)]
    full0 = col_gather(hold(own0))
    blocks_a1 = blocks_of(pieces_a1)
    ready = near if rows == BLOCKS else 0
    others_a1 = [swapped(w) for w in blocks_a1[:ready]]
    close(full0, blocks_a1, others_a1, pieces_b1)
    weights_a1 = (blocks_a1, others_a1 + [swapped(hold(w)) for w in blocks_a1[ready:]])
    full0 = hold(full0)
    squares0 = full0[:, width : width + 1].astype(F32) + full0[:, width + 1 : width + 2].astype(F32)
    rho0 = lax.rsqrt(squares0 / norm_width + EPSILON)
    x1 = (layer_in.astype(F32) + rho0 * full0[:, :width].astype(F32)).astype(BF16)

    before1 = relative_order(from_before(x1[tokens - LEAD :], rows, 1), 1, "row", other_order)
    close(x1, before1, weights_a1)
    weights_b1 = both_cores([hold(w) for w in blocks_of(pieces_b1)])
    made1 = enter[1](core_id, hold(x1), before1, params[1], aux, *weights_a1[0], *weights_a1[1])
    normed1, scale1, z1, conv1, value1, scaled1, bc1, step1, cum1, cumt1, lead1, carry1, message1 = made1
    close(message1, weights_b1)
    messages1 = [from_before(hold(message1), rows, d) for d in distances]
    inside1 = intra(hold(scaled1), value1, bc1, cum1, cumt1, aux, seg_t, params[1])
    gate1 = gate_product(core_id, hold(normed1), *weights_b1[0], *weights_b1[1])
    close(messages1, inside1, gate1)
    gbranch1 = branch_product(core_id, hold(g_out1), *weights_b1[0], *weights_b1[1])
    ssd1, state1, partial1, sums1 = gates[1](
        core_id, inside1, bc1, carry1, gate1, params[1], *messages1, *weights_b1[0], *weights_b1[1], gbranch1
    )
    sums1 = [sums1] + [sent_to(sums1, "col", b) for b in range(1, lax.axis_size("col"))]
    norm1 = on_chip(functools.partial(norm_kernel, norm_width), shaped((tokens, LANE)))(*sums1)
    close(norm1)

    def scan_back(layer, gbranch, norm, gate, ssd, state, made, beside):
        _, scale, z, conv, value, scaled, bc, step, cum, cumt, lead, carry, _ = made
        gssd, ggate, branch, message, ggain = ungates[layer](gbranch, norm, gate, ssd, params[layer], carry, bc)
        close(message)
        messages = [from_after(hold(message), rows, d) for d in distances]
        gscaled, gbc, gcum = intra_grad(scaled, hold(gssd), bc, cum, cumt, aux, seg_t)
        close(messages, gscaled, beside("intra"))
        gpre, gstep, gtaps = inter_grad(
            state, scaled, value, gssd, hold(gscaled), bc, gbc, gcum, step, lead, carry, z, conv, aux, params[layer],
            ggain, *messages,
        )
        close(gpre, beside("inter"))
        return gpre, gstep, gtaps, ggate, branch

    def reduce_back(scanned, normed, scale, x, g_out, weights_a, weights_b, beside):
        gpre, gstep, gtaps, ggate, branch = scanned
        from_next = from_after(hold(gpre[:LEAD]), rows, 1)
        other_b, gg_mine, gg_other, normed_t, g_out_t = give_b(core_id, hold(ggate), normed, g_out, branch)
        kept_b = keep_b(core_id, normed_t, g_out_t, branch, gg_mine, swapped(other_b))
        close(from_next, kept_b, beside("halo"))
        other_a, ga_mine, ga_other = give_a(core_id, gpre, hold(from_next), gstep, normed_t, gtaps)
        close(other_a)
        their_a = swapped(hold(other_a))
        partial, ggain = pull(
            hold(ga_mine), ga_other, gstep, gg_mine, gg_other, x, scale,
            *weights_a[0], *weights_a[1], *weights_b[0], *weights_b[1],
        )
        close(their_a, partial, beside("pull"))
        ggain = hold(ggain)
        ggain = relative_order(ggain + swapped(ggain), 1, "row")
        kept_a = keep_a(normed_t, hold(ga_mine), gstep, their_a, gtaps, ggain)
        close(kept_a, beside("keep"))

        def sends(blocks, which):
            return [sent_to(hold(blocks[b]), "row", b) for b in which]

        early, late = range(1, near), range(near, rows)
        got_a, got_b = sends(kept_a, early), sends(kept_b, early)
        own = parts_sum(hold(partial), "col").astype(BF16)
        close(own, got_a, got_b, beside("scatter"))
        got_a += sends(kept_a, late)
        got_b += sends(kept_b, late)
        full = col_gather(hold(own))
        close(full, got_a, got_b)

        return hold(full), [hold(kept_a[0])] + got_a, [hold(kept_b[0])] + got_b

    def total(pieces):
        return functools.reduce(lambda u, v: u + v.astype(F32), pieces[1:], pieces[0].astype(F32))

    stack = on_chip(stack_kernel, shaped((2, tokens, width)), far_in=(1, 2), far_out=(0,))
    stack_low = on_chip(stack_kernel, shaped((2, tokens, width), BF16), far_out=(0,))

    def in_order_both(pair):
        return pair if ordered else relative_order(pair, 2, "row")

    cols = lax.axis_size("col")
    col = lax.axis_index("col")
    chunk = tokens // cols
    slots = ("intra", "halo", "pull")
    parts1 = [lax.dynamic_slice_in_dim(hold(partial1), (col ^ b) * chunk, chunk, 0) for b in range(cols)]
    received = {1: [], 0: []}
    store = {}

    def exchange(layer, name, sources):
        if name not in slots:
            return ()
        at = slots.index(name)
        mine = range(1 + at, cols) if name == slots[-1] else range(1 + at, min(2 + at, cols))
        got = [sent_to(hold(sources[b]), "col", b) for b in mine]
        received[layer] += got
        return got

    def beside1(name):
        return exchange(1, name, parts1)

    def beside0(name):
        got = list(exchange(0, name, [store["chunk"]] * cols))
        if name == "intra":
            store["state"] = hold(total([p[:shard, half:] for p in store["pieces"][0]]).astype(BF16))
            store["state_got"] = sent_to(store["state"], "col", 1)
            got.append(store["state_got"])
        if name == "inter":
            summed = store["state"].astype(F32) + hold(store["state_got"]).astype(F32)
            step_out = 2
            while step_out < cols:
                summed = summed.astype(BF16)
                summed = summed.astype(F32) + sent_to(summed, "col", step_out).astype(F32)
                step_out *= 2
            store["state"] = summed
            got.append(summed)
        if name == "scatter":
            store["shares"] = [total([hold(p) for p in pieces]) for pieces in store["pieces"]]
            got.append(store["shares"])
            made = on_chip(functools.partial(outputs_kernel, ordered), (shaped((tokens, width), BF16),) * 2)(
                ids, hold(x1), norm1, store["chunk"], *received[0]
            )
            store["outputs"] = in_order_both(stack_low(core_id, made[0], swapped(made[1])))
            got.append(store["outputs"])
        return got

    scanned1 = scan_back(1, gbranch1, norm1, gate1, ssd1, state1, made1, beside1)
    grad_full1, pieces_a, pieces_b = reduce_back(
        scanned1, normed1, scale1, x1, g_out1, weights_a1, weights_b1, beside1
    )
    store["chunk"] = functools.reduce(lambda u, v: u + v.astype(F32), received[1], parts1[0].astype(F32)).astype(BF16)
    store["pieces"] = (pieces_a, pieces_b)
    g_in1, g_out0, norm0 = leave[1](ids, grad_full1, x1, scale1, params[1], g_out1, full0)
    gbranch0 = branch_product(core_id, g_out0, *weights_b0[0], *weights_b0[1])
    scanned0 = scan_back(0, gbranch0, norm0, gate0, ssd0, state0, made0, beside0)
    grad_full0, pieces_a, pieces_b = reduce_back(
        scanned0, normed0, scale0, layer_in, g_out0, weights_a0, weights_b0, beside0
    )
    tiles = (2 * states + a_width) // LANE
    mine_a, give_a_, mine_b, give_b_, message, d_cv, d_cvb, d_gain, d_heads = on_chip(
        functools.partial(sum_kernel, inner, states, heads_tile),
        (shaped((shard + STEPS, a_width), BF16),) * 2
        + (shaped((shard, b_width), BF16),) * 2
        + (shaped((shard + 16 * tiles, LANE), BF16), shaped((4, inner)), shaped((1, inner)), shaped((1, inner)), shaped((8, LANE))),
        far_in=(1, 2), far_out=(0, 1, 2, 3),
    )(ids, *store["shares"], *[hold(p) for p in pieces_a], *pieces_b)
    close(message)
    messages = [hold(message)] + [sent_to(hold(message), "col", b) for b in range(1, cols)]
    their_a, their_b = swapped(hold(give_a_)), swapped(hold(give_b_))
    mine, give = leave[0](ids, hold(grad_full0), layer_in, scale0, params[0], g_out0, g_in1)
    close(mine, their_a, their_b, messages[1])
    other_grad = swapped(hold(give))
    d_value, d_step, d_gate, d_out = on_chip(
        join_kernel, (shaped((shard, inner)), shaped((heads, shard)), shaped((shard, inner)), shaped((inner, shard))),
        far_in=(1, 2, 3, 4), far_out=(0, 1, 2, 3),
    )(ids, hold(mine_a), their_a, mine_b, their_b)
    place = jnp.where(first, batch_order[0], core).reshape(1).astype(jnp.int32)
    input_grads = in_order_both(stack(place, mine, other_grad))
    close(d_value, input_grads, messages)
    mine_s, give_s, d_cs, d_csb, d_norm = on_chip(
        functools.partial(col_kernel, states),
        (shaped((shard, states), BF16),) * 2 + (shaped((4, 2 * states)), shaped((1, 2 * states)), shaped((1, width))),
    )(ids, store["state"], *[hold(m) for m in messages])
    their_s = swapped(give_s)
    d_state = jnp.concatenate([pick_mine(mine_s, their_s), pick_mine(their_s, mine_s)], axis=1).astype(F32)

    return (
        store["outputs"][None],
        input_grads[None],
        d_norm,
        d_gate[None],
        d_value[None],
        d_step.T[None],
        d_state[None],
        d_cv[None],
        d_cvb,
        d_cs[None],
        d_csb,
        d_heads[0:1, :heads],
        d_heads[1:2, :heads],
        d_heads[5:6, :heads],
        d_gain,
        d_out[None],
    )


def solution(mesh):
    in_specs = (
        P(None, "row", None),
        P(None, "row", None),
        P(None, "row"),
        P(),
        P("pipe", None),
        P("pipe", "row", "col"),
        P("pipe", "row", "col"),
        P("pipe", "row", "col"),
        P("pipe", "row", None),
        P("pipe", None, "col"),
        P("pipe", "col"),
        P("pipe", None, None),
        P("pipe", None),
        P("pipe", "col"),
        P("pipe", "col"),
        P("pipe", "col"),
        P("pipe", "col"),
        P("pipe", "col", "row"),
    )
    out_specs = (
        P("pipe", None, "row", None),
        P("pipe", None, "row", None),
        P("pipe", None),
        P("pipe", "row", "col"),
        P("pipe", "row", "col"),
        P("pipe", "row", "col"),
        P("pipe", "row", None),
        P("pipe", None, "col"),
        P("pipe", "col"),
        P("pipe", None, None),
        P("pipe", None),
        P("pipe", "col"),
        P("pipe", "col"),
        P("pipe", "col"),
        P("pipe", "col"),
        P("pipe", "col", "row"),
    )
    return jax.shard_map(local, mesh=mesh, in_specs=in_specs, out_specs=out_specs, check_vma=False)
```

```python
import functools
import math

import jax
import jax.numpy as jnp
from jax import lax
from jax.experimental import pallas as pl
from jax.experimental.pallas import tpu as pltpu
from jax.sharding import PartitionSpec as P

EPSILON = 1e-05
LOG2E = math.log2(math.e)
LANE = 128
F32 = jnp.float32
BF16 = jnp.bfloat16
SMALL_ROWS = 16
LEAD = 16
VMEM_MIB = 16
TAPS_ROWS = 32
SMALL = 48
STEPS = 16
BLOCKS = 4


def dot_nn(a, b):
    return lax.dot_general(a, b, (((1,), (0,)), ((), ())), preferred_element_type=F32)


def dot_nt(a, b):
    return lax.dot_general(a, b, (((1,), (1,)), ((), ())), preferred_element_type=F32)


def dot_tn(a, b):
    return lax.dot_general(a, b, (((0,), (0,)), ((), ())), preferred_element_type=F32)


def dot_exact(a, b):
    return lax.dot_general(
        a, b, (((1,), (0,)), ((), ())), precision=lax.Precision.HIGHEST, preferred_element_type=F32
    )


def sigmoid(v):
    return 1.0 / (1.0 + jnp.exp(-v))


def split_pair(v):
    high = v.astype(BF16)
    return high, (v - high.astype(F32)).astype(BF16)


def on_chip(kernel, out_shapes, scratch=(), far_in=(), far_out=()):
    whole = pl.BlockSpec(memory_space=pltpu.VMEM)
    scalar = pl.BlockSpec(memory_space=pltpu.SMEM)
    single = not isinstance(out_shapes, tuple)
    shapes = (out_shapes,) if single else out_shapes
    shapes = tuple(pltpu.HBM(o.shape, o.dtype) if i in far_out else o for i, o in enumerate(shapes))

    def call(*operands):
        operands = [
            pltpu.with_memory_space_constraint(o, pltpu.HBM) if i in far_in else o for i, o in enumerate(operands)
        ]
        return pl.pallas_call(
            kernel,
            out_shape=shapes[0] if single else shapes,
            in_specs=[scalar if o.dtype == jnp.int32 else whole for o in operands],
            out_specs=whole if single else (whole,) * len(shapes),
            scratch_shapes=scratch,
            compiler_params=pltpu.CompilerParams(vmem_limit_bytes=VMEM_MIB * 1024 * 1024),
        )(*operands)

    return call


def shaped(shape, dtype=F32):
    return jax.ShapeDtypeStruct(shape, dtype)


def tile_of(q):
    return slice(q * LANE, (q + 1) * LANE)


def spread(columns, q, heads_tile, lane_head):
    first = q * heads_tile
    out = columns[:, first : first + 1]
    for i in range(1, heads_tile):
        out = jnp.where(lane_head == i, columns[:, first + i : first + i + 1], out)
    return out


def lane_heads(rows, heads_tile):
    lanes = lax.broadcasted_iota(jnp.int32, (rows, LANE), 1)
    return lanes // (LANE // heads_tile)


def tri_mask(tokens, seg_col, seg_row, transposed):
    first = lax.broadcasted_iota(jnp.int32, (tokens, tokens), 0)
    second = lax.broadcasted_iota(jnp.int32, (tokens, tokens), 1)
    order = first <= second if transposed else first >= second
    return order & (seg_col == seg_row)


def pack_a_kernel(core_ref, value_ref, state_ref, step_ref, keep_ref, give_ref):
    shard, half = value_ref.shape[0], value_ref.shape[1] // 2
    heads = step_ref.shape[0]
    core = core_ref[0]
    for ref, place in ((keep_ref, core), (give_ref, 1 - core)):
        ref[:shard, :half] = value_ref[:, pl.ds(pl.multiple_of(place * half, LANE), half)]
        ref[:shard, half:] = state_ref[:, pl.ds(pl.multiple_of(place * LANE, LANE), LANE)]
        ref[shard:, :] = jnp.zeros((STEPS, ref.shape[1]), BF16)
        ref[shard : shard + heads, :shard] = step_ref[...]


def pack_b_kernel(core_ref, gate_ref, out_ref, keep_ref, give_ref):
    half = gate_ref.shape[1] // 2
    core = core_ref[0]
    for ref, place in ((keep_ref, core), (give_ref, 1 - core)):
        ref[:, :half] = gate_ref[:, pl.ds(pl.multiple_of(place * half, LANE), half)]
        ref[:, half:] = out_ref[pl.ds(pl.multiple_of(place * half, LANE), half), :].astype(F32).T.astype(BF16)


def enter_kernel(
    inner, heads_tile, places, core_ref, x_ref, before_ref, small_ref, aux_ref, *refs,
):
    taps_ref, heads_ref, gain_ref, _ = views(small_ref, places)
    mine, other = refs[:BLOCKS], refs[BLOCKS : 2 * BLOCKS]
    (
        normed_ref, scale_ref, z_ref, conv_ref, value_ref, scaled_ref, bc_ref, step_ref, cum_ref, cumt_ref, lead_ref,
        carry_ref, msg_ref, leadu_ref,
    ) = refs[2 * BLOCKS :]
    tokens, width = x_ref.shape
    half = inner // 2
    conv_width = conv_ref.shape[1]
    for ref, at in ((before_ref, slice(0, LEAD)), (x_ref, slice(LEAD, LEAD + tokens))):
        x = ref[...].astype(F32)
        scale = lax.rsqrt(jnp.mean(x * x, axis=1, keepdims=True) + EPSILON)
        normed_ref[at, :] = (x * scale * gain_ref[0:1, :]).astype(BF16)
    scale_ref[...] = jnp.broadcast_to(scale, scale_ref.shape)
    core = core_ref[0]
    block = width // BLOCKS
    step = None
    for pieces, place in ((mine, core), (other, 1 - core)):
        z = None
        for i in range(BLOCKS):
            normed = normed_ref[:, i * block : (i + 1) * block]
            term = dot_nn(normed, pieces[i][:block, :])
            z = term if z is None else z + term
            if pieces is mine:
                term = dot_nt(normed, pieces[i][block:, :block])
                step = term if step is None else step + term
        z_ref[:, pl.ds(pl.multiple_of(place * half, LANE), half)] = z[:, :half]
        z_ref[:, pl.ds(pl.multiple_of(inner + place * LANE, LANE), LANE)] = z[:, half:]
    z_ref[:, conv_width:] = jnp.zeros((z_ref.shape[0], LANE), F32)
    z_ref[:, conv_width : conv_width + STEPS] = step
    aux = aux_ref[...]
    raw = z_ref[LEAD:, conv_width:] + heads_ref[0:1, :]
    step = jnp.maximum(raw, 0.0) + jnp.log1p(jnp.exp(-jnp.abs(raw)))
    rates = -step * jnp.exp(heads_ref[1:2, :])
    rows = lax.broadcasted_iota(jnp.int32, (tokens, tokens), 0)
    cols = lax.broadcasted_iota(jnp.int32, (tokens, tokens), 1)
    cum = dot_exact((rows >= cols).astype(F32), rates) * LOG2E
    lead = aux[:, 5:6] * jnp.exp2(cum[tokens - 1 : tokens, :] - cum)
    carry = aux[:, 4:5] * jnp.exp2(cum)
    step_ref[...] = step
    cum_ref[...] = cum
    cumt_ref[...] = cum.T
    lead_ref[...] = lead
    carry_ref[...] = carry
    lane_head = lane_heads(tokens, heads_tile)
    for q in range(conv_width // LANE):
        at = tile_of(q)
        acc = taps_ref[4:5, at] + taps_ref[3:4, at] * z_ref[LEAD:, at]
        for j in range(3):
            shifted = z_ref[LEAD - 3 + j : LEAD - 3 + j + tokens, at]
            acc = acc + taps_ref[j : j + 1, at] * (aux[:, j : j + 1] * shifted)
        conv_ref[:, at] = acc
        value = acc * sigmoid(acc)
        if q < inner // LANE:
            value_ref[:, at] = value
            scaled = spread(step, q, heads_tile, lane_head) * value
            scaled_ref[:, at] = scaled.astype(BF16)
            leadu_ref[:, at] = (spread(lead, q, heads_tile, lane_head) * scaled).astype(BF16)
        else:
            bc_ref[:, tile_of(q - inner // LANE)] = value.astype(BF16)
    msg_ref[0:LANE, :] = dot_tn(bc_ref[:, :LANE], leadu_ref[...]).astype(BF16)
    put_through(msg_ref, carry[tokens - 1 : tokens, :], inner, heads_tile)


def enter_first_kernel(
    inner, heads_tile, places, core_ref, x_ref, before_ref, small_ref, seg_ref, seg_before_ref, *refs,
):
    weights, refs = refs[: 2 * BLOCKS], refs[2 * BLOCKS :]
    aux_ref, segt_ref, *made, seg_ext_ref, leadu_ref = refs
    tokens = x_ref.shape[0]
    seg = seg_ref[...]
    seg_ext_ref[0:LEAD, :] = seg_before_ref[...]
    seg_ext_ref[LEAD:, :] = seg
    lanes = lax.broadcasted_iota(jnp.int32, (tokens, LANE), 1)
    flags = jnp.where(lanes == 3, seg, 0.0)
    for j in range(3):
        same = (seg_ext_ref[LEAD - 3 + j : LEAD - 3 + j + tokens, :] == seg).astype(F32)
        flags = jnp.where(lanes == j, same, flags)
    flags = jnp.where(lanes == 4, (seg == seg_ext_ref[LEAD - 1 : LEAD, :]).astype(F32), flags)
    flags = jnp.where(lanes == 5, (seg == seg[tokens - 1 :, :]).astype(F32), flags)
    aux_ref[...] = flags
    segt_ref[...] = seg.T[0:8, :]
    enter_kernel(
        inner, heads_tile, places, core_ref, x_ref, before_ref, small_ref, aux_ref, *weights, *made, leadu_ref
    )


def views(ref, places):
    return tuple(ref.at[:, p] for p in places)


def put_through(msg_ref, last, inner, heads_tile):
    msg_ref[LANE:, :] = jnp.zeros((SMALL_ROWS, inner), BF16)
    lane_row = lane_heads(1, heads_tile)
    for q in range(inner // LANE):
        high, low = split_pair(spread(last, q, heads_tile, lane_row))
        msg_ref[LANE : LANE + 1, tile_of(q)] = high
        msg_ref[LANE + 1 : LANE + 2, tile_of(q)] = low


def wide_kernel(offset, lead, core_ref, a_ref, *refs):
    mine, other = refs[:BLOCKS], refs[BLOCKS : 2 * BLOCKS]
    out_ref = refs[2 * BLOCKS]
    core = core_ref[0]
    half = out_ref.shape[1] // 2
    block = a_ref.shape[1] // BLOCKS
    for pieces, place in ((mine, core), (other, 1 - core)):
        total = None
        for i in range(BLOCKS):
            term = dot_nn(a_ref[lead:, i * block : (i + 1) * block], pieces[i][:, offset : offset + half])
            total = term if total is None else total + term
        out_ref[:, pl.ds(pl.multiple_of(place * half, LANE), half)] = total


def intra_kernel(
    inner, heads_tile, places, scaled_ref, value_ref, bc_ref, cum_ref, cumt_ref, aux_ref, segt_ref, small_ref,
    out_ref,
):
    heads_ref = views(small_ref, places)[1]
    tokens = scaled_ref.shape[0]
    scores = dot_nt(bc_ref[:, LANE:], bc_ref[:, :LANE])
    scores = jnp.where(tri_mask(tokens, aux_ref[:, 3:4], segt_ref[0:1, :], False), scores, 0.0)
    lane_head = lane_heads(tokens, heads_tile)
    lane_row = lane_heads(1, heads_tile)
    for q in range(inner // LANE):
        at = tile_of(q)
        total = spread(heads_ref[2:3, :], q, heads_tile, lane_row) * value_ref[:, at]
        scaled = scaled_ref[:, at]
        for i in range(heads_tile):
            h = q * heads_tile + i
            gap = jnp.minimum(cum_ref[:, h : h + 1] - cumt_ref[h : h + 1, :], 0.0)
            mixed = (jnp.exp2(gap) * scores).astype(BF16)
            total = total + jnp.where(lane_head == i, dot_nn(mixed, scaled), 0.0)
        out_ref[:, at] = total


def enter_states(messages):
    state = None
    for message in reversed(messages):
        own = message[0:LANE, :].astype(F32)
        through = message[LANE : LANE + 1, :].astype(F32) + message[LANE + 1 : LANE + 2, :].astype(F32)
        state = own if state is None else own + through * state
    return state


def gate_kernel(
    inner, heads_tile, places, count, with_grad, core_ref, intra_ref, bc_ref, carry_ref, gate_ref, small_ref, *refs
):
    gain_ref = views(small_ref, places)[3]
    messages = refs[:count]
    mine, other = refs[count : count + BLOCKS], refs[count + BLOCKS : count + 2 * BLOCKS]
    refs = refs[count + 2 * BLOCKS :]
    if with_grad:
        branch_grad_ref, refs = refs[0], refs[1:]
        ssd_ref, state_ref, msg_ref, sums_ref, gated_ref = refs
    else:
        ssd_ref, state_ref, msg_ref, gated_ref = refs
    tokens = intra_ref.shape[0]
    state = enter_states([m[...] for m in messages]).astype(BF16)
    state_ref[...] = state
    inter = dot_nn(bc_ref[:, LANE:], state)
    lane_head = lane_heads(tokens, heads_tile)
    carry = carry_ref[...]
    squares = jnp.zeros((tokens, LANE), F32)
    products = jnp.zeros((tokens, LANE), F32)
    for q in range(inner // LANE):
        at = tile_of(q)
        ssd = intra_ref[:, at] + spread(carry, q, heads_tile, lane_head) * inter[:, at]
        ssd_ref[:, at] = ssd
        gate = gate_ref[:, at]
        gated = ssd * (gate * sigmoid(gate))
        squares = squares + gated * gated
        scaled = gated * gain_ref[0:1, at]
        gated_ref[:, at] = scaled.astype(BF16)
        if with_grad:
            products = products + scaled * branch_grad_ref[:, at]
    half = inner // 2
    core = core_ref[0]
    low = gated_ref[:, pl.ds(pl.multiple_of(core * half, LANE), half)]
    high = gated_ref[:, pl.ds(pl.multiple_of((1 - core) * half, LANE), half)]
    block = mine[0].shape[0]
    for i in range(BLOCKS):
        part = dot_nt(low, mine[i][:, half:]) + dot_nt(high, other[i][:, half:])
        msg_ref[:, i * block : (i + 1) * block] = part.astype(BF16)
    total = jnp.sum(squares, axis=1, keepdims=True)
    lanes = lax.broadcasted_iota(jnp.int32, (tokens, LANE), 1)
    if with_grad:
        packed = jnp.where(lanes == 0, total, 0.0)
        packed = packed + jnp.where(lanes == 1, jnp.sum(products, axis=1, keepdims=True), 0.0)
        sums_ref[...] = packed.T[0:8, :]
    else:
        rest = total - total.astype(BF16).astype(F32)
        packed = jnp.where(lanes == 0, total, jnp.where(lanes == 1, rest, 0.0))
        msg_ref[:, BLOCKS * block :] = packed.astype(BF16)


def next_kernel(norm_width, full_ref, x_ref, out_ref, tail_ref):
    tokens, width = x_ref.shape
    squares = full_ref[:, width : width + 1].astype(F32) + full_ref[:, width + 1 : width + 2].astype(F32)
    rho = lax.rsqrt(squares / norm_width + EPSILON)
    out_ref[...] = (x_ref[...].astype(F32) + rho * full_ref[:, :width].astype(F32)).astype(BF16)
    tail_ref[...] = out_ref[tokens - LEAD :, :]


def norm_kernel(norm_width, *refs):
    parts = [r[...] for r in refs[:-1]]
    while len(parts) > 1:
        parts = [parts[i] + parts[i + 1] for i in range(0, len(parts), 2)]
    total = parts[0]
    rows = lax.broadcasted_iota(jnp.int32, total.shape, 0)
    total = jnp.where(rows == 0, lax.rsqrt(total / norm_width + EPSILON), total)
    total = jnp.concatenate([total, jnp.zeros((LANE - total.shape[0], total.shape[1]), F32)], axis=0)
    refs[-1][...] = total.T


def ungate_kernel(
    inner, heads_tile, places, norm_width, branch_grad_ref, norm_ref, gate_ref, ssd_ref, small_ref, carry_ref, bc_ref,
    gssd_ref, ggate_ref, branch_ref, msg_ref, ggain_ref, cg_ref,
):
    gain_ref = views(small_ref, places)[3]
    tokens = branch_grad_ref.shape[0]
    rho = norm_ref[:, 0:1]
    pull = norm_ref[:, 1:2] * (rho * rho * rho / norm_width)
    lane_head = lane_heads(tokens, heads_tile)
    carry = carry_ref[...]
    ggain_ref[...] = jnp.zeros(ggain_ref.shape, F32)
    for q in range(inner // LANE):
        at = tile_of(q)
        gate = gate_ref[:, at]
        sig = sigmoid(gate)
        ssd = ssd_ref[:, at]
        gated = ssd * (gate * sig)
        grad = branch_grad_ref[:, at]
        gain = gain_ref[0:1, at]
        normed = gated * rho
        ggain_ref[0:1, at] = jnp.sum(grad * normed, axis=0, keepdims=True)
        branch_ref[:, at] = (normed * gain).astype(BF16)
        ggated = rho * (gain * grad) - gated * pull
        gssd = ggated * (gate * sig)
        gssd_ref[:, at] = gssd
        ggate_ref[:, at] = (ggated * ssd * (sig * (1.0 + gate * (1.0 - sig)))).astype(BF16)
        cg_ref[:, at] = (spread(carry, q, heads_tile, lane_head) * gssd).astype(BF16)
    msg_ref[0:LANE, :] = dot_tn(bc_ref[:, LANE:], cg_ref[...]).astype(BF16)
    put_through(msg_ref, carry[tokens - 1 : tokens, :], inner, heads_tile)


def intra_grad_kernel(
    inner, heads_tile, scaled_ref, gssd_ref, bc_ref, cum_ref, cumt_ref, aux_ref, segt_ref,
    gscaled_ref, gbc_ref, gcum_ref, sums_ref,
):
    tokens = scaled_ref.shape[0]
    mask = tri_mask(tokens, aux_ref[:, 3:4], segt_ref[0:1, :], True)
    scores = jnp.where(mask, dot_nt(bc_ref[:, :LANE], bc_ref[:, LANE:]), 0.0)
    lane_head = lane_heads(tokens, heads_tile)
    gscores = jnp.zeros((tokens, tokens), F32)
    gcum_ref[...] = jnp.zeros(gcum_ref.shape, F32)
    sums_ref[...] = jnp.zeros(sums_ref.shape, F32)
    for q in range(inner // LANE):
        at = tile_of(q)
        grad = gssd_ref[:, at].astype(BF16)
        scaled = scaled_ref[:, at]
        total = jnp.zeros((tokens, LANE), F32)
        for i in range(heads_tile):
            h = q * heads_tile + i
            gap = jnp.minimum(cumt_ref[h : h + 1, :] - cum_ref[:, h : h + 1], 0.0)
            decay = jnp.exp2(gap)
            mixed = decay * scores
            picked = jnp.where(lane_head == i, scaled, jnp.zeros_like(scaled))
            gmixed = dot_nt(picked, grad)
            total = total + jnp.where(lane_head == i, dot_nn(mixed.astype(BF16), grad), 0.0)
            product = gmixed * mixed
            sums_ref[h : h + 1, :] = jnp.sum(product, axis=0, keepdims=True)
            gcum_ref[:, h : h + 1] = -jnp.sum(product, axis=1, keepdims=True)
            gscores = gscores + gmixed * decay
        gscaled_ref[:, at] = total
    gscores = jnp.where(mask, gscores, 0.0)
    gbc_ref[:, :LANE] = dot_nn(gscores.astype(BF16), bc_ref[:, LANE:])
    gbc_ref[:, LANE:] = dot_nn(gscores.T.astype(BF16), bc_ref[:, :LANE])
    gcum_ref[...] = gcum_ref[...] + sums_ref[...].T


def inter_grad_kernel(
    inner, heads_tile, places, count, state_ref, scaled_ref, value_ref, gssd_ref, gscaled_ref, bc_ref, gbc_ref, gcum_ref,
    step_ref, lead_ref, carry_ref, z_ref, conv_ref, aux_ref, small_ref, ggain_ref, *refs,
):
    taps_ref, heads_ref, _, _ = views(small_ref, places)
    messages = refs[:count]
    gpre_ref, gstep_ref, gtaps_ref, em_ref, leadu_ref, cg_ref, gain_ref, lose_ref, gsize_ref = refs[count:]
    tokens = scaled_ref.shape[0]
    width = conv_ref.shape[1]
    aux = aux_ref[...]
    adjoint = enter_states([m[...] for m in messages])
    adjoint_low = adjoint.astype(BF16)
    state = state_ref[...]
    from_adjoint = dot_nn(bc_ref[:, :LANE], adjoint_low)
    from_state = dot_nn(bc_ref[:, LANE:], state)
    overlap = jnp.sum(adjoint * state.astype(F32), axis=0, keepdims=True)
    lane_head = lane_heads(tokens, heads_tile)
    lane_row = lane_heads(1, heads_tile)
    step = step_ref[...]
    lead = lead_ref[...]
    carry = carry_ref[...]
    em_ref[0:8, :] = jnp.zeros((8, LANE), F32)
    em_ref[8 + tokens :, :] = jnp.zeros((8, LANE), F32)
    gpre_ref[0:8, :] = jnp.zeros((8, width), F32)
    gtaps_ref[...] = jnp.zeros(gtaps_ref.shape, F32)

    def through_conv(q, grad):
        at = tile_of(q)
        conv = conv_ref[:, at]
        sig = sigmoid(conv)
        e = grad * (sig * (1.0 + conv * (1.0 - sig)))
        gtaps_ref[4:5, at] = jnp.sum(e, axis=0, keepdims=True)
        gtaps_ref[3:4, at] = jnp.sum(e * z_ref[LEAD:, at], axis=0, keepdims=True)
        total = None
        for j in range(3):
            masked = aux[:, j : j + 1] * e
            shifted = z_ref[LEAD - 3 + j : LEAD - 3 + j + tokens, at]
            gtaps_ref[j : j + 1, at] = jnp.sum(masked * shifted, axis=0, keepdims=True)
            em_ref[8 : 8 + tokens, :] = masked
            term = taps_ref[j : j + 1, at] * em_ref[3 - j : 11 - j + tokens, :]
            total = term if total is None else total + term
        gpre_ref[8:LEAD, at] = total[0:8, :]
        gpre_ref[LEAD:, at] = total[8:, :] + taps_ref[3:4, at] * e

    for q in range(inner // LANE):
        at = tile_of(q)
        scaled = scaled_ref[:, at].astype(F32)
        grad = gssd_ref[:, at]
        value = value_ref[:, at]
        leads = spread(lead, q, heads_tile, lane_head)
        carries = spread(carry, q, heads_tile, lane_head)
        pushed = leads * from_adjoint[:, at]
        gscaled = gscaled_ref[:, at] + pushed
        carried = carries * grad
        leadu_ref[:, at] = (leads * scaled).astype(BF16)
        cg_ref[:, at] = carried.astype(BF16)
        gain_ref[:, at] = (carried * from_state[:, at]).astype(BF16)
        lose_ref[:, at] = (scaled * pushed).astype(BF16)
        gsize_ref[:, at] = (gscaled * value).astype(BF16)
        gtaps_ref[5:6, at] = jnp.sum(grad * value, axis=0, keepdims=True)
        gvalue = spread(step, q, heads_tile, lane_head) * gscaled
        gvalue = gvalue + spread(heads_ref[2:3, :], q, heads_tile, lane_row) * grad
        through_conv(q, gvalue)
    gb = gbc_ref[:, :LANE] + dot_nt(leadu_ref[...], adjoint_low)
    gc = gbc_ref[:, LANE:] + dot_nt(cg_ref[...], state)
    through_conv(inner // LANE, gb)
    through_conv(inner // LANE + 1, gc)
    head_of = lax.broadcasted_iota(jnp.int32, (inner, LANE), 0) // (LANE // heads_tile)
    pick = (head_of == lax.broadcasted_iota(jnp.int32, (inner, LANE), 1)).astype(BF16)
    lose = dot_nn(lose_ref[...], pick)
    gcum = gcum_ref[...] + dot_nn(gain_ref[...], pick) - lose
    high, low = split_pair(overlap)
    ends = dot_nn(jnp.broadcast_to(high, (8, inner)), pick) + dot_nn(jnp.broadcast_to(low, (8, inner)), pick)
    last = carry[tokens - 1 : tokens, :] * ends[0:1, :] + jnp.sum(lose, axis=0, keepdims=True)
    row_of = lax.broadcasted_iota(jnp.int32, (tokens, LANE), 0)
    gcum = gcum + jnp.where(row_of == tokens - 1, last, 0.0)
    rows = lax.broadcasted_iota(jnp.int32, (tokens, tokens), 0)
    cols = lax.broadcasted_iota(jnp.int32, (tokens, tokens), 1)
    grate = dot_exact((rows <= cols).astype(F32), gcum)
    speed = jnp.exp(heads_ref[1:2, :])
    gsize = dot_nn(gsize_ref[...], pick) - speed * grate
    raw = z_ref[LEAD:, width:] + heads_ref[0:1, :]
    graw = gsize * sigmoid(raw)
    gstep_ref[...] = graw.astype(BF16)
    gtaps_ref[6:7, :inner] = ggain_ref[0:1, :]
    gtaps_ref[7:8, 0:LANE] = jnp.sum(graw, axis=0, keepdims=True)
    gtaps_ref[7:8, LANE : 2 * LANE] = jnp.sum(grate * (-speed * step), axis=0, keepdims=True)


def give_b_kernel(
    core_ref, ggate_ref, normed_ref, g_out_ref, branch_ref,
    other_b_ref, gg_mine_ref, gg_other_ref, normed_t_ref, g_out_t_ref,
):
    width = g_out_ref.shape[1]
    half = ggate_ref.shape[1] // 2
    core = core_ref[0]
    gg_mine_ref[...] = ggate_ref[:, pl.ds(pl.multiple_of(core * half, LANE), half)]
    gg_other_ref[...] = ggate_ref[:, pl.ds(pl.multiple_of((1 - core) * half, LANE), half)]
    block = width // BLOCKS
    for i in range(BLOCKS):
        at = slice(i * block, (i + 1) * block)
        normed_t_ref[at, :] = normed_ref[LEAD:, at].astype(F32).T.astype(BF16)
        g_out_t_ref[at, :] = g_out_ref[:, at].astype(F32).T.astype(BF16)
    other_b_ref[:, :half] = dot_nn(normed_t_ref[...], gg_other_ref[...]).astype(BF16)
    branch = branch_ref[:, pl.ds(pl.multiple_of((1 - core) * half, LANE), half)]
    other_b_ref[:, half:] = dot_nn(g_out_t_ref[...], branch).astype(BF16)


def keep_b_kernel(core_ref, normed_t_ref, g_out_t_ref, branch_ref, gg_mine_ref, their_ref, *refs):
    size = normed_t_ref.shape[0] // len(refs)
    half = gg_mine_ref.shape[1]
    branch = branch_ref[:, pl.ds(pl.multiple_of(core_ref[0] * half, LANE), half)]
    for i, ref in enumerate(refs):
        at = slice(i * size, (i + 1) * size)
        part = dot_nn(normed_t_ref[at, :], gg_mine_ref[...]) + their_ref[at, :half].astype(F32)
        ref[:, :half] = part.astype(BF16)
        part = dot_nn(g_out_t_ref[at, :], branch) + their_ref[at, half:].astype(F32)
        ref[:, half:] = part.astype(BF16)


def taps_rows(taps, wide):
    left, right = taps[:, :wide], taps[:, wide:]
    rows = []
    for part in (left, right):
        high = part.astype(BF16).astype(F32)
        rows += [high, part - high]
    return jnp.concatenate(rows, axis=0).astype(BF16)


def gain_rows(gain, wide):
    high = gain.astype(BF16).astype(F32)
    index = lax.broadcasted_iota(jnp.int32, (16, wide), 0)
    out = jnp.zeros((16, wide), F32)
    count = -(-gain.shape[1] // wide)
    for i in range(count):
        for base, part in ((0, high), (8, gain - high)):
            piece = part[:, i * wide : (i + 1) * wide]
            if piece.shape[1] < wide:
                piece = jnp.concatenate([piece, jnp.zeros((1, wide - piece.shape[1]), F32)], axis=1)
            out = jnp.where(index == base + i, piece, out)
    return out.astype(BF16)


def give_a_kernel(
    core_ref, gpre_ref, next_ref, gstep_ref, normed_t_ref, gtaps_ref, other_a_ref, ga_mine_ref, ga_other_ref, glow_ref
):
    tokens, width = glow_ref.shape
    inner = width - 2 * LANE
    half = inner // 2
    core = core_ref[0]
    cut = tokens - LEAD
    glow_ref[:cut, :] = gpre_ref[LEAD : LEAD + cut, :].astype(BF16)
    glow_ref[cut:, :] = (gpre_ref[LEAD + cut :, :] + next_ref[...]).astype(BF16)
    for ga_ref, place in ((ga_mine_ref, core), (ga_other_ref, 1 - core)):
        ga_ref[:, :half] = glow_ref[:, pl.ds(pl.multiple_of(place * half, LANE), half)]
        ga_ref[:, half:] = glow_ref[:, pl.ds(pl.multiple_of(inner + place * LANE, LANE), LANE)]
    rows, wide = normed_t_ref.shape[0], other_a_ref.shape[1]
    other_a_ref[:rows, :] = dot_nn(normed_t_ref[...], ga_other_ref[...]).astype(BF16)
    steps = step_grads(gstep_ref, normed_t_ref)
    for i in range(rows // wide):
        other_a_ref[rows + STEPS * i : rows + STEPS * (i + 1), :] = steps[:, i * wide : (i + 1) * wide].astype(BF16)
    other_a_ref[rows + STEPS * (rows // wide) :, :] = taps_rows(gtaps_ref[...], wide)


def step_grads(gstep_ref, normed_t_ref):
    return dot_nt(gstep_ref[...].astype(F32).T[0:STEPS, :].astype(BF16), normed_t_ref[...])


def keep_a_kernel(normed_t_ref, ga_mine_ref, gstep_ref, their_ref, gtaps_ref, ggain_ref, *refs):
    rows = normed_t_ref.shape[0]
    size = rows // len(refs)
    wide = ga_mine_ref.shape[1]
    groups = [
        their_ref[rows + STEPS * i : rows + STEPS * (i + 1), :].astype(F32) for i in range(rows // wide + TAPS_ROWS // STEPS)
    ]
    steps = step_grads(gstep_ref, normed_t_ref) + jnp.concatenate(groups[: rows // wide], axis=1)
    taps = jnp.concatenate([t[0:8] + t[8:16] for t in groups[rows // wide :]], axis=1)[:, : gtaps_ref.shape[1]]
    small = taps_rows(taps + gtaps_ref[...], wide)
    gain = gain_rows(ggain_ref[0:1, :], wide)
    below = size + STEPS
    for i, ref in enumerate(refs):
        at = slice(i * size, (i + 1) * size)
        ref[:size, :] = (dot_nn(normed_t_ref[at, :], ga_mine_ref[...]) + their_ref[at, :].astype(F32)).astype(BF16)
        ref[size:below, :] = jnp.zeros((STEPS, wide), BF16)
        ref[size:below, :size] = steps[:, at].astype(BF16)
        ref[below : below + TAPS_ROWS, :] = small
        ref[below + TAPS_ROWS :, :] = gain


def pull_kernel(ga_mine_ref, ga_other_ref, gstep_ref, gg_mine_ref, gg_other_ref, x_ref, scale_ref, *refs):
    mine_a, other_a, mine_b, other_b = (refs[i * BLOCKS : (i + 1) * BLOCKS] for i in range(4))
    msg_ref, ggain_ref = refs[4 * BLOCKS :]
    half = gg_mine_ref.shape[1]
    block = mine_b[0].shape[0]
    scale = scale_ref[:, 0:1]
    ggain_ref[...] = jnp.zeros(ggain_ref.shape, F32)
    for i in range(BLOCKS):
        at = slice(i * block, (i + 1) * block)
        part = dot_nt(ga_mine_ref[...], mine_a[i][:block, :])
        part = part + dot_nt(ga_other_ref[...], other_a[i][:block, :])
        part = part + dot_nn(gstep_ref[:, :STEPS], mine_a[i][block:, :block])
        part = part + dot_nt(gg_mine_ref[...], mine_b[i][:, :half])
        part = part + dot_nt(gg_other_ref[...], other_b[i][:, :half])
        msg_ref[:, at] = part.astype(BF16)
        ggain_ref[0:1, at] = jnp.sum(part * (x_ref[:, at].astype(F32) * scale), axis=0, keepdims=True)


def leave_kernel(norm_width, places, below, ordered, ids_ref, full_ref, x_ref, scale_ref, small_ref, g_out_ref, *refs):
    gain_ref = views(small_ref, places)[2]
    tokens, width = x_ref.shape
    scale = scale_ref[:, 0:1]
    x = x_ref[...].astype(F32)
    pulled = full_ref[...].astype(F32) * gain_ref[0:1, :]
    slope = jnp.sum(pulled * x, axis=1, keepdims=True) * (scale * scale * scale / width)
    grad = g_out_ref[...].astype(F32) + scale * pulled - x * slope
    core = ids_ref[0]

    def put(ref):
        put_blocks(ordered, ids_ref[1], ref, slice(None), grad)

    if below:
        raw_ref, grad_ref, low_ref, norm_ref = refs
        put(grad_ref)
        low = grad.astype(BF16)
        low_ref[...] = low
        dots = jnp.sum(low.astype(F32) * raw_ref[:, :width].astype(F32), axis=1, keepdims=True)
        squares = raw_ref[:, width : width + 1].astype(F32) + raw_ref[:, width + 1 : width + 2].astype(F32)
        lanes = lax.broadcasted_iota(jnp.int32, (tokens, LANE), 1)
        norm_ref[...] = jnp.where(lanes == 0, lax.rsqrt(squares / norm_width + EPSILON), dots)
        return
    above_ref, mine_ref, give_ref = refs

    @pl.when(core == 0)
    def _():
        put(mine_ref)
        give_ref[...] = above_ref[...]

    @pl.when(core != 0)
    def _():
        put(give_ref)
        mine_ref[...] = above_ref[...]


def put_blocks(ordered, row, ref, at, value):
    block = value.shape[1] // BLOCKS
    for i in range(BLOCKS):
        part = value[:, i * block : (i + 1) * block]
        if ordered:
            ref[at, pl.ds(pl.multiple_of((row ^ i) * block, LANE), block)] = part
        else:
            ref[at, i * block : (i + 1) * block] = part


def outputs_kernel(ordered, ids_ref, x_ref, norm_ref, *refs):
    chunks, (mine_ref, give_ref) = refs[:-2], refs[-2:]
    size = chunks[0].shape[0]
    for b, chunk in enumerate(chunks):
        at = pl.ds(pl.multiple_of((ids_ref[2] ^ b) * size, size), size)
        below = x_ref[at, :]
        above = (below.astype(F32) + norm_ref[at, 0:1] * chunk[...].astype(F32)).astype(BF16)
        for first, second, chosen in ((mine_ref, give_ref, 0), (give_ref, mine_ref, 1)):

            @pl.when(ids_ref[0] == chosen)
            def _():
                put_blocks(ordered, ids_ref[1], first, at, below)
                put_blocks(ordered, ids_ref[1], second, at, above)


def stack_kernel(place_ref, mine_ref, their_ref, out_ref):
    out_ref[place_ref[0]] = mine_ref[...]
    out_ref[1 - place_ref[0]] = their_ref[...]


def sum_kernel(inner, states, heads_tile, ids_ref, share_a_ref, share_b_ref, *refs):
    mine_a_ref, give_a_ref, mine_b_ref, give_b_ref, msg_ref, taps_ref, bias_ref, gain_ref, heads_ref = refs[-9:]
    pieces = refs[:-9]
    count = len(pieces) // 2
    a = functools.reduce(lambda u, v: u + v, [p[...].astype(F32) for p in pieces[:count]])
    b = functools.reduce(lambda u, v: u + v, [p[...].astype(F32) for p in pieces[count:]])
    shard = mine_b_ref.shape[0]
    half = inner // 2
    below = shard + STEPS
    msg_ref[:shard, :] = a[:shard, half:].astype(BF16)

    def small(part):
        vec = jnp.concatenate([part[0:8] + part[8:16], part[16:24] + part[24:32]], axis=1)
        taps_ref[...] = vec[0:4, :inner]
        bias_ref[...] = vec[4:5, :inner]
        gain_ref[...] = vec[6:7, :inner]
        head_of = lax.broadcasted_iota(jnp.int32, (inner, LANE), 0) // (LANE // heads_tile)
        pick = (head_of == lax.broadcasted_iota(jnp.int32, (inner, LANE), 1)).astype(F32)
        heads_ref[0:1, :] = vec[7:8, 0:LANE]
        heads_ref[1:2, :] = vec[7:8, LANE : 2 * LANE]
        heads_ref[2:8, :] = dot_exact(vec[:, :inner], pick)[2:8, :]
        rest = jnp.concatenate(
            [vec[:, inner : inner + 2 * states], part[TAPS_ROWS : TAPS_ROWS + 8] + part[TAPS_ROWS + 8 :]], axis=1
        )
        high = rest.astype(BF16).astype(F32)
        both = jnp.concatenate([high, rest - high], axis=0).astype(BF16)
        for i in range(rest.shape[1] // LANE):
            msg_ref[shard + 16 * i : shard + 16 * (i + 1), :] = both[:, tile_of(i)]

    @pl.when(ids_ref[0] == 0)
    def _():
        mine_a_ref[...] = a[:below].astype(BF16)
        give_a_ref[...] = share_a_ref[:below, :].astype(BF16)
        mine_b_ref[...] = b.astype(BF16)
        give_b_ref[...] = share_b_ref[...].astype(BF16)
        small(a[below:])

    @pl.when(ids_ref[0] != 0)
    def _():
        mine_a_ref[...] = share_a_ref[:below, :].astype(BF16)
        give_a_ref[...] = a[:below].astype(BF16)
        mine_b_ref[...] = share_b_ref[...].astype(BF16)
        give_b_ref[...] = b.astype(BF16)
        small(share_a_ref[below:, :])


def col_kernel(states, ids_ref, state_ref, *refs):
    mine_ref, give_ref, taps_ref, bias_ref, gain_ref = refs[-5:]
    parts = [r[...].astype(F32) for r in refs[:-5]]
    while len(parts) > 1:
        parts = [parts[i] + parts[i + 1] for i in range(0, len(parts), 2)]
    shard = mine_ref.shape[0]
    own, rest = parts[0][:shard].astype(BF16), parts[0][shard:]
    tiles = [rest[16 * i : 16 * i + 8] + rest[16 * i + 8 : 16 * (i + 1)] for i in range(rest.shape[0] // 16)]
    count = 2 * states // LANE
    for i in range(count):
        taps_ref[:, tile_of(i)] = tiles[i][0:4]
        bias_ref[:, tile_of(i)] = tiles[i][4:5]
    wide = len(tiles) - count
    for i in range(gain_ref.shape[1] // LANE):
        gain_ref[:, tile_of(i)] = tiles[count + i % wide][i // wide : i // wide + 1]
    for first, second, chosen in ((mine_ref, give_ref, 0), (give_ref, mine_ref, 1)):

        @pl.when(ids_ref[0] == chosen)
        def _():
            first[...] = own
            second[...] = state_ref[...].astype(BF16)


def join_kernel(ids_ref, mine_a_ref, their_a_ref, mine_b_ref, their_b_ref, value_ref, step_ref, gate_ref, out_ref):
    shard, half = value_ref.shape[0], value_ref.shape[1] // 2
    core = ids_ref[0]
    for a_ref, b_ref, place in ((mine_a_ref, mine_b_ref, core), (their_a_ref, their_b_ref, 1 - core)):
        at = pl.ds(pl.multiple_of(place * half, LANE), half)
        value_ref[:, at] = a_ref[:shard, :half].astype(F32)
        gate_ref[:, at] = b_ref[:, :half].astype(F32)
        out_ref[at, :] = b_ref[:, half:].astype(F32).T
    step_ref[...] = mine_a_ref[shard:, :shard].astype(F32)[: step_ref.shape[0], :]


def permute(block, axis, route):
    return lax.ppermute(block, axis, route)


def from_before(block, count, distance):
    return permute(block, "row", [(i, i + distance) for i in range(count - distance)])


def from_after(block, count, distance):
    return permute(block, "row", [(i + distance, i) for i in range(count - distance)])


def swapped(block):
    return permute(block, "pipe", [(0, 1), (1, 0)])


def exchanged(blocks, axis):
    return lax.all_to_all(blocks, axis, 0, 0)


def spread_out(block, axis):
    count = lax.axis_size(axis)
    return exchanged(jnp.broadcast_to(block[None], (count,) + block.shape), axis).reshape(
        (count * block.shape[0],) + block.shape[1:]
    )


def parts_sum(block, axis):
    count = lax.axis_size(axis)
    parts = exchanged(block.reshape((count, block.shape[0] // count) + block.shape[1:]), axis)
    return jnp.sum(parts.astype(F32), axis=0)


def sent_to(block, axis, flip):
    count = lax.axis_size(axis)
    return permute(block, axis, [(i, i ^ flip) for i in range(count)])


def relative_order(block, dim, axis, place=None):
    count = lax.axis_size(axis)
    size = block.shape[dim] // count
    place = lax.axis_index(axis) if place is None else place
    return jnp.concatenate(
        [lax.dynamic_slice_in_dim(block, (place ^ b) * size, size, dim) for b in range(count)], axis=dim
    )


class Phases:
    def __init__(self, token):
        self.token = token

    def hold(self, value):
        return lax.optimization_barrier((value, self.token))[0]

    def close(self, *values):
        self.token = lax.optimization_barrier((self.token,) + tuple(jax.tree.leaves(values)))[0]


def col_gather(block):
    return lax.all_gather(block, "col", axis=0, tiled=True)


def after(block, *others):
    return lax.optimization_barrier((block,) + others)[0]


def local(
    inputs, cotangent, segment_ids, batch_order, norm_gain, gate_proj, value_proj, step_proj, state_proj,
    conv_value, conv_value_bias, conv_state, conv_state_bias, step_bias, decay_log, skip_gain, gate_gain, out_proj,
):
    core = lax.axis_index("pipe")
    first = core == 0
    core_id = core.reshape(1).astype(jnp.int32)
    rows = lax.axis_size("row")
    row = lax.axis_index("row")
    tokens, width = inputs.shape[1], inputs.shape[2]
    inner = gate_proj.shape[2]
    heads = step_proj.shape[2]
    states = state_proj.shape[2] // 2
    heads_tile = LANE // (inner // heads)
    half = inner // 2
    conv_width = inner + 2 * states
    norm_width = inner * lax.axis_size("col")
    reach = max(rows // 2, 1)
    distances = range(1, reach + 1)
    group = rows // BLOCKS

    def pick_mine(a, b):
        return jnp.where(first, a, b)

    phases = Phases(core_id)
    hold, close = phases.hold, phases.close

    shard = gate_proj.shape[1]
    a_width, b_width = half + states, inner
    own_a, away_a = on_chip(pack_a_kernel, (shaped((shard + STEPS, a_width), BF16),) * 2, far_in=(1, 2, 3))(
        core_id, value_proj[0], state_proj[0], step_proj[0].T
    )
    close(away_a)
    take_a = swapped(hold(away_a))
    own_b, away_b = on_chip(pack_b_kernel, (shaped((shard, b_width), BF16),) * 2, far_in=(1, 2))(core_id, hold(gate_proj[0]), out_proj[0])
    close(take_a, away_b)

    def blocks_of(pieces):
        if pieces[0].shape[0] > shard and group > 1:
            made = []
            for i in range(BLOCKS):
                part = pieces[i * group : (i + 1) * group]
                steps = jnp.concatenate([p[shard:, :shard] for p in part], axis=1)
                steps = jnp.pad(steps, ((0, 0), (0, a_width - steps.shape[1])))
                made.append(jnp.concatenate([p[:shard] for p in part] + [steps], axis=0))
            return made
        return [jnp.concatenate(pieces[i * group : (i + 1) * group], axis=0) for i in range(BLOCKS)]

    near = 3 if rows == BLOCKS else rows

    def sent_near(block):
        return [block] + [sent_to(block, "row", b) for b in range(1, near)]

    def passed_on(pieces):
        if rows != BLOCKS:
            return []
        cut = -(-pieces[0].shape[0] // 32) * 16
        return [jnp.concatenate([sent_to(pieces[1][:cut], "row", 2), sent_to(pieces[2][cut:], "row", 1)], axis=0)]

    def both_cores(mine):
        return mine, [swapped(p) for p in mine]

    piece_a0 = hold(pick_mine(own_a, take_a))
    pieces_a0 = sent_near(piece_a0)
    take_b = swapped(hold(away_b))
    piece_b0 = pick_mine(own_b, take_b)

    taps_own = jnp.concatenate(
        [
            jnp.concatenate([hold(conv_value[0]), conv_state[0]], axis=1),
            jnp.concatenate([conv_value_bias, conv_state_bias], axis=1),
            jnp.zeros((3, conv_width), F32),
        ],
        axis=0,
    )
    heads_own = jnp.pad(jnp.concatenate([hold(step_bias), decay_log, skip_gain], axis=0), ((0, 5), (0, LANE - heads)))
    gains_own = jnp.concatenate([relative_order(hold(norm_gain), 1, "row"), gate_gain], axis=1)
    gains_own = jnp.pad(gains_own, ((0, 7), (0, 0)))
    small = jnp.concatenate([taps_own, heads_own, gains_own], axis=1)
    small_other = swapped(small)
    params = (pick_mine(small, small_other), pick_mine(small_other, small))
    places = (slice(0, conv_width), slice(conv_width, conv_width + LANE))
    places += (slice(conv_width + LANE, conv_width + LANE + width), slice(conv_width + LANE + width, small.shape[1]))

    source = hold(batch_order)[core]
    layer_in = relative_order(inputs[source], 1, "row")
    seg = jnp.broadcast_to(segment_ids[source].astype(F32)[:, None], (tokens, LANE))
    sent_rows = jnp.concatenate([layer_in[tokens - LEAD :], seg[tokens - LEAD :].astype(BF16)], axis=1)
    got_rows = from_before(sent_rows, rows, 1)
    other_order = row ^ jnp.maximum(row - 1, 0)
    before0 = relative_order(got_rows[:, :width], 1, "row", other_order)
    seg_before = jnp.where(row == 0, -1.0, got_rows[:, width:].astype(F32))
    g_out1 = relative_order(hold(cotangent)[core], 1, "row")
    close(pieces_a0, piece_b0, params, layer_in, seg, before0, seg_before, g_out1)

    long = tokens + LEAD
    message_shape = shaped((states + SMALL_ROWS, inner), BF16)
    entered = (
        shaped((long, width), BF16), shaped((tokens, LANE)), shaped((long, conv_width + LANE)),
        shaped((tokens, conv_width)), shaped((tokens, inner)), shaped((tokens, inner), BF16),
        shaped((tokens, 2 * states), BF16), shaped((tokens, LANE)), shaped((tokens, LANE)), shaped((LANE, tokens)),
        shaped((tokens, LANE)), shaped((tokens, LANE)), message_shape,
    )
    enter = [
        on_chip(
            functools.partial(enter_first_kernel, inner, heads_tile, places),
            (shaped((tokens, LANE)), shaped((8, tokens))) + entered,
            [pltpu.VMEM((long, LANE), F32), pltpu.VMEM((tokens, inner), BF16)],
        ),
        on_chip(
            functools.partial(enter_kernel, inner, heads_tile, places), entered, [pltpu.VMEM((tokens, inner), BF16)]
        ),
    ]
    intra = on_chip(functools.partial(intra_kernel, inner, heads_tile, places), shaped((tokens, inner)))
    gate_product = on_chip(functools.partial(wide_kernel, 0, LEAD), shaped((tokens, inner)))
    branch_product = on_chip(functools.partial(wide_kernel, half, 0), shaped((tokens, inner)))
    gates = [
        on_chip(
            functools.partial(gate_kernel, inner, heads_tile, places, reach, with_grad),
            (shaped((tokens, inner)), shaped((states, inner), BF16))
            + ((shaped((tokens, width), BF16), shaped((8, tokens))) if with_grad else (shaped((tokens, width + LANE), BF16),)),
            [pltpu.VMEM((tokens, inner), BF16)],
        )
        for with_grad in (False, True)
    ]
    ungates = [on_chip(
        functools.partial(ungate_kernel, inner, heads_tile, places, norm_width),
        (
            shaped((tokens, inner)), shaped((tokens, inner), BF16), shaped((tokens, inner), BF16), message_shape,
            shaped((8, inner)),
        ),
        [pltpu.VMEM((tokens, inner), BF16)],
        far_in=far,
    ) for far in ((), (0, 2, 3, 4, 5, 6))]
    intra_grad = on_chip(
        functools.partial(intra_grad_kernel, inner, heads_tile),
        (shaped((tokens, inner)), shaped((tokens, 2 * states)), shaped((tokens, LANE))),
        [pltpu.VMEM((LANE, tokens), F32)],
    )
    inter_grad = on_chip(
        functools.partial(inter_grad_kernel, inner, heads_tile, places, reach),
        (shaped((long, conv_width)), shaped((tokens, LANE), BF16), shaped((8, conv_width))),
        [pltpu.VMEM((tokens + 16, LANE), F32)] + [pltpu.VMEM((tokens, inner), BF16)] * 5,
    )
    pull = on_chip(pull_kernel, (shaped((tokens, width), BF16), shaped((8, width))))
    weight_t = shaped((width, tokens), BF16)
    give_a = on_chip(
        give_a_kernel,
        (shaped((width + STEPS * (width // a_width) + TAPS_ROWS, a_width), BF16),) + (shaped((tokens, a_width), BF16),) * 2,
        [pltpu.VMEM((tokens, conv_width), BF16)],
    )
    give_b = on_chip(
        give_b_kernel,
        (shaped((width, b_width), BF16), shaped((tokens, half), BF16), shaped((tokens, half), BF16), weight_t, weight_t),
    )
    keep_a = on_chip(keep_a_kernel, (shaped((shard + STEPS + SMALL, a_width), BF16),) * rows, far_out=range(1, rows))
    keep_b = on_chip(keep_b_kernel, (shaped((shard, b_width), BF16),) * rows, far_out=range(1, rows))
    ids = jnp.stack([core, row, lax.axis_index("col")]).astype(jnp.int32)
    ordered = rows == BLOCKS and shard % LANE == 0
    leave = [
        on_chip(
            functools.partial(leave_kernel, norm_width, places, False, ordered), (shaped((tokens, width)),) * 2,
            far_in=(3, 4, 6), far_out=(0, 1),
        ),
        on_chip(
            functools.partial(leave_kernel, norm_width, places, True, ordered),
            (shaped((tokens, width)), shaped((tokens, width), BF16), shaped((tokens, LANE))),
            far_in=(3, 4, 6), far_out=(0,),
        ),
    ]

    pieces_a0 = [hold(p) for p in pieces_a0]
    pieces_a0 += passed_on(pieces_a0)
    close(pieces_a0)
    weights_a0 = both_cores(blocks_of(pieces_a0))
    pieces_b0 = sent_near(hold(piece_b0))
    aux, seg_t, *made0 = enter[0](
        core_id, hold(layer_in), before0, params[0], seg, seg_before, *weights_a0[0], *weights_a0[1]
    )
    normed0, scale0, z0, conv0, value0, scaled0, bc0, step0, cum0, cumt0, lead0, carry0, message0 = made0
    close(message0, pieces_b0)
    messages0 = [from_before(hold(message0), rows, d) for d in distances]
    inside0 = intra(hold(scaled0), value0, bc0, cum0, cumt0, aux, seg_t, params[0])
    close(messages0, inside0)
    pieces_b0 = [hold(p) for p in pieces_b0]
    pieces_b0 += passed_on(pieces_b0)
    weights_b0 = both_cores(blocks_of(pieces_b0))
    close(weights_b0)
    gate0 = gate_product(core_id, hold(normed0), *weights_b0[0], *weights_b0[1])
    ssd0, state0, partial0 = gates[0](
        core_id, inside0, bc0, carry0, gate0, params[0], *messages0, *weights_b0[0], *weights_b0[1]
    )
    close(partial0)
    pieces_a1 = sent_near(hold(pick_mine(take_a, own_a)))
    pieces_b1 = sent_near(hold(pick_mine(take_b, own_b)))
    own0 = parts_sum(hold(partial0), "col")
    square = own0[:, width : width + 1] + own0[:, width + 1 : width + 2]
    rest = square - square.astype(BF16).astype(F32)
    lanes = lax.broadcasted_iota(jnp.int32, own0.shape, 1)
    own0 = jnp.where(lanes == width, square, jnp.where(lanes == width + 1, rest, own0)).astype(BF16)
    close(own0, pieces_a1, pieces_b1)
    pieces_a1, pieces_b1 = [hold(p) for p in pieces_a1], [hold(p) for p in pieces_b1]
    pieces_a1 += [sent_to(pieces_a1[0], "row", b) for b in range(near, rows)]
    pieces_b1 += [sent_to(pieces_b1[0], "row", b) for b in range(near, rows)]
    full0 = col_gather(hold(own0))
    blocks_a1 = blocks_of(pieces_a1)
    ready = near if rows == BLOCKS else 0
    others_a1 = [swapped(w) for w in blocks_a1[:ready]]
    close(full0, blocks_a1, others_a1, pieces_b1)
    weights_a1 = (blocks_a1, others_a1 + [swapped(hold(w)) for w in blocks_a1[ready:]])
    full0 = hold(full0)
    x1, tail1 = on_chip(
        functools.partial(next_kernel, norm_width), (shaped((tokens, width), BF16), shaped((LEAD, width), BF16))
    )(full0, layer_in)

    before1 = relative_order(from_before(tail1, rows, 1), 1, "row", other_order)
    close(x1, before1, weights_a1)
    weights_b1 = both_cores([hold(w) for w in blocks_of(pieces_b1)])
    made1 = enter[1](core_id, hold(x1), before1, params[1], aux, *weights_a1[0], *weights_a1[1])
    normed1, scale1, z1, conv1, value1, scaled1, bc1, step1, cum1, cumt1, lead1, carry1, message1 = made1
    close(message1, weights_b1)
    messages1 = [from_before(hold(message1), rows, d) for d in distances]
    inside1 = intra(hold(scaled1), value1, bc1, cum1, cumt1, aux, seg_t, params[1])
    gate1 = gate_product(core_id, hold(normed1), *weights_b1[0], *weights_b1[1])
    close(messages1, inside1, gate1)
    gbranch1 = branch_product(core_id, hold(g_out1), *weights_b1[0], *weights_b1[1])
    ssd1, state1, partial1, sums1 = gates[1](
        core_id, inside1, bc1, carry1, gate1, params[1], *messages1, *weights_b1[0], *weights_b1[1], gbranch1
    )
    sums1 = [sums1] + [sent_to(sums1, "col", b) for b in range(1, lax.axis_size("col"))]
    norm1 = on_chip(functools.partial(norm_kernel, norm_width), shaped((tokens, LANE)))(*sums1)
    close(norm1)

    def scan_back(layer, gbranch, norm, gate, ssd, state, made, beside):
        _, scale, z, conv, value, scaled, bc, step, cum, cumt, lead, carry, _ = made
        gssd, ggate, branch, message, ggain = ungates[layer](gbranch, norm, gate, ssd, params[layer], carry, bc)
        close(message)
        messages = [from_after(hold(message), rows, d) for d in distances]
        gscaled, gbc, gcum = intra_grad(scaled, hold(gssd), bc, cum, cumt, aux, seg_t)
        close(messages, gscaled, beside("intra"))
        gpre, gstep, gtaps = inter_grad(
            state, scaled, value, gssd, hold(gscaled), bc, gbc, gcum, step, lead, carry, z, conv, aux, params[layer],
            ggain, *messages,
        )
        close(gpre, beside("inter"))
        return gpre, gstep, gtaps, ggate, branch

    def reduce_back(scanned, normed, scale, x, g_out, weights_a, weights_b, beside):
        gpre, gstep, gtaps, ggate, branch = scanned
        from_next = from_after(hold(gpre[:LEAD]), rows, 1)
        other_b, gg_mine, gg_other, normed_t, g_out_t = give_b(core_id, hold(ggate), normed, g_out, branch)
        kept_b = keep_b(core_id, normed_t, g_out_t, branch, gg_mine, swapped(other_b))
        close(from_next, kept_b, beside("halo"))
        other_a, ga_mine, ga_other = give_a(core_id, gpre, hold(from_next), gstep, normed_t, gtaps)
        close(other_a)
        their_a = swapped(hold(other_a))
        partial, ggain = pull(
            hold(ga_mine), ga_other, gstep, gg_mine, gg_other, x, scale,
            *weights_a[0], *weights_a[1], *weights_b[0], *weights_b[1],
        )
        close(their_a, partial, beside("pull"))
        ggain = hold(ggain)
        ggain = relative_order(ggain + swapped(ggain), 1, "row")
        kept_a = keep_a(normed_t, hold(ga_mine), gstep, their_a, gtaps, ggain)
        close(kept_a, beside("keep"))

        def sends(blocks, which):
            return [sent_to(hold(blocks[b]), "row", b) for b in which]

        early, late = range(1, near), range(near, rows)
        got_a, got_b = sends(kept_a, early), sends(kept_b, early)
        own = parts_sum(hold(partial), "col").astype(BF16)
        close(own, got_a, got_b, beside("scatter"))
        got_a += sends(kept_a, late)
        got_b += sends(kept_b, late)
        full = col_gather(hold(own))
        close(full, got_a, got_b)

        return hold(full), [hold(kept_a[0])] + got_a, [hold(kept_b[0])] + got_b

    def total(pieces):
        return functools.reduce(lambda u, v: u + v.astype(F32), pieces[1:], pieces[0].astype(F32))

    stack = on_chip(stack_kernel, shaped((2, tokens, width)), far_in=(1, 2), far_out=(0,))
    stack_low = on_chip(stack_kernel, shaped((2, tokens, width), BF16), far_out=(0,))

    def in_order_both(pair):
        return pair if ordered else relative_order(pair, 2, "row")

    cols = lax.axis_size("col")
    col = lax.axis_index("col")
    chunk = tokens // cols
    slots = ("intra", "halo", "pull")
    parts1 = [lax.dynamic_slice_in_dim(hold(partial1), (col ^ b) * chunk, chunk, 0) for b in range(cols)]
    received = {1: [], 0: []}
    store = {}

    def exchange(layer, name, sources):
        if name not in slots:
            return ()
        at = slots.index(name)
        mine = range(1 + at, cols) if name == slots[-1] else range(1 + at, min(2 + at, cols))
        got = [sent_to(hold(sources[b]), "col", b) for b in mine]
        received[layer] += got
        return got

    def beside1(name):
        return exchange(1, name, parts1)

    def beside0(name):
        got = list(exchange(0, name, [store["chunk"]] * cols))
        if name == "intra":
            store["state"] = hold(total([p[:shard, half:] for p in store["pieces"][0]]).astype(BF16))
            store["state_got"] = sent_to(store["state"], "col", 1)
            got.append(store["state_got"])
        if name == "inter":
            summed = store["state"].astype(F32) + hold(store["state_got"]).astype(F32)
            step_out = 2
            while step_out < cols:
                summed = summed.astype(BF16)
                summed = summed.astype(F32) + sent_to(summed, "col", step_out).astype(F32)
                step_out *= 2
            store["state"] = summed
            got.append(summed)
        if name == "scatter":
            store["shares"] = [total([hold(p) for p in pieces]) for pieces in store["pieces"]]
            got.append(store["shares"])
            made = on_chip(functools.partial(outputs_kernel, ordered), (shaped((tokens, width), BF16),) * 2)(
                ids, hold(x1), norm1, store["chunk"], *received[0]
            )
            store["outputs"] = in_order_both(stack_low(core_id, made[0], swapped(made[1])))
            got.append(store["outputs"])
        return got

    scanned1 = scan_back(1, gbranch1, norm1, gate1, ssd1, state1, made1, beside1)
    grad_full1, pieces_a, pieces_b = reduce_back(
        scanned1, normed1, scale1, x1, g_out1, weights_a1, weights_b1, beside1
    )
    store["chunk"] = functools.reduce(lambda u, v: u + v.astype(F32), received[1], parts1[0].astype(F32)).astype(BF16)
    store["pieces"] = (pieces_a, pieces_b)
    g_in1, g_out0, norm0 = leave[1](ids, grad_full1, x1, scale1, params[1], g_out1, full0)
    gbranch0 = branch_product(core_id, g_out0, *weights_b0[0], *weights_b0[1])
    scanned0 = scan_back(0, gbranch0, norm0, gate0, ssd0, state0, made0, beside0)
    grad_full0, pieces_a, pieces_b = reduce_back(
        scanned0, normed0, scale0, layer_in, g_out0, weights_a0, weights_b0, beside0
    )
    tiles = (2 * states + a_width) // LANE
    mine_a, give_a_, mine_b, give_b_, message, d_cv, d_cvb, d_gain, d_heads = on_chip(
        functools.partial(sum_kernel, inner, states, heads_tile),
        (shaped((shard + STEPS, a_width), BF16),) * 2
        + (shaped((shard, b_width), BF16),) * 2
        + (shaped((shard + 16 * tiles, LANE), BF16), shaped((4, inner)), shaped((1, inner)), shaped((1, inner)), shaped((8, LANE))),
        far_in=(1, 2), far_out=(0, 1, 2, 3),
    )(ids, *store["shares"], *[hold(p) for p in pieces_a], *pieces_b)
    close(message)
    messages = [hold(message)] + [sent_to(hold(message), "col", b) for b in range(1, cols)]
    their_a, their_b = swapped(hold(give_a_)), swapped(hold(give_b_))
    mine, give = leave[0](ids, hold(grad_full0), layer_in, scale0, params[0], g_out0, g_in1)
    close(mine, their_a, their_b, messages[1])
    other_grad = swapped(hold(give))
    d_value, d_step, d_gate, d_out = on_chip(
        join_kernel, (shaped((shard, inner)), shaped((heads, shard)), shaped((shard, inner)), shaped((inner, shard))),
        far_in=(1, 2, 3, 4), far_out=(0, 1, 2, 3),
    )(ids, hold(mine_a), their_a, mine_b, their_b)
    place = jnp.where(first, batch_order[0], core).reshape(1).astype(jnp.int32)
    input_grads = in_order_both(stack(place, mine, other_grad))
    close(d_value, input_grads, messages)
    mine_s, give_s, d_cs, d_csb, d_norm = on_chip(
        functools.partial(col_kernel, states),
        (shaped((shard, states), BF16),) * 2 + (shaped((4, 2 * states)), shaped((1, 2 * states)), shaped((1, width))),
    )(ids, store["state"], *[hold(m) for m in messages])
    their_s = swapped(give_s)
    d_state = jnp.concatenate([pick_mine(mine_s, their_s), pick_mine(their_s, mine_s)], axis=1).astype(F32)

    return (
        store["outputs"][None],
        input_grads[None],
        d_norm,
        d_gate[None],
        d_value[None],
        d_step.T[None],
        d_state[None],
        d_cv[None],
        d_cvb,
        d_cs[None],
        d_csb,
        d_heads[0:1, :heads],
        d_heads[1:2, :heads],
        d_heads[5:6, :heads],
        d_gain,
        d_out[None],
    )


def solution(mesh):
    in_specs = (
        P(None, "row", None),
        P(None, "row", None),
        P(None, "row"),
        P(),
        P("pipe", None),
        P("pipe", "row", "col"),
        P("pipe", "row", "col"),
        P("pipe", "row", "col"),
        P("pipe", "row", None),
        P("pipe", None, "col"),
        P("pipe", "col"),
        P("pipe", None, None),
        P("pipe", None),
        P("pipe", "col"),
        P("pipe", "col"),
        P("pipe", "col"),
        P("pipe", "col"),
        P("pipe", "col", "row"),
    )
    out_specs = (
        P("pipe", None, "row", None),
        P("pipe", None, "row", None),
        P("pipe", None),
        P("pipe", "row", "col"),
        P("pipe", "row", "col"),
        P("pipe", "row", "col"),
        P("pipe", "row", None),
        P("pipe", None, "col"),
        P("pipe", "col"),
        P("pipe", None, None),
        P("pipe", None),
        P("pipe", "col"),
        P("pipe", "col"),
        P("pipe", "col"),
        P("pipe", "col"),
        P("pipe", "col", "row"),
    )
    return jax.shard_map(local, mesh=mesh, in_specs=in_specs, out_specs=out_specs, check_vma=False)
```
